128 devices in a mesh: dp: 16 (over x, y), ctx: 8 (over z, core).
Axes of the slice: x: 4, y: 4, z: 4, core: 2. Of those that a mesh axis runs over, the one named last changes fastest.
Arguments:
- hidden_acts: bfloat16 [131072, 1536], P(('dp', 'ctx')), may hold values from -6 to 6
- out_grad: bfloat16 [131072, 5120], P(('dp', 'ctx')), may hold values from -96 to 96
- old_logp: float32 [16, 8192], P('dp', 'ctx'), may hold values from -4 to -0.3
- new_logp: float32 [16, 8192], P('dp', 'ctx'), may hold values from -4.3 to 0
- roll_len: int32 [16], P('dp'), may hold values from 2048 to 8192, as said below
- resp_mask: int32 [16, 8192], P('dp', 'ctx'), may hold values 0 or 1
- advantage: float32 [16, 1], P('dp'), may hold values from -4 to 4
Outputs:
- bucket_grad: float32 [1536, 5120], P('dp', 'ctx')
The draws below stay inside these ranges and needn't reach their ends.
Inputs may be any that keep to these rules, and one draw needn't show every extreme that they name: `roll_len`: some rollout fills all 8192 positions.
All inputs are finite; a program needn't handle non-finite values. No bound on the sum of `resp_mask` on one device may be relied on, other than what follows from the above.
Results may differ from the reference program's by a relative error of at most 0.0028.
Values sent between devices are 32-bit elements; how exact they have to be, the bound alone decides.
A program may use at most 192 MiB of HBM per device.

```python
import jax
import jax.numpy as jnp
from jax import lax

D = 5120
HB = 1536
ROW = 8192
ROWS = 16


def ratio_parts(key):
    base = jax.random.fold_in(key, 7)
    first_key, second_key, third_key = jax.random.split(base, 3)
    behaviour = -jax.random.uniform(first_key, (ROWS, ROW), jnp.float32, 0.3, 4.0)
    offset = jax.random.uniform(second_key, (ROWS, 1), jnp.float32, -0.0015, 0.0015)
    noise = jax.random.normal(third_key, (ROWS, ROW), jnp.float32)
    noise = jnp.clip(noise, -4.0, 4.0)
    ramp = 0.5 + 1.5 * jnp.arange(ROW, dtype=jnp.float32)[None, :] / ROW
    log_gap = (offset + 0.02 * noise) * ramp
    current = jnp.minimum(behaviour + log_gap, 0.0)
    return (behaviour, current)


def draw_old_logp(key, part):
    return ratio_parts(key)[0]


def draw_new_logp(key, part):
    return ratio_parts(key)[1]


def draw_roll_len(key, part):
    base = jax.random.fold_in(key, 11)
    len_key, pick_key = jax.random.split(base, 2)
    drawn = jax.random.randint(len_key, (ROWS,), ROW // 4, ROW + 1)
    chosen = jax.random.randint(pick_key, (), 0, ROWS)
    return jnp.where(jnp.arange(ROWS, dtype=jnp.int32) == chosen, ROW, drawn).astype(jnp.int32)


def plant(array, stream_key, least, largest):
    dims = array.shape
    spot = [jax.random.randint(jax.random.fold_in(stream_key, axis), (), 0, dims[axis]) for axis in range(len(dims))]
    array = array.at[tuple(spot)].set(least)
    longest = dims.index(max(dims))
    spot[longest] = (spot[longest] + 1) % dims[longest]
    return array.at[tuple(spot)].set(largest)


def strengthened(entries, own_key, source, target, parts, factor):
    def block_of(position):
        return (jnp.arange(entries.shape[position]) // (entries.shape[position] // parts)).reshape((-1,) + (1,) * (entries.ndim - 1 - position))

    near = jax.random.permutation(own_key, parts)[block_of(target)]
    far = (block_of(target) + parts // 2) % parts
    return jnp.where((block_of(source) == near) | (block_of(source) == far), factor * entries, entries)


def shard_levels(rng, shape, pieces, smallest, high):
    def one(position, shards_of):
        steps = jax.random.uniform(jax.random.fold_in(jax.random.fold_in(rng, 6), position), (shards_of,), jnp.float32, smallest / len(pieces), high / len(pieces))
        return jnp.repeat(jnp.exp(steps), shape[position] // shards_of).reshape((-1,) + (1,) * (len(shape) - position - 1))

    factor_of = one(*pieces[0])
    for cut in pieces[1:]:
        factor_of = factor_of * one(*cut)
    return factor_of


def scatter_about(own_key, dims, width, bound, pieces=(), kind=jnp.bfloat16):
    values = width * jax.random.normal(own_key, dims, jnp.float32)
    if pieces:
        values = values * shard_levels(own_key, dims, pieces, -0.22, 0.18)
    return jnp.clip(values, -bound, bound).astype(kind)


def noise_with(stream_key, extent, deviation, bound, cuts, heavy, held_as=jnp.bfloat16):
    values = deviation * jax.random.normal(stream_key, extent, jnp.float32)
    if cuts:
        values = values * shard_levels(stream_key, extent, cuts, -0.22, 0.18)
    return jnp.clip(strengthened(values, jax.random.fold_in(stream_key, 3), *heavy), -bound, bound).astype(held_as)


def setup_inputs(seed: int = 0) -> dict:
    key_list = jax.random.split(jax.random.key(seed), 8)
    hidden_acts = scatter_about(key_list[0], (ROWS * ROW, HB), 1.0, 6.0, ((0, 128),))
    out_grad = noise_with(key_list[1], (ROWS * ROW, D), 4.0, 96.0, ((0, 128),), (0, 1, 128, 5.5))
    old_logp = draw_old_logp(jax.random.fold_in(key_list[7], 71), 0)
    new_logp = draw_new_logp(jax.random.fold_in(key_list[7], 71), 0)
    roll_len = draw_roll_len(jax.random.fold_in(key_list[7], 71), 0)
    resp_mask = plant((jax.random.randint(key_list[5], (ROWS, ROW), 0, 4) < 3).astype(jnp.int32), jax.random.fold_in(key_list[5], 1), 0, 1)
    advantage = scatter_about(key_list[6], (ROWS, 1), 1.0, 4.0, ((0, 16),), jnp.float32)
    return {"hidden_acts": hidden_acts, "out_grad": out_grad, "old_logp": old_logp, "new_logp": new_logp, "roll_len": roll_len, "resp_mask": resp_mask, "advantage": advantage}


CLIP_LOW = 0.0003
CLIP_HIGH = 0.0004


def reference(hidden_acts, out_grad, old_logp, new_logp, roll_len, resp_mask, advantage):
    places = jnp.arange(ROW, dtype=jnp.int32)
    hid_rows = hidden_acts.reshape(ROWS, ROW, HB)
    grad_rows = out_grad.reshape(ROWS, ROW, D)

    def one_row(total, inputs):
        hid_row, grad_row, old_row, new_row, len_row, mask_row, adv_row = inputs
        masked = jnp.where(places < len_row, mask_row, 0).astype(jnp.float32)
        gap_sum = jnp.sum((new_row - old_row) * masked)
        count = jnp.sum(masked)
        length = jnp.maximum(count, 1.0)
        seq_ratio = jnp.exp(gap_sum / length)
        adv = adv_row[0]
        active = jnp.where(adv >= 0.0, seq_ratio < 1.0 + CLIP_HIGH, seq_ratio > 1.0 - CLIP_LOW).astype(jnp.float32)
        seq_weight = -adv * seq_ratio * active / length
        token_coef = masked * seq_weight
        scaled = (token_coef[:, None] * grad_row.astype(jnp.float32)).astype(jnp.bfloat16)
        product = lax.dot_general(hid_row, scaled, (((0,), (0,)), ((), ())), preferred_element_type=jnp.float32)
        return total + product, None

    bucket_grad, _ = lax.scan(one_row, jnp.zeros((HB, D), jnp.float32),
                              (hid_rows, grad_rows, old_logp, new_logp, roll_len, resp_mask, advantage))
    return bucket_grad
```

```python
import jax
import jax.numpy as jnp
from jax import lax
from jax.sharding import PartitionSpec as P

CLIP_LOW = 0.0003
CLIP_HIGH = 0.0004


def shards(hidden_acts, out_grad, old_logp, new_logp, roll_len, resp_mask, advantage, n_dp, n_ctx):
    width = old_logp.shape[1]
    places = lax.axis_index("ctx") * width + jnp.arange(width, dtype=jnp.int32)
    masked = jnp.where(places < roll_len[0], resp_mask[0], 0).astype(jnp.float32)
    gap_sum, count = lax.psum(
        (jnp.sum((new_logp[0] - old_logp[0]) * masked), jnp.sum(masked)), "ctx"
    )
    adv = advantage[0, 0]
    length = jnp.maximum(count, 1.0)
    seq_ratio = jnp.exp(gap_sum / length)
    active = jnp.where(adv >= 0.0, seq_ratio < 1.0 + CLIP_HIGH, seq_ratio > 1.0 - CLIP_LOW).astype(
        jnp.float32
    )
    seq_weight = -adv * seq_ratio * active / length
    token_coef = masked * seq_weight
    scaled = (token_coef[:, None] * out_grad).astype(jnp.bfloat16)
    t, hb = hidden_acts.shape
    d = out_grad.shape[1]
    h3 = hidden_acts.reshape(t, n_dp, hb // n_dp)
    s3 = scaled.reshape(t, n_ctx, d // n_ctx)
    part = jnp.einsum("tar,tbc->barc", h3, s3, preferred_element_type=jnp.float32)
    part = part.reshape(n_dp * n_ctx, hb // n_dp, d // n_ctx)
    out = lax.psum_scatter(part, ("ctx", "dp"), scatter_dimension=0, tiled=True)
    return out[0]


def solution(mesh):
    placed = (
        P(("dp", "ctx"), None),
        P(("dp", "ctx"), None),
        P("dp", "ctx"),
        P("dp", "ctx"),
        P("dp"),
        P("dp", "ctx"),
        P("dp", None),
    )
    n_dp, n_ctx = mesh.shape["dp"], mesh.shape["ctx"]

    def f(*a):
        return shards(*a, n_dp, n_ctx)

    return jax.shard_map(
        f, mesh=mesh, in_specs=placed, out_specs=P("dp", "ctx"), check_vma=False
    )
```

```python
import jax
import jax.numpy as jnp
import numpy as np
from jax import lax
from jax.experimental import pallas as pl
from jax.experimental.pallas import tpu as pltpu
from jax.sharding import Mesh
from jax.sharding import PartitionSpec as P

CLIP_LOW = 0.0003
CLIP_HIGH = 0.0004
ROW_TILE = 384


def half_matmul(sel, coef, grad, hid_t, n_dp, n_z, width):
    hb, t = hid_t.shape
    rows = hb // n_dp
    per_tile = ROW_TILE // rows
    n_tiles = hb // ROW_TILE

    def kernel(sel_ref, coef_ref, grad_ref, hid_ref, out_ref, scaled_ref):
        @pl.when(pl.program_id(1) == 0)
        def _():
            scaled_ref[...] = (coef_ref[...] * grad_ref[...].astype(jnp.float32)).astype(jnp.bfloat16)

        acc = jnp.dot(hid_ref[...], scaled_ref[...], preferred_element_type=jnp.float32)
        for k in range(per_tile):
            out_ref[k, 0] = acc[k * rows:(k + 1) * rows, :]

    grid_spec = pltpu.PrefetchScalarGridSpec(
        num_scalar_prefetch=1,
        grid=(n_z, n_tiles),
        in_specs=[
            pl.BlockSpec((t, 1), lambda z, i, s: (0, 0)),
            pl.BlockSpec((t, width), lambda z, i, s: (0, z * 2 + s[0])),
            pl.BlockSpec((ROW_TILE, t), lambda z, i, s: (i, 0)),
        ],
        out_specs=pl.BlockSpec((per_tile, 1, rows, width), lambda z, i, s: (i, z, 0, 0)),
        scratch_shapes=[pltpu.VMEM((t, width), jnp.bfloat16)],
    )
    flops = 2 * hb * t * width * n_z
    return pl.pallas_call(
        kernel,
        grid_spec=grid_spec,
        out_shape=jax.ShapeDtypeStruct((n_dp, n_z, rows, width), jnp.float32),
        compiler_params=pltpu.CompilerParams(vmem_limit_bytes=48 * 1024 * 1024),
        cost_estimate=pl.CostEstimate(
            flops=flops, transcendentals=0,
            bytes_accessed=hb * t * 2 + t * width * n_z * 2 + hb * width * n_z * 4,
        ),
    )(sel, coef, grad, hid_t)


def shards(hidden_acts, out_grad, old_logp, new_logp, roll_len, resp_mask, advantage):
    n_dp = lax.axis_size("dp")
    n_z = lax.axis_size("z")
    n_core = lax.axis_size("core")
    width = old_logp.shape[1]
    ctx = lax.axis_index("z") * n_core + lax.axis_index("core")
    places = ctx * width + jnp.arange(width, dtype=jnp.int32)
    masked = jnp.where(places < roll_len[0], resp_mask[0], 0).astype(jnp.float32)
    gap_sum, count = lax.psum(
        (jnp.sum((new_logp[0] - old_logp[0]) * masked), jnp.sum(masked)), ("z", "core")
    )
    adv = advantage[0, 0]
    length = jnp.maximum(count, 1.0)
    seq_ratio = jnp.exp(gap_sum / length)
    active = jnp.where(adv >= 0.0, seq_ratio < 1.0 + CLIP_HIGH, seq_ratio > 1.0 - CLIP_LOW).astype(
        jnp.float32
    )
    seq_weight = -adv * seq_ratio * active / length
    token_coef = (masked * seq_weight)[:, None]
    d = out_grad.shape[1]
    col = d // (n_z * n_core)
    hid_t = hidden_acts.T
    core = lax.axis_index("core")
    other = jnp.reshape(1 - core, (1,)).astype(jnp.int32)
    mine = jnp.reshape(core, (1,)).astype(jnp.int32)
    theirs = half_matmul(other, token_coef, out_grad, hid_t, n_dp, n_z, col)
    got = lax.ppermute(theirs, "core", perm=[(0, 1), (1, 0)])
    own = half_matmul(mine, token_coef, out_grad, hid_t, n_dp, n_z, col)
    chip = own + got
    rows = lax.psum_scatter(chip, "dp", scatter_dimension=0, tiled=True)[0]
    return lax.psum_scatter(rows, "z", scatter_dimension=0, tiled=True)[0]


def solution(mesh):
    n_dp, n_ctx = mesh.shape["dp"], mesh.shape["ctx"]
    fine = Mesh(np.asarray(mesh.devices).reshape(n_dp, n_ctx // 2, 2), ("dp", "z", "core"))
    tok = ("dp", "z", "core")
    placed = (
        P(tok, None),
        P(tok, None),
        P("dp", ("z", "core")),
        P("dp", ("z", "core")),
        P("dp"),
        P("dp", ("z", "core")),
        P("dp", None),
    )
    return jax.shard_map(
        shards, mesh=fine, in_specs=placed, out_specs=P("dp", ("z", "core")), check_vma=False
    )
```

```python
import jax
import jax.numpy as jnp
import numpy as np
from jax import lax
from jax.experimental import pallas as pl
from jax.experimental.pallas import tpu as pltpu
from jax.sharding import Mesh
from jax.sharding import PartitionSpec as P

CLIP_LOW = 0.0003
CLIP_HIGH = 0.0004
ROW_TILE = 1536


def half_matmul(sel, coef, grad, hid_t, n_dp, n_z, width):
    hb, t = hid_t.shape
    rows = hb // n_dp
    per_tile = ROW_TILE // rows
    n_tiles = hb // ROW_TILE

    def kernel(sel_ref, coef_ref, grad_ref, hid_ref, out_ref, scaled_ref):
        @pl.when(pl.program_id(1) == 0)
        def _():
            scaled_ref[...] = (coef_ref[...] * grad_ref[...].astype(jnp.float32)).astype(jnp.bfloat16)

        acc = jnp.dot(hid_ref[...], scaled_ref[...], preferred_element_type=jnp.float32)
        for k in range(per_tile):
            out_ref[k, 0] = acc[k * rows:(k + 1) * rows, :]

    grid_spec = pltpu.PrefetchScalarGridSpec(
        num_scalar_prefetch=1,
        grid=(n_z, n_tiles),
        in_specs=[
            pl.BlockSpec((t, 1), lambda z, i, s: (0, 0)),
            pl.BlockSpec((t, width), lambda z, i, s: (0, z * 2 + s[0])),
            pl.BlockSpec((ROW_TILE, t), lambda z, i, s: (i, 0)),
        ],
        out_specs=pl.BlockSpec((per_tile, 1, rows, width), lambda z, i, s: (i, z, 0, 0)),
        scratch_shapes=[pltpu.VMEM((t, width), jnp.bfloat16)],
    )
    flops = 2 * hb * t * width * n_z
    return pl.pallas_call(
        kernel,
        grid_spec=grid_spec,
        out_shape=jax.ShapeDtypeStruct((n_dp, n_z, rows, width), jnp.float32),
        compiler_params=pltpu.CompilerParams(vmem_limit_bytes=48 * 1024 * 1024),
        cost_estimate=pl.CostEstimate(
            flops=flops, transcendentals=0,
            bytes_accessed=hb * t * 2 + t * width * n_z * 2 + hb * width * n_z * 4,
        ),
    )(sel, coef, grad, hid_t)


def shards(hidden_acts, out_grad, old_logp, new_logp, roll_len, resp_mask, advantage):
    n_dp = lax.axis_size("dp")
    n_z = lax.axis_size("z")
    n_core = lax.axis_size("core")
    width = old_logp.shape[1]
    ctx = lax.axis_index("z") * n_core + lax.axis_index("core")
    places = ctx * width + jnp.arange(width, dtype=jnp.int32)
    masked = jnp.where(places < roll_len[0], resp_mask[0], 0).astype(jnp.float32)
    gap_sum, count = lax.psum(
        (jnp.sum((new_logp[0] - old_logp[0]) * masked), jnp.sum(masked)), ("z", "core")
    )
    adv = advantage[0, 0]
    length = jnp.maximum(count, 1.0)
    seq_ratio = jnp.exp(gap_sum / length)
    active = jnp.where(adv >= 0.0, seq_ratio < 1.0 + CLIP_HIGH, seq_ratio > 1.0 - CLIP_LOW).astype(
        jnp.float32
    )
    seq_weight = -adv * seq_ratio * active / length
    token_coef = (masked * seq_weight)[:, None]
    d = out_grad.shape[1]
    col = d // (n_z * n_core)
    hid_t = hidden_acts.T
    core = lax.axis_index("core")
    other = jnp.reshape(1 - core, (1,)).astype(jnp.int32)
    mine = jnp.reshape(core, (1,)).astype(jnp.int32)
    theirs = half_matmul(other, token_coef, out_grad, hid_t, n_dp, n_z, col)
    got = lax.ppermute(theirs, "core", perm=[(0, 1), (1, 0)])
    own = half_matmul(mine, token_coef, out_grad, hid_t, n_dp, n_z, col)
    chip = own + got
    flat = chip.reshape((n_dp * n_z,) + chip.shape[2:])
    return lax.psum_scatter(flat, ("dp", "z"), scatter_dimension=0, tiled=True)[0]


def solution(mesh):
    n_dp, n_ctx = mesh.shape["dp"], mesh.shape["ctx"]
    fine = Mesh(np.asarray(mesh.devices).reshape(n_dp, n_ctx // 2, 2), ("dp", "z", "core"))
    tok = ("dp", "z", "core")
    placed = (
        P(tok, None),
        P(tok, None),
        P("dp", ("z", "core")),
        P("dp", ("z", "core")),
        P("dp"),
        P("dp", ("z", "core")),
        P("dp", None),
    )
    return jax.shard_map(
        shards, mesh=fine, in_specs=placed, out_specs=P("dp", ("z", "core")), check_vma=False
    )
```

```python
import jax
import jax.numpy as jnp
import numpy as np
from jax import lax
from jax.experimental import pallas as pl
from jax.experimental.pallas import tpu as pltpu
from jax.sharding import Mesh
from jax.sharding import PartitionSpec as P

CLIP_LOW = 0.0003
CLIP_HIGH = 0.0004
ROW_TILE = 384


def block_matmul(col, coef, grad, hid_t, n_dp, width, addend=None, into=None, slot=0, n_slots=1):
    hb, t = hid_t.shape
    rows = hb // n_dp
    per_tile = ROW_TILE // rows
    n_tiles = hb // ROW_TILE
    grouped = n_slots > 1

    def kernel(col_ref, coef_ref, grad_ref, hid_ref, *rest):
        rest = list(rest)
        add_ref = rest.pop(0) if addend is not None else None
        if into is not None:
            rest.pop(0)
        out_ref, scaled_ref = rest

        @pl.when(pl.program_id(0) == 0)
        def _():
            scaled_ref[...] = (coef_ref[...] * grad_ref[...].astype(jnp.float32)).astype(jnp.bfloat16)

        acc = jnp.dot(hid_ref[...], scaled_ref[...], preferred_element_type=jnp.float32)
        for k in range(per_tile):
            part = acc[k * rows:(k + 1) * rows, :]
            if add_ref is not None:
                part = part + add_ref[k]
            if grouped:
                out_ref[k, 0] = part
            else:
                out_ref[k] = part

    in_specs = [
        pl.BlockSpec((t, 1), lambda i, c: (0, 0)),
        pl.BlockSpec((t, width), lambda i, c: (0, c[0])),
        pl.BlockSpec((ROW_TILE, t), lambda i, c: (i, 0)),
    ]
    args = [col, coef, grad, hid_t]
    if addend is not None:
        in_specs.append(pl.BlockSpec((per_tile, rows, width), lambda i, c: (i, 0, 0)))
        args.append(addend)
    aliases = {}
    if into is not None:
        in_specs.append(pl.BlockSpec(memory_space=pl.ANY))
        aliases = {len(args): 0}
        args.append(into)
    if grouped:
        out_shape = jax.ShapeDtypeStruct((n_dp, n_slots, rows, width), jnp.float32)
        out_spec = pl.BlockSpec((per_tile, 1, rows, width), lambda i, c: (i, slot, 0, 0))
    else:
        out_shape = jax.ShapeDtypeStruct((n_dp, rows, width), jnp.float32)
        out_spec = pl.BlockSpec((per_tile, rows, width), lambda i, c: (i, 0, 0))
    grid_spec = pltpu.PrefetchScalarGridSpec(
        num_scalar_prefetch=1,
        grid=(n_tiles,),
        in_specs=in_specs,
        out_specs=out_spec,
        scratch_shapes=[pltpu.VMEM((t, width), jnp.bfloat16)],
    )
    extra = hb * width * 4 if addend is not None else 0
    return pl.pallas_call(
        kernel,
        grid_spec=grid_spec,
        out_shape=out_shape,
        input_output_aliases=aliases,
        compiler_params=pltpu.CompilerParams(vmem_limit_bytes=48 * 1024 * 1024),
        cost_estimate=pl.CostEstimate(
            flops=2 * hb * t * width, transcendentals=0,
            bytes_accessed=hb * t * 2 + t * width * 2 + hb * width * 4 + extra,
        ),
    )(*args)


def shards(hidden_acts, out_grad, old_logp, new_logp, roll_len, resp_mask, advantage):
    n_dp = lax.axis_size("dp")
    n_z = lax.axis_size("z")
    n_core = lax.axis_size("core")
    width = old_logp.shape[1]
    ctx = lax.axis_index("z") * n_core + lax.axis_index("core")
    places = ctx * width + jnp.arange(width, dtype=jnp.int32)
    masked = jnp.where(places < roll_len[0], resp_mask[0], 0).astype(jnp.float32)
    gap_sum, count = lax.psum(
        (jnp.sum((new_logp[0] - old_logp[0]) * masked), jnp.sum(masked)), ("z", "core")
    )
    adv = advantage[0, 0]
    length = jnp.maximum(count, 1.0)
    seq_ratio = jnp.exp(gap_sum / length)
    active = jnp.where(adv >= 0.0, seq_ratio < 1.0 + CLIP_HIGH, seq_ratio > 1.0 - CLIP_LOW).astype(
        jnp.float32
    )
    seq_weight = -adv * seq_ratio * active / length
    token_coef = (masked * seq_weight)[:, None]
    d = out_grad.shape[1]
    col = d // (n_z * n_core)
    hid_t = hidden_acts.T
    core = lax.axis_index("core").astype(jnp.int32)

    def col_index(k, which):
        return jnp.reshape(k * n_core + which, (1,)).astype(jnp.int32)

    got = []
    for k in range(n_z):
        theirs = block_matmul(col_index(k, 1 - core), token_coef, out_grad, hid_t, n_dp, col)
        got.append(lax.ppermute(theirs, "core", perm=[(0, 1), (1, 0)]))
    chip = None
    for k in range(n_z):
        chip = block_matmul(col_index(k, core), token_coef, out_grad, hid_t, n_dp, col,
                            addend=got[k], into=chip, slot=k, n_slots=n_z)
    rows = lax.psum_scatter(chip, "dp", scatter_dimension=0, tiled=True)[0]
    return lax.psum_scatter(rows, "z", scatter_dimension=0, tiled=True)[0]


def solution(mesh):
    n_dp, n_ctx = mesh.shape["dp"], mesh.shape["ctx"]
    fine = Mesh(np.asarray(mesh.devices).reshape(n_dp, n_ctx // 2, 2), ("dp", "z", "core"))
    tok = ("dp", "z", "core")
    placed = (
        P(tok, None),
        P(tok, None),
        P("dp", ("z", "core")),
        P("dp", ("z", "core")),
        P("dp"),
        P("dp", ("z", "core")),
        P("dp", None),
    )
    return jax.shard_map(
        shards, mesh=fine, in_specs=placed, out_specs=P("dp", ("z", "core")), check_vma=False
    )
```

```python
import jax
import jax.numpy as jnp
import numpy as np
from jax import lax
from jax.experimental import pallas as pl
from jax.experimental.pallas import tpu as pltpu
from jax.sharding import Mesh
from jax.sharding import PartitionSpec as P

CLIP_LOW = 0.0003
CLIP_HIGH = 0.0004
ROW_TILE = 768


def block_matmul(col, coef, grad, hid_t, n_dp, width, addend=None, into=None, slot=0, n_slots=1):
    hb, t = hid_t.shape
    rows = hb // n_dp
    per_tile = ROW_TILE // rows
    n_tiles = hb // ROW_TILE
    grouped = n_slots > 1

    def kernel(col_ref, coef_ref, grad_ref, hid_ref, *rest):
        rest = list(rest)
        add_ref = rest.pop(0) if addend is not None else None
        if into is not None:
            rest.pop(0)
        out_ref, scaled_ref = rest

        @pl.when(pl.program_id(0) == 0)
        def _():
            scaled_ref[...] = (coef_ref[...] * grad_ref[...].astype(jnp.float32)).astype(jnp.bfloat16)

        acc = jnp.dot(hid_ref[...], scaled_ref[...], preferred_element_type=jnp.float32)
        for k in range(per_tile):
            part = acc[k * rows:(k + 1) * rows, :]
            if add_ref is not None:
                part = part + add_ref[k]
            if grouped:
                out_ref[k, 0] = part
            else:
                out_ref[k] = part

    in_specs = [
        pl.BlockSpec((t, 1), lambda i, c: (0, 0)),
        pl.BlockSpec((t, width), lambda i, c: (0, c[0])),
        pl.BlockSpec((ROW_TILE, t), lambda i, c: (i, 0)),
    ]
    args = [col, coef, grad, hid_t]
    if addend is not None:
        in_specs.append(pl.BlockSpec((per_tile, rows, width), lambda i, c: (i, 0, 0)))
        args.append(addend)
    aliases = {}
    if into is not None:
        in_specs.append(pl.BlockSpec(memory_space=pl.ANY))
        aliases = {len(args): 0}
        args.append(into)
    if grouped:
        out_shape = jax.ShapeDtypeStruct((n_dp, n_slots, rows, width), jnp.float32)
        out_spec = pl.BlockSpec((per_tile, 1, rows, width), lambda i, c: (i, slot, 0, 0))
    else:
        out_shape = jax.ShapeDtypeStruct((n_dp, rows, width), jnp.float32)
        out_spec = pl.BlockSpec((per_tile, rows, width), lambda i, c: (i, 0, 0))
    grid_spec = pltpu.PrefetchScalarGridSpec(
        num_scalar_prefetch=1,
        grid=(n_tiles,),
        in_specs=in_specs,
        out_specs=out_spec,
        scratch_shapes=[pltpu.VMEM((t, width), jnp.bfloat16)],
    )
    extra = hb * width * 4 if addend is not None else 0
    return pl.pallas_call(
        kernel,
        grid_spec=grid_spec,
        out_shape=out_shape,
        input_output_aliases=aliases,
        compiler_params=pltpu.CompilerParams(vmem_limit_bytes=48 * 1024 * 1024),
        cost_estimate=pl.CostEstimate(
            flops=2 * hb * t * width, transcendentals=0,
            bytes_accessed=hb * t * 2 + t * width * 2 + hb * width * 4 + extra,
        ),
    )(*args)


def z_reduce_scatter(x, axis, n):
    _, r, c = x.shape

    def kernel(x_ref, out_ref, recv, send_sem, recv_sem):
        me = lax.axis_index(axis)
        barrier = pltpu.get_barrier_semaphore()
        for d in range(1, n):
            peer = lax.rem(me + d, n)
            pl.semaphore_signal(barrier, inc=1, device_id={axis: peer},
                                device_id_type=pl.DeviceIdType.MESH)
        pl.semaphore_wait(barrier, n - 1)
        copies = []
        for d in range(1, n):
            peer = lax.rem(me + d, n)
            cp = pltpu.make_async_remote_copy(
                src_ref=x_ref.at[peer], dst_ref=recv.at[me],
                send_sem=send_sem.at[d], recv_sem=recv_sem.at[me],
                device_id={axis: peer}, device_id_type=pl.DeviceIdType.MESH)
            cp.start()
            copies.append(cp)
        total = x_ref[me]
        for d in range(1, n):
            src = lax.rem(me + n - d, n)
            incoming = pltpu.make_async_remote_copy(
                src_ref=x_ref.at[src], dst_ref=recv.at[src],
                send_sem=send_sem.at[d], recv_sem=recv_sem.at[src],
                device_id={axis: src}, device_id_type=pl.DeviceIdType.MESH)
            incoming.wait_recv()
            total = total + recv[src]
        for cp in copies:
            cp.wait_send()
        out_ref[...] = total

    return pl.pallas_call(
        kernel,
        out_shape=jax.ShapeDtypeStruct((r, c), jnp.float32),
        in_specs=[pl.BlockSpec(memory_space=pltpu.VMEM)],
        out_specs=pl.BlockSpec(memory_space=pltpu.VMEM),
        scratch_shapes=[
            pltpu.VMEM((n, r, c), jnp.float32),
            pltpu.SemaphoreType.DMA((n,)),
            pltpu.SemaphoreType.DMA((n,)),
        ],
        compiler_params=pltpu.CompilerParams(collective_id=0, has_side_effects=True),
        cost_estimate=pl.CostEstimate(flops=n * r * c, transcendentals=0,
                                      bytes_accessed=3 * n * r * c * 4),
    )(x)


def shards(hidden_acts, out_grad, old_logp, new_logp, roll_len, resp_mask, advantage):
    n_dp = lax.axis_size("dp")
    n_z = lax.axis_size("z")
    n_core = lax.axis_size("core")
    width = old_logp.shape[1]
    ctx = lax.axis_index("z") * n_core + lax.axis_index("core")
    places = ctx * width + jnp.arange(width, dtype=jnp.int32)
    masked = jnp.where(places < roll_len[0], resp_mask[0], 0).astype(jnp.float32)
    gap_sum, count = lax.psum(
        (jnp.sum((new_logp[0] - old_logp[0]) * masked), jnp.sum(masked)), ("z", "core")
    )
    adv = advantage[0, 0]
    length = jnp.maximum(count, 1.0)
    seq_ratio = jnp.exp(gap_sum / length)
    active = jnp.where(adv >= 0.0, seq_ratio < 1.0 + CLIP_HIGH, seq_ratio > 1.0 - CLIP_LOW).astype(
        jnp.float32
    )
    seq_weight = -adv * seq_ratio * active / length
    token_coef = (masked * seq_weight)[:, None]
    d = out_grad.shape[1]
    col = d // (n_z * n_core)
    hid_t = hidden_acts.T
    core = lax.axis_index("core").astype(jnp.int32)

    def col_index(k, which):
        return jnp.reshape(k * n_core + which, (1,)).astype(jnp.int32)

    got = []
    for k in range(n_z):
        theirs = block_matmul(col_index(k, 1 - core), token_coef, out_grad, hid_t, n_dp, col)
        got.append(lax.ppermute(theirs, "core", perm=[(0, 1), (1, 0)]))
    chip = None
    for k in range(n_z):
        chip = block_matmul(col_index(k, core), token_coef, out_grad, hid_t, n_dp, col,
                            addend=got[k], into=chip, slot=k, n_slots=n_z)
    rows = lax.psum_scatter(chip, "dp", scatter_dimension=0, tiled=True)[0]
    return z_reduce_scatter(rows, "z", n_z)


def solution(mesh):
    n_dp, n_ctx = mesh.shape["dp"], mesh.shape["ctx"]
    fine = Mesh(np.asarray(mesh.devices).reshape(n_dp, n_ctx // 2, 2), ("dp", "z", "core"))
    tok = ("dp", "z", "core")
    placed = (
        P(tok, None),
        P(tok, None),
        P("dp", ("z", "core")),
        P("dp", ("z", "core")),
        P("dp"),
        P("dp", ("z", "core")),
        P("dp", None),
    )
    return jax.shard_map(
        shards, mesh=fine, in_specs=placed, out_specs=P("dp", ("z", "core")), check_vma=False
    )
```

```python
import jax
import jax.numpy as jnp
import numpy as np
from jax import lax
from jax.experimental import pallas as pl
from jax.experimental.pallas import tpu as pltpu
from jax.sharding import Mesh
from jax.sharding import PartitionSpec as P

CLIP_LOW = 0.0003
CLIP_HIGH = 0.0004
ROW_TILE = 768
Z_FIRST = 256


def block_matmul(col, coef, grad, hid_t, n_dp, width, addend=None, into=None, slot=0, n_slots=1):
    hb, t = hid_t.shape
    rows = hb // n_dp
    per_tile = ROW_TILE // rows
    n_tiles = hb // ROW_TILE
    grouped = n_slots > 1
    keep = width - Z_FIRST

    def kernel(col_ref, coef_ref, grad_ref, hid_ref, *rest):
        rest = list(rest)
        add_ref = rest.pop(0) if addend is not None else None
        if into is not None:
            rest.pop(0)
            rest.pop(0)
        if grouped:
            out_ref, zout_ref, scaled_ref = rest
        else:
            out_ref, scaled_ref = rest

        @pl.when(pl.program_id(0) == 0)
        def _():
            scaled_ref[...] = (coef_ref[...] * grad_ref[...].astype(jnp.float32)).astype(jnp.bfloat16)

        acc = jnp.dot(hid_ref[...], scaled_ref[...], preferred_element_type=jnp.float32)
        for k in range(per_tile):
            part = acc[k * rows:(k + 1) * rows, :]
            if add_ref is not None:
                part = part + add_ref[k]
            if grouped:
                out_ref[k, 0] = part[:, :keep]
                zout_ref[0, k] = part[:, keep:]
            else:
                out_ref[k] = part

    in_specs = [
        pl.BlockSpec((t, 1), lambda i, c: (0, 0)),
        pl.BlockSpec((t, width), lambda i, c: (0, c[0])),
        pl.BlockSpec((ROW_TILE, t), lambda i, c: (i, 0)),
    ]
    args = [col, coef, grad, hid_t]
    if addend is not None:
        in_specs.append(pl.BlockSpec((per_tile, rows, width), lambda i, c: (i, 0, 0)))
        args.append(addend)
    aliases = {}
    if into is not None:
        in_specs += [pl.BlockSpec(memory_space=pl.ANY)] * 2
        aliases = {len(args): 0, len(args) + 1: 1}
        args += list(into)
    if grouped:
        out_shape = (jax.ShapeDtypeStruct((n_dp, n_slots, rows, keep), jnp.float32),
                     jax.ShapeDtypeStruct((n_slots, n_dp, rows, Z_FIRST), jnp.float32))
        out_spec = (pl.BlockSpec((per_tile, 1, rows, keep), lambda i, c: (i, slot, 0, 0)),
                    pl.BlockSpec((1, per_tile, rows, Z_FIRST), lambda i, c: (slot, i, 0, 0)))
    else:
        out_shape = jax.ShapeDtypeStruct((n_dp, rows, width), jnp.float32)
        out_spec = pl.BlockSpec((per_tile, rows, width), lambda i, c: (i, 0, 0))
    grid_spec = pltpu.PrefetchScalarGridSpec(
        num_scalar_prefetch=1,
        grid=(n_tiles,),
        in_specs=in_specs,
        out_specs=out_spec,
        scratch_shapes=[pltpu.VMEM((t, width), jnp.bfloat16)],
    )
    extra = hb * width * 4 if addend is not None else 0
    return pl.pallas_call(
        kernel,
        grid_spec=grid_spec,
        out_shape=out_shape,
        input_output_aliases=aliases,
        compiler_params=pltpu.CompilerParams(vmem_limit_bytes=48 * 1024 * 1024),
        cost_estimate=pl.CostEstimate(
            flops=2 * hb * t * width, transcendentals=0,
            bytes_accessed=hb * t * 2 + t * width * 2 + hb * width * 4 + extra,
        ),
    )(*args)


def z_reduce_scatter(x, axis, n, cid):
    rest_shape = x.shape[1:]
    size = 1
    for s in x.shape:
        size *= s

    def kernel(x_ref, out_ref, recv, send_sem, recv_sem):
        me = lax.axis_index(axis)
        barrier = pltpu.get_barrier_semaphore()
        for d in range(1, n):
            peer = lax.rem(me + d, n)
            pl.semaphore_signal(barrier, inc=1, device_id={axis: peer},
                                device_id_type=pl.DeviceIdType.MESH)
        pl.semaphore_wait(barrier, n - 1)
        copies = []
        for d in range(1, n):
            peer = lax.rem(me + d, n)
            cp = pltpu.make_async_remote_copy(
                src_ref=x_ref.at[peer], dst_ref=recv.at[me],
                send_sem=send_sem.at[d], recv_sem=recv_sem.at[me],
                device_id={axis: peer}, device_id_type=pl.DeviceIdType.MESH)
            cp.start()
            copies.append(cp)
        total = x_ref[me]
        for d in range(1, n):
            src = lax.rem(me + n - d, n)
            incoming = pltpu.make_async_remote_copy(
                src_ref=x_ref.at[src], dst_ref=recv.at[src],
                send_sem=send_sem.at[d], recv_sem=recv_sem.at[src],
                device_id={axis: src}, device_id_type=pl.DeviceIdType.MESH)
            incoming.wait_recv()
            total = total + recv[src]
        for cp in copies:
            cp.wait_send()
        out_ref[...] = total

    return pl.pallas_call(
        kernel,
        out_shape=jax.ShapeDtypeStruct(rest_shape, jnp.float32),
        in_specs=[pl.BlockSpec(memory_space=pltpu.VMEM)],
        out_specs=pl.BlockSpec(memory_space=pltpu.VMEM),
        scratch_shapes=[
            pltpu.VMEM(x.shape, jnp.float32),
            pltpu.SemaphoreType.DMA((n,)),
            pltpu.SemaphoreType.DMA((n,)),
        ],
        compiler_params=pltpu.CompilerParams(
            collective_id=cid, has_side_effects=True, vmem_limit_bytes=40 * 1024 * 1024),
        cost_estimate=pl.CostEstimate(flops=size, transcendentals=0, bytes_accessed=3 * size * 4),
    )(x)


def shards(hidden_acts, out_grad, old_logp, new_logp, roll_len, resp_mask, advantage):
    n_dp = lax.axis_size("dp")
    n_z = lax.axis_size("z")
    n_core = lax.axis_size("core")
    width = old_logp.shape[1]
    ctx = lax.axis_index("z") * n_core + lax.axis_index("core")
    places = ctx * width + jnp.arange(width, dtype=jnp.int32)
    masked = jnp.where(places < roll_len[0], resp_mask[0], 0).astype(jnp.float32)
    gap_sum, count = lax.psum(
        (jnp.sum((new_logp[0] - old_logp[0]) * masked), jnp.sum(masked)), ("z", "core")
    )
    adv = advantage[0, 0]
    length = jnp.maximum(count, 1.0)
    seq_ratio = jnp.exp(gap_sum / length)
    active = jnp.where(adv >= 0.0, seq_ratio < 1.0 + CLIP_HIGH, seq_ratio > 1.0 - CLIP_LOW).astype(
        jnp.float32
    )
    seq_weight = -adv * seq_ratio * active / length
    token_coef = (masked * seq_weight)[:, None]
    d = out_grad.shape[1]
    col = d // (n_z * n_core)
    hid_t = hidden_acts.T
    core = lax.axis_index("core").astype(jnp.int32)

    def col_index(k, which):
        return jnp.reshape(k * n_core + which, (1,)).astype(jnp.int32)

    got = []
    for k in range(n_z):
        theirs = block_matmul(col_index(k, 1 - core), token_coef, out_grad, hid_t, n_dp, col)
        got.append(lax.ppermute(theirs, "core", perm=[(0, 1), (1, 0)]))
    chip = None
    for k in range(n_z):
        chip = block_matmul(col_index(k, core), token_coef, out_grad, hid_t, n_dp, col,
                            addend=got[k], into=chip, slot=k, n_slots=n_z)
    dp_first, z_first = chip
    rows = lax.psum_scatter(dp_first, "dp", scatter_dimension=0, tiled=True)[0]
    late = z_reduce_scatter(z_first, "z", n_z, 0)
    late = lax.psum_scatter(late, "dp", scatter_dimension=0, tiled=True)[0]
    early = z_reduce_scatter(rows, "z", n_z, 1)
    return jnp.concatenate([early, late], axis=1)


def solution(mesh):
    n_dp, n_ctx = mesh.shape["dp"], mesh.shape["ctx"]
    fine = Mesh(np.asarray(mesh.devices).reshape(n_dp, n_ctx // 2, 2), ("dp", "z", "core"))
    tok = ("dp", "z", "core")
    placed = (
        P(tok, None),
        P(tok, None),
        P("dp", ("z", "core")),
        P("dp", ("z", "core")),
        P("dp"),
        P("dp", ("z", "core")),
        P("dp", None),
    )
    return jax.shard_map(
        shards, mesh=fine, in_specs=placed, out_specs=P("dp", ("z", "core")), check_vma=False
    )
```

```python
import jax
import jax.numpy as jnp
import numpy as np
from jax import lax
from jax.experimental import pallas as pl
from jax.experimental.pallas import tpu as pltpu
from jax.sharding import Mesh
from jax.sharding import PartitionSpec as P

CLIP_LOW = 0.0003
CLIP_HIGH = 0.0004
ROW_TILE = 768


def block_matmul(col, coef, grad, hid_t, n_dp, width, addend=None, into=None, slot=0, n_slots=1):
    hb, t = hid_t.shape
    rows = hb // n_dp
    per_tile = ROW_TILE // rows
    n_tiles = hb // ROW_TILE
    grouped = n_slots > 1

    def kernel(col_ref, coef_ref, grad_ref, hid_ref, *rest):
        rest = list(rest)
        add_ref = rest.pop(0) if addend is not None else None
        if into is not None:
            rest.pop(0)
        out_ref, scaled_ref = rest

        @pl.when(pl.program_id(0) == 0)
        def _():
            scaled_ref[...] = (coef_ref[...] * grad_ref[...].astype(jnp.float32)).astype(jnp.bfloat16)

        acc = jnp.dot(hid_ref[...], scaled_ref[...], preferred_element_type=jnp.float32)
        for k in range(per_tile):
            part = acc[k * rows:(k + 1) * rows, :]
            if add_ref is not None:
                part = part + add_ref[k]
            if grouped:
                out_ref[k, 0] = part
            else:
                out_ref[k] = part

    in_specs = [
        pl.BlockSpec((t, 1), lambda i, c: (0, 0)),
        pl.BlockSpec((t, width), lambda i, c: (0, c[0])),
        pl.BlockSpec((ROW_TILE, t), lambda i, c: (i, 0)),
    ]
    args = [col, coef, grad, hid_t]
    if addend is not None:
        in_specs.append(pl.BlockSpec((per_tile, rows, width), lambda i, c: (i, 0, 0)))
        args.append(addend)
    aliases = {}
    if into is not None:
        in_specs.append(pl.BlockSpec(memory_space=pl.ANY))
        aliases = {len(args): 0}
        args.append(into)
    if grouped:
        out_shape = jax.ShapeDtypeStruct((n_dp, n_slots, rows, width), jnp.float32)
        out_spec = pl.BlockSpec((per_tile, 1, rows, width), lambda i, c: (i, slot, 0, 0))
    else:
        out_shape = jax.ShapeDtypeStruct((n_dp, rows, width), jnp.float32)
        out_spec = pl.BlockSpec((per_tile, rows, width), lambda i, c: (i, 0, 0))
    grid_spec = pltpu.PrefetchScalarGridSpec(
        num_scalar_prefetch=1,
        grid=(n_tiles,),
        in_specs=in_specs,
        out_specs=out_spec,
        scratch_shapes=[pltpu.VMEM((t, width), jnp.bfloat16)],
    )
    extra = hb * width * 4 if addend is not None else 0
    return pl.pallas_call(
        kernel,
        grid_spec=grid_spec,
        out_shape=out_shape,
        input_output_aliases=aliases,
        compiler_params=pltpu.CompilerParams(vmem_limit_bytes=48 * 1024 * 1024),
        cost_estimate=pl.CostEstimate(
            flops=2 * hb * t * width, transcendentals=0,
            bytes_accessed=hb * t * 2 + t * width * 2 + hb * width * 4 + extra,
        ),
    )(*args)


def z_reduce_scatter(x, axis, n):
    _, r, c = x.shape

    def kernel(x_ref, out_ref, recv, send_sem, recv_sem):
        me = lax.axis_index(axis)
        barrier = pltpu.get_barrier_semaphore()
        for d in range(1, n):
            peer = lax.rem(me + d, n)
            pl.semaphore_signal(barrier, inc=1, device_id={axis: peer},
                                device_id_type=pl.DeviceIdType.MESH)
        pl.semaphore_wait(barrier, n - 1)
        copies = []
        for d in range(1, n):
            peer = lax.rem(me + d, n)
            cp = pltpu.make_async_remote_copy(
                src_ref=x_ref.at[peer], dst_ref=recv.at[me],
                send_sem=send_sem.at[d], recv_sem=recv_sem.at[me],
                device_id={axis: peer}, device_id_type=pl.DeviceIdType.MESH)
            cp.start()
            copies.append(cp)
        total = x_ref[me]
        for d in range(1, n):
            src = lax.rem(me + n - d, n)
            incoming = pltpu.make_async_remote_copy(
                src_ref=x_ref.at[src], dst_ref=recv.at[src],
                send_sem=send_sem.at[d], recv_sem=recv_sem.at[src],
                device_id={axis: src}, device_id_type=pl.DeviceIdType.MESH)
            incoming.wait_recv()
            total = total + recv[src]
        for cp in copies:
            cp.wait_send()
        out_ref[...] = total

    return pl.pallas_call(
        kernel,
        out_shape=jax.ShapeDtypeStruct((r, c), jnp.float32),
        in_specs=[pl.BlockSpec(memory_space=pltpu.VMEM)],
        out_specs=pl.BlockSpec(memory_space=pltpu.VMEM),
        scratch_shapes=[
            pltpu.VMEM((n, r, c), jnp.float32),
            pltpu.SemaphoreType.DMA((n,)),
            pltpu.SemaphoreType.DMA((n,)),
        ],
        compiler_params=pltpu.CompilerParams(collective_id=0, has_side_effects=True),
        cost_estimate=pl.CostEstimate(flops=n * r * c, transcendentals=0,
                                      bytes_accessed=3 * n * r * c * 4),
    )(x)

def ctx_sum(vals, n_z, n_core):
    n = n_z * n_core

    def kernel(v_ref, out_ref, recv, send_sem, recv_sem):
        me = lax.axis_index("z") * n_core + lax.axis_index("core")

        def peer_of(p):
            return {"z": p // n_core, "core": p % n_core}

        barrier = pltpu.get_barrier_semaphore()
        for d in range(1, n):
            pl.semaphore_signal(barrier, inc=1, device_id=peer_of(lax.rem(me + d, n)),
                                device_id_type=pl.DeviceIdType.MESH)
        pl.semaphore_wait(barrier, n - 1)
        copies = []
        for d in range(1, n):
            cp = pltpu.make_async_remote_copy(
                src_ref=v_ref, dst_ref=recv.at[me],
                send_sem=send_sem.at[d], recv_sem=recv_sem.at[me],
                device_id=peer_of(lax.rem(me + d, n)), device_id_type=pl.DeviceIdType.MESH)
            cp.start()
            copies.append(cp)
        recv[me] = v_ref[...]
        for d in range(1, n):
            src = lax.rem(me + n - d, n)
            pltpu.make_async_remote_copy(
                src_ref=v_ref, dst_ref=recv.at[src],
                send_sem=send_sem.at[d], recv_sem=recv_sem.at[src],
                device_id=peer_of(src), device_id_type=pl.DeviceIdType.MESH).wait_recv()
        total = recv[0]
        for p in range(1, n):
            total = total + recv[p]
        for cp in copies:
            cp.wait_send()
        out_ref[...] = total

    return pl.pallas_call(
        kernel,
        out_shape=jax.ShapeDtypeStruct(vals.shape, jnp.float32),
        in_specs=[pl.BlockSpec(memory_space=pltpu.VMEM)],
        out_specs=pl.BlockSpec(memory_space=pltpu.VMEM),
        scratch_shapes=[
            pltpu.VMEM((n,) + vals.shape, jnp.float32),
            pltpu.SemaphoreType.DMA((n,)),
            pltpu.SemaphoreType.DMA((n,)),
        ],
        compiler_params=pltpu.CompilerParams(collective_id=1, has_side_effects=True),
    )(vals)


def shards(hidden_acts, out_grad, old_logp, new_logp, roll_len, resp_mask, advantage):
    n_dp = lax.axis_size("dp")
    n_z = lax.axis_size("z")
    n_core = lax.axis_size("core")
    width = old_logp.shape[1]
    ctx = lax.axis_index("z") * n_core + lax.axis_index("core")
    places = ctx * width + jnp.arange(width, dtype=jnp.int32)
    masked = jnp.where(places < roll_len[0], resp_mask[0], 0).astype(jnp.float32)
    lanes = jnp.arange(128, dtype=jnp.int32)[None, :]
    local = jnp.where(lanes == 0, jnp.sum((new_logp[0] - old_logp[0]) * masked),
                      jnp.where(lanes == 1, jnp.sum(masked), 0.0))
    summed = ctx_sum(jnp.broadcast_to(local, (8, 128)).astype(jnp.float32), n_z, n_core)
    gap_sum, count = summed[0, 0], summed[0, 1]
    adv = advantage[0, 0]
    length = jnp.maximum(count, 1.0)
    seq_ratio = jnp.exp(gap_sum / length)
    active = jnp.where(adv >= 0.0, seq_ratio < 1.0 + CLIP_HIGH, seq_ratio > 1.0 - CLIP_LOW).astype(
        jnp.float32
    )
    seq_weight = -adv * seq_ratio * active / length
    token_coef = (masked * seq_weight)[:, None]
    d = out_grad.shape[1]
    col = d // (n_z * n_core)
    hid_t = hidden_acts.T
    core = lax.axis_index("core").astype(jnp.int32)

    def col_index(k, which):
        return jnp.reshape(k * n_core + which, (1,)).astype(jnp.int32)

    got = []
    for k in range(n_z):
        theirs = block_matmul(col_index(k, 1 - core), token_coef, out_grad, hid_t, n_dp, col)
        got.append(lax.ppermute(theirs, "core", perm=[(0, 1), (1, 0)]))
    chip = None
    for k in range(n_z):
        chip = block_matmul(col_index(k, core), token_coef, out_grad, hid_t, n_dp, col,
                            addend=got[k], into=chip, slot=k, n_slots=n_z)
    rows = lax.psum_scatter(chip, "dp", scatter_dimension=0, tiled=True)[0]
    return z_reduce_scatter(rows, "z", n_z)


def solution(mesh):
    n_dp, n_ctx = mesh.shape["dp"], mesh.shape["ctx"]
    fine = Mesh(np.asarray(mesh.devices).reshape(n_dp, n_ctx // 2, 2), ("dp", "z", "core"))
    tok = ("dp", "z", "core")
    placed = (
        P(tok, None),
        P(tok, None),
        P("dp", ("z", "core")),
        P("dp", ("z", "core")),
        P("dp"),
        P("dp", ("z", "core")),
        P("dp", None),
    )
    return jax.shard_map(
        shards, mesh=fine, in_specs=placed, out_specs=P("dp", ("z", "core")), check_vma=False
    )
```

```python
import jax
import jax.numpy as jnp
import numpy as np
from jax import lax
from jax.experimental import pallas as pl
from jax.experimental.pallas import tpu as pltpu
from jax.sharding import Mesh
from jax.sharding import PartitionSpec as P

CLIP_LOW = 0.0003
CLIP_HIGH = 0.0004
ROW_TILE = 768
Z_FIRST = 128


def block_matmul(col, coef, grad, hid_t, n_dp, width, addend=None, into=None, slot=0, n_slots=1):
    hb, t = hid_t.shape
    rows = hb // n_dp
    per_tile = ROW_TILE // rows
    n_tiles = hb // ROW_TILE
    grouped = n_slots > 1
    keep = width - Z_FIRST

    def kernel(col_ref, coef_ref, grad_ref, hid_ref, *rest):
        rest = list(rest)
        add_ref = rest.pop(0) if addend is not None else None
        if into is not None:
            rest.pop(0)
            rest.pop(0)
        if grouped:
            out_ref, zout_ref, scaled_ref = rest
        else:
            out_ref, scaled_ref = rest

        @pl.when(pl.program_id(0) == 0)
        def _():
            scaled_ref[...] = (coef_ref[...] * grad_ref[...].astype(jnp.float32)).astype(jnp.bfloat16)

        acc = jnp.dot(hid_ref[...], scaled_ref[...], preferred_element_type=jnp.float32)
        for k in range(per_tile):
            part = acc[k * rows:(k + 1) * rows, :]
            if add_ref is not None:
                part = part + add_ref[k]
            if grouped:
                out_ref[k, 0] = part[:, :keep]
                zout_ref[0, k] = part[:, keep:]
            else:
                out_ref[k] = part

    in_specs = [
        pl.BlockSpec((t, 1), lambda i, c: (0, 0)),
        pl.BlockSpec((t, width), lambda i, c: (0, c[0])),
        pl.BlockSpec((ROW_TILE, t), lambda i, c: (i, 0)),
    ]
    args = [col, coef, grad, hid_t]
    if addend is not None:
        in_specs.append(pl.BlockSpec((per_tile, rows, width), lambda i, c: (i, 0, 0)))
        args.append(addend)
    aliases = {}
    if into is not None:
        in_specs += [pl.BlockSpec(memory_space=pl.ANY)] * 2
        aliases = {len(args): 0, len(args) + 1: 1}
        args += list(into)
    if grouped:
        out_shape = (jax.ShapeDtypeStruct((n_dp, n_slots, rows, keep), jnp.float32),
                     jax.ShapeDtypeStruct((n_slots, n_dp, rows, Z_FIRST), jnp.float32))
        out_spec = (pl.BlockSpec((per_tile, 1, rows, keep), lambda i, c: (i, slot, 0, 0)),
                    pl.BlockSpec((1, per_tile, rows, Z_FIRST), lambda i, c: (slot, i, 0, 0)))
    else:
        out_shape = jax.ShapeDtypeStruct((n_dp, rows, width), jnp.float32)
        out_spec = pl.BlockSpec((per_tile, rows, width), lambda i, c: (i, 0, 0))
    grid_spec = pltpu.PrefetchScalarGridSpec(
        num_scalar_prefetch=1,
        grid=(n_tiles,),
        in_specs=in_specs,
        out_specs=out_spec,
        scratch_shapes=[pltpu.VMEM((t, width), jnp.bfloat16)],
    )
    extra = hb * width * 4 if addend is not None else 0
    return pl.pallas_call(
        kernel,
        grid_spec=grid_spec,
        out_shape=out_shape,
        input_output_aliases=aliases,
        compiler_params=pltpu.CompilerParams(vmem_limit_bytes=48 * 1024 * 1024),
        cost_estimate=pl.CostEstimate(
            flops=2 * hb * t * width, transcendentals=0,
            bytes_accessed=hb * t * 2 + t * width * 2 + hb * width * 4 + extra,
        ),
    )(*args)


def z_reduce_scatter(x, axis, n, cid):
    rest_shape = x.shape[1:]
    size = 1
    for s in x.shape:
        size *= s

    def kernel(x_ref, out_ref, recv, send_sem, recv_sem):
        me = lax.axis_index(axis)
        barrier = pltpu.get_barrier_semaphore()
        for d in range(1, n):
            peer = lax.rem(me + d, n)
            pl.semaphore_signal(barrier, inc=1, device_id={axis: peer},
                                device_id_type=pl.DeviceIdType.MESH)
        pl.semaphore_wait(barrier, n - 1)
        copies = []
        for d in range(1, n):
            peer = lax.rem(me + d, n)
            cp = pltpu.make_async_remote_copy(
                src_ref=x_ref.at[peer], dst_ref=recv.at[me],
                send_sem=send_sem.at[d], recv_sem=recv_sem.at[me],
                device_id={axis: peer}, device_id_type=pl.DeviceIdType.MESH)
            cp.start()
            copies.append(cp)
        total = x_ref[me]
        for d in range(1, n):
            src = lax.rem(me + n - d, n)
            incoming = pltpu.make_async_remote_copy(
                src_ref=x_ref.at[src], dst_ref=recv.at[src],
                send_sem=send_sem.at[d], recv_sem=recv_sem.at[src],
                device_id={axis: src}, device_id_type=pl.DeviceIdType.MESH)
            incoming.wait_recv()
            total = total + recv[src]
        for cp in copies:
            cp.wait_send()
        out_ref[...] = total

    return pl.pallas_call(
        kernel,
        out_shape=jax.ShapeDtypeStruct(rest_shape, jnp.float32),
        in_specs=[pl.BlockSpec(memory_space=pltpu.VMEM)],
        out_specs=pl.BlockSpec(memory_space=pltpu.VMEM),
        scratch_shapes=[
            pltpu.VMEM(x.shape, jnp.float32),
            pltpu.SemaphoreType.DMA((n,)),
            pltpu.SemaphoreType.DMA((n,)),
        ],
        compiler_params=pltpu.CompilerParams(
            collective_id=cid, has_side_effects=True, vmem_limit_bytes=40 * 1024 * 1024),
        cost_estimate=pl.CostEstimate(flops=size, transcendentals=0, bytes_accessed=3 * size * 4),
    )(x)

def ctx_sum(vals, n_z, n_core):
    n = n_z * n_core

    def kernel(v_ref, out_ref, recv, send_sem, recv_sem):
        me = lax.axis_index("z") * n_core + lax.axis_index("core")

        def peer_of(p):
            return {"z": p // n_core, "core": p % n_core}

        barrier = pltpu.get_barrier_semaphore()
        for d in range(1, n):
            pl.semaphore_signal(barrier, inc=1, device_id=peer_of(lax.rem(me + d, n)),
                                device_id_type=pl.DeviceIdType.MESH)
        pl.semaphore_wait(barrier, n - 1)
        copies = []
        for d in range(1, n):
            cp = pltpu.make_async_remote_copy(
                src_ref=v_ref, dst_ref=recv.at[me],
                send_sem=send_sem.at[d], recv_sem=recv_sem.at[me],
                device_id=peer_of(lax.rem(me + d, n)), device_id_type=pl.DeviceIdType.MESH)
            cp.start()
            copies.append(cp)
        recv[me] = v_ref[...]
        for d in range(1, n):
            src = lax.rem(me + n - d, n)
            pltpu.make_async_remote_copy(
                src_ref=v_ref, dst_ref=recv.at[src],
                send_sem=send_sem.at[d], recv_sem=recv_sem.at[src],
                device_id=peer_of(src), device_id_type=pl.DeviceIdType.MESH).wait_recv()
        total = recv[0]
        for p in range(1, n):
            total = total + recv[p]
        for cp in copies:
            cp.wait_send()
        out_ref[...] = total

    return pl.pallas_call(
        kernel,
        out_shape=jax.ShapeDtypeStruct(vals.shape, jnp.float32),
        in_specs=[pl.BlockSpec(memory_space=pltpu.VMEM)],
        out_specs=pl.BlockSpec(memory_space=pltpu.VMEM),
        scratch_shapes=[
            pltpu.VMEM((n,) + vals.shape, jnp.float32),
            pltpu.SemaphoreType.DMA((n,)),
            pltpu.SemaphoreType.DMA((n,)),
        ],
        compiler_params=pltpu.CompilerParams(collective_id=1, has_side_effects=True),
    )(vals)


def shards(hidden_acts, out_grad, old_logp, new_logp, roll_len, resp_mask, advantage):
    n_dp = lax.axis_size("dp")
    n_z = lax.axis_size("z")
    n_core = lax.axis_size("core")
    width = old_logp.shape[1]
    ctx = lax.axis_index("z") * n_core + lax.axis_index("core")
    places = ctx * width + jnp.arange(width, dtype=jnp.int32)
    masked = jnp.where(places < roll_len[0], resp_mask[0], 0).astype(jnp.float32)
    lanes = jnp.arange(128, dtype=jnp.int32)[None, :]
    local = jnp.where(lanes == 0, jnp.sum((new_logp[0] - old_logp[0]) * masked),
                      jnp.where(lanes == 1, jnp.sum(masked), 0.0))
    summed = ctx_sum(jnp.broadcast_to(local, (8, 128)).astype(jnp.float32), n_z, n_core)
    gap_sum, count = summed[0, 0], summed[0, 1]
    adv = advantage[0, 0]
    length = jnp.maximum(count, 1.0)
    seq_ratio = jnp.exp(gap_sum / length)
    active = jnp.where(adv >= 0.0, seq_ratio < 1.0 + CLIP_HIGH, seq_ratio > 1.0 - CLIP_LOW).astype(
        jnp.float32
    )
    seq_weight = -adv * seq_ratio * active / length
    token_coef = (masked * seq_weight)[:, None]
    d = out_grad.shape[1]
    col = d // (n_z * n_core)
    hid_t = hidden_acts.T
    core = lax.axis_index("core").astype(jnp.int32)

    def col_index(k, which):
        return jnp.reshape(k * n_core + which, (1,)).astype(jnp.int32)

    got = []
    for k in range(n_z):
        theirs = block_matmul(col_index(k, 1 - core), token_coef, out_grad, hid_t, n_dp, col)
        got.append(lax.ppermute(theirs, "core", perm=[(0, 1), (1, 0)]))
    chip = None
    for k in range(n_z):
        chip = block_matmul(col_index(k, core), token_coef, out_grad, hid_t, n_dp, col,
                            addend=got[k], into=chip, slot=k, n_slots=n_z)
    dp_first, z_first = chip
    rows = lax.psum_scatter(dp_first, "dp", scatter_dimension=0, tiled=True)[0]
    late = z_reduce_scatter(z_first, "z", n_z, 0)
    late = z_reduce_scatter(late, "dp", n_dp, 2)
    early = z_reduce_scatter(rows, "z", n_z, 3)
    return jnp.concatenate([early, late], axis=1)


def solution(mesh):
    n_dp, n_ctx = mesh.shape["dp"], mesh.shape["ctx"]
    fine = Mesh(np.asarray(mesh.devices).reshape(n_dp, n_ctx // 2, 2), ("dp", "z", "core"))
    tok = ("dp", "z", "core")
    placed = (
        P(tok, None),
        P(tok, None),
        P("dp", ("z", "core")),
        P("dp", ("z", "core")),
        P("dp"),
        P("dp", ("z", "core")),
        P("dp", None),
    )
    return jax.shard_map(
        shards, mesh=fine, in_specs=placed, out_specs=P("dp", ("z", "core")), check_vma=False
    )
```

```python
import jax
import jax.numpy as jnp
import numpy as np
from jax import lax
from jax.experimental import pallas as pl
from jax.experimental.pallas import tpu as pltpu
from jax.sharding import Mesh
from jax.sharding import PartitionSpec as P

CLIP_LOW = 0.0003
CLIP_HIGH = 0.0004
ROW_TILE = 768
Z_FIRST = 128


def block_matmul(col, coef, grad, hid_t, n_dp, width, lo, hi, addend=None, into=None, slot=0,
                 n_slots=1, z_major=False):
    hb, t = hid_t.shape
    rows = hb // n_dp
    per_tile = ROW_TILE // rows
    n_tiles = hb // ROW_TILE
    grouped = n_slots > 1
    w = hi - lo

    def kernel(col_ref, coef_ref, grad_ref, hid_ref, *rest):
        rest = list(rest)
        add_ref = rest.pop(0) if addend is not None else None
        if into is not None:
            rest.pop(0)
        out_ref, scaled_ref = rest

        @pl.when(pl.program_id(0) == 0)
        def _():
            scaled_ref[...] = (coef_ref[...] * grad_ref[:, lo:hi].astype(jnp.float32)).astype(
                jnp.bfloat16)

        acc = jnp.dot(hid_ref[...], scaled_ref[...], preferred_element_type=jnp.float32)
        for k in range(per_tile):
            part = acc[k * rows:(k + 1) * rows, :]
            if add_ref is not None:
                part = part + add_ref[k]
            if not grouped:
                out_ref[k] = part
            elif z_major:
                out_ref[0, k] = part
            else:
                out_ref[k, 0] = part

    in_specs = [
        pl.BlockSpec((t, 1), lambda i, c: (0, 0)),
        pl.BlockSpec((t, width), lambda i, c: (0, c[0])),
        pl.BlockSpec((ROW_TILE, t), lambda i, c: (i, 0)),
    ]
    args = [col, coef, grad, hid_t]
    if addend is not None:
        in_specs.append(pl.BlockSpec((per_tile, rows, w), lambda i, c: (i, 0, 0)))
        args.append(addend)
    aliases = {}
    if into is not None:
        in_specs.append(pl.BlockSpec(memory_space=pl.ANY))
        aliases = {len(args): 0}
        args.append(into)
    if not grouped:
        out_shape = jax.ShapeDtypeStruct((n_dp, rows, w), jnp.float32)
        out_spec = pl.BlockSpec((per_tile, rows, w), lambda i, c: (i, 0, 0))
    elif z_major:
        out_shape = jax.ShapeDtypeStruct((n_slots, n_dp, rows, w), jnp.float32)
        out_spec = pl.BlockSpec((1, per_tile, rows, w), lambda i, c: (slot, i, 0, 0))
    else:
        out_shape = jax.ShapeDtypeStruct((n_dp, n_slots, rows, w), jnp.float32)
        out_spec = pl.BlockSpec((per_tile, 1, rows, w), lambda i, c: (i, slot, 0, 0))
    grid_spec = pltpu.PrefetchScalarGridSpec(
        num_scalar_prefetch=1,
        grid=(n_tiles,),
        in_specs=in_specs,
        out_specs=out_spec,
        scratch_shapes=[pltpu.VMEM((t, w), jnp.bfloat16)],
    )
    extra = hb * w * 4 if addend is not None else 0
    return pl.pallas_call(
        kernel,
        grid_spec=grid_spec,
        out_shape=out_shape,
        input_output_aliases=aliases,
        compiler_params=pltpu.CompilerParams(vmem_limit_bytes=48 * 1024 * 1024),
        cost_estimate=pl.CostEstimate(
            flops=2 * hb * t * w, transcendentals=0,
            bytes_accessed=hb * t * 2 + t * width * 2 + hb * w * 4 + extra,
        ),
    )(*args)


def z_reduce_scatter(x, axis, n, cid):
    rest_shape = x.shape[1:]
    size = 1
    for s in x.shape:
        size *= s

    def kernel(x_ref, out_ref, recv, send_sem, recv_sem):
        me = lax.axis_index(axis)
        barrier = pltpu.get_barrier_semaphore()
        for d in range(1, n):
            peer = lax.rem(me + d, n)
            pl.semaphore_signal(barrier, inc=1, device_id={axis: peer},
                                device_id_type=pl.DeviceIdType.MESH)
        pl.semaphore_wait(barrier, n - 1)
        copies = []
        for d in range(1, n):
            peer = lax.rem(me + d, n)
            cp = pltpu.make_async_remote_copy(
                src_ref=x_ref.at[peer], dst_ref=recv.at[me],
                send_sem=send_sem.at[d], recv_sem=recv_sem.at[me],
                device_id={axis: peer}, device_id_type=pl.DeviceIdType.MESH)
            cp.start()
            copies.append(cp)
        total = x_ref[me]
        for d in range(1, n):
            src = lax.rem(me + n - d, n)
            incoming = pltpu.make_async_remote_copy(
                src_ref=x_ref.at[src], dst_ref=recv.at[src],
                send_sem=send_sem.at[d], recv_sem=recv_sem.at[src],
                device_id={axis: src}, device_id_type=pl.DeviceIdType.MESH)
            incoming.wait_recv()
            total = total + recv[src]
        for cp in copies:
            cp.wait_send()
        out_ref[...] = total

    return pl.pallas_call(
        kernel,
        out_shape=jax.ShapeDtypeStruct(rest_shape, jnp.float32),
        in_specs=[pl.BlockSpec(memory_space=pltpu.VMEM)],
        out_specs=pl.BlockSpec(memory_space=pltpu.VMEM),
        scratch_shapes=[
            pltpu.VMEM(x.shape, jnp.float32),
            pltpu.SemaphoreType.DMA((n,)),
            pltpu.SemaphoreType.DMA((n,)),
        ],
        compiler_params=pltpu.CompilerParams(
            collective_id=cid, has_side_effects=True, vmem_limit_bytes=40 * 1024 * 1024),
        cost_estimate=pl.CostEstimate(flops=size, transcendentals=0, bytes_accessed=3 * size * 4),
    )(x)

def ctx_sum(vals, n_z, n_core):
    n = n_z * n_core

    def kernel(v_ref, out_ref, recv, send_sem, recv_sem):
        me = lax.axis_index("z") * n_core + lax.axis_index("core")

        def peer_of(p):
            return {"z": p // n_core, "core": p % n_core}

        barrier = pltpu.get_barrier_semaphore()
        for d in range(1, n):
            pl.semaphore_signal(barrier, inc=1, device_id=peer_of(lax.rem(me + d, n)),
                                device_id_type=pl.DeviceIdType.MESH)
        pl.semaphore_wait(barrier, n - 1)
        copies = []
        for d in range(1, n):
            cp = pltpu.make_async_remote_copy(
                src_ref=v_ref, dst_ref=recv.at[me],
                send_sem=send_sem.at[d], recv_sem=recv_sem.at[me],
                device_id=peer_of(lax.rem(me + d, n)), device_id_type=pl.DeviceIdType.MESH)
            cp.start()
            copies.append(cp)
        recv[me] = v_ref[...]
        for d in range(1, n):
            src = lax.rem(me + n - d, n)
            pltpu.make_async_remote_copy(
                src_ref=v_ref, dst_ref=recv.at[src],
                send_sem=send_sem.at[d], recv_sem=recv_sem.at[src],
                device_id=peer_of(src), device_id_type=pl.DeviceIdType.MESH).wait_recv()
        total = recv[0]
        for p in range(1, n):
            total = total + recv[p]
        for cp in copies:
            cp.wait_send()
        out_ref[...] = total

    return pl.pallas_call(
        kernel,
        out_shape=jax.ShapeDtypeStruct(vals.shape, jnp.float32),
        in_specs=[pl.BlockSpec(memory_space=pltpu.VMEM)],
        out_specs=pl.BlockSpec(memory_space=pltpu.VMEM),
        scratch_shapes=[
            pltpu.VMEM((n,) + vals.shape, jnp.float32),
            pltpu.SemaphoreType.DMA((n,)),
            pltpu.SemaphoreType.DMA((n,)),
        ],
        compiler_params=pltpu.CompilerParams(collective_id=1, has_side_effects=True),
    )(vals)


def shards(hidden_acts, out_grad, old_logp, new_logp, roll_len, resp_mask, advantage):
    n_dp = lax.axis_size("dp")
    n_z = lax.axis_size("z")
    n_core = lax.axis_size("core")
    width = old_logp.shape[1]
    ctx = lax.axis_index("z") * n_core + lax.axis_index("core")
    places = ctx * width + jnp.arange(width, dtype=jnp.int32)
    masked = jnp.where(places < roll_len[0], resp_mask[0], 0).astype(jnp.float32)
    lanes = jnp.arange(128, dtype=jnp.int32)[None, :]
    local = jnp.where(lanes == 0, jnp.sum((new_logp[0] - old_logp[0]) * masked),
                      jnp.where(lanes == 1, jnp.sum(masked), 0.0))
    summed = ctx_sum(jnp.broadcast_to(local, (8, 128)).astype(jnp.float32), n_z, n_core)
    gap_sum, count = summed[0, 0], summed[0, 1]
    adv = advantage[0, 0]
    length = jnp.maximum(count, 1.0)
    seq_ratio = jnp.exp(gap_sum / length)
    active = jnp.where(adv >= 0.0, seq_ratio < 1.0 + CLIP_HIGH, seq_ratio > 1.0 - CLIP_LOW).astype(
        jnp.float32
    )
    seq_weight = -adv * seq_ratio * active / length
    token_coef = (masked * seq_weight)[:, None]
    d = out_grad.shape[1]
    col = d // (n_z * n_core)
    hid_t = hidden_acts.T
    core = lax.axis_index("core").astype(jnp.int32)

    def col_index(k, which):
        return jnp.reshape(k * n_core + which, (1,)).astype(jnp.int32)

    swap = [(0, 1), (1, 0)]

    def pre_reduced(lo, hi, z_major):
        got = []
        for k in range(n_z):
            theirs = block_matmul(col_index(k, 1 - core), token_coef, out_grad, hid_t, n_dp, col,
                                  lo, hi)
            got.append(lax.ppermute(theirs, "core", perm=swap))
        chip = None
        for k in range(n_z):
            chip = block_matmul(col_index(k, core), token_coef, out_grad, hid_t, n_dp, col, lo, hi,
                                addend=got[k], into=chip, slot=k, n_slots=n_z, z_major=z_major)
        return chip

    keep = col - Z_FIRST
    dp_first = pre_reduced(0, keep, False)
    rows = lax.psum_scatter(dp_first, "dp", scatter_dimension=0, tiled=True)[0]
    z_first = pre_reduced(keep, col, True)
    late = z_reduce_scatter(z_first, "z", n_z, 0)
    late = z_reduce_scatter(late, "dp", n_dp, 2)
    early = z_reduce_scatter(rows, "z", n_z, 3)
    return jnp.concatenate([early, late], axis=1)


def solution(mesh):
    n_dp, n_ctx = mesh.shape["dp"], mesh.shape["ctx"]
    fine = Mesh(np.asarray(mesh.devices).reshape(n_dp, n_ctx // 2, 2), ("dp", "z", "core"))
    tok = ("dp", "z", "core")
    placed = (
        P(tok, None),
        P(tok, None),
        P("dp", ("z", "core")),
        P("dp", ("z", "core")),
        P("dp"),
        P("dp", ("z", "core")),
        P("dp", None),
    )
    return jax.shard_map(
        shards, mesh=fine, in_specs=placed, out_specs=P("dp", ("z", "core")), check_vma=False
    )
```

```python
import jax
import jax.numpy as jnp
import numpy as np
from jax import lax
from jax.experimental import pallas as pl
from jax.experimental.pallas import tpu as pltpu
from jax.sharding import Mesh
from jax.sharding import PartitionSpec as P

CLIP_LOW = 0.0003
CLIP_HIGH = 0.0004
ROW_TILE = 768
Z_FIRST = 128


def block_matmul(col, coef, grad, hid_t, n_dp, width, lo, hi, n_blocks, addend=None, into=None,
                 slot=0, n_slots=1, z_major=False):
    hb, t = hid_t.shape
    rows = hb // n_dp
    per_tile = ROW_TILE // rows
    n_tiles = hb // ROW_TILE
    w = hi - lo

    def kernel(col_ref, coef_ref, grad_ref, hid_ref, *rest):
        rest = list(rest)
        add_ref = rest.pop(0) if addend is not None else None
        if into is not None:
            rest.pop(0)
        out_ref, scaled_ref = rest

        @pl.when(pl.program_id(1) == 0)
        def _():
            scaled_ref[...] = (coef_ref[...] * grad_ref[:, lo:hi].astype(jnp.float32)).astype(
                jnp.bfloat16)

        acc = jnp.dot(hid_ref[...], scaled_ref[...], preferred_element_type=jnp.float32)
        for k in range(per_tile):
            part = acc[k * rows:(k + 1) * rows, :]
            if add_ref is None:
                out_ref[0, k] = part
                continue
            part = part + add_ref[0, k]
            if z_major:
                out_ref[0, k] = part
            else:
                out_ref[k, 0] = part

    in_specs = [
        pl.BlockSpec((t, 1), lambda b, i, c: (0, 0)),
        pl.BlockSpec((t, width), lambda b, i, c: (0, c[0] + 2 * b)),
        pl.BlockSpec((ROW_TILE, t), lambda b, i, c: (i, 0)),
    ]
    args = [col, coef, grad, hid_t]
    if addend is not None:
        in_specs.append(pl.BlockSpec((1, per_tile, rows, w), lambda b, i, c: (b, i, 0, 0)))
        args.append(addend)
    aliases = {}
    if into is not None:
        in_specs.append(pl.BlockSpec(memory_space=pl.ANY))
        aliases = {len(args): 0}
        args.append(into)
    if addend is None:
        out_shape = jax.ShapeDtypeStruct((n_blocks, n_dp, rows, w), jnp.float32)
        out_spec = pl.BlockSpec((1, per_tile, rows, w), lambda b, i, c: (b, i, 0, 0))
    elif z_major:
        out_shape = jax.ShapeDtypeStruct((n_slots, n_dp, rows, w), jnp.float32)
        out_spec = pl.BlockSpec((1, per_tile, rows, w), lambda b, i, c: (slot + b, i, 0, 0))
    else:
        out_shape = jax.ShapeDtypeStruct((n_dp, n_slots, rows, w), jnp.float32)
        out_spec = pl.BlockSpec((per_tile, 1, rows, w), lambda b, i, c: (i, slot + b, 0, 0))
    grid_spec = pltpu.PrefetchScalarGridSpec(
        num_scalar_prefetch=1,
        grid=(n_blocks, n_tiles),
        in_specs=in_specs,
        out_specs=out_spec,
        scratch_shapes=[pltpu.VMEM((t, w), jnp.bfloat16)],
    )
    extra = hb * w * 4 * n_blocks if addend is not None else 0
    return pl.pallas_call(
        kernel,
        grid_spec=grid_spec,
        out_shape=out_shape,
        input_output_aliases=aliases,
        compiler_params=pltpu.CompilerParams(vmem_limit_bytes=48 * 1024 * 1024),
        cost_estimate=pl.CostEstimate(
            flops=2 * hb * t * w * n_blocks, transcendentals=0,
            bytes_accessed=hb * t * 2 + (t * width * 2 + hb * w * 4) * n_blocks + extra,
        ),
    )(*args)


def z_reduce_scatter(x, axis, n, cid):
    rest_shape = x.shape[1:]
    size = 1
    for s in x.shape:
        size *= s

    def kernel(x_ref, out_ref, recv, send_sem, recv_sem):
        me = lax.axis_index(axis)
        barrier = pltpu.get_barrier_semaphore()
        for d in range(1, n):
            peer = lax.rem(me + d, n)
            pl.semaphore_signal(barrier, inc=1, device_id={axis: peer},
                                device_id_type=pl.DeviceIdType.MESH)
        pl.semaphore_wait(barrier, n - 1)
        copies = []
        for d in range(1, n):
            peer = lax.rem(me + d, n)
            cp = pltpu.make_async_remote_copy(
                src_ref=x_ref.at[peer], dst_ref=recv.at[me],
                send_sem=send_sem.at[d], recv_sem=recv_sem.at[me],
                device_id={axis: peer}, device_id_type=pl.DeviceIdType.MESH)
            cp.start()
            copies.append(cp)
        total = x_ref[me]
        for d in range(1, n):
            src = lax.rem(me + n - d, n)
            incoming = pltpu.make_async_remote_copy(
                src_ref=x_ref.at[src], dst_ref=recv.at[src],
                send_sem=send_sem.at[d], recv_sem=recv_sem.at[src],
                device_id={axis: src}, device_id_type=pl.DeviceIdType.MESH)
            incoming.wait_recv()
            total = total + recv[src]
        for cp in copies:
            cp.wait_send()
        out_ref[...] = total

    return pl.pallas_call(
        kernel,
        out_shape=jax.ShapeDtypeStruct(rest_shape, jnp.float32),
        in_specs=[pl.BlockSpec(memory_space=pltpu.VMEM)],
        out_specs=pl.BlockSpec(memory_space=pltpu.VMEM),
        scratch_shapes=[
            pltpu.VMEM(x.shape, jnp.float32),
            pltpu.SemaphoreType.DMA((n,)),
            pltpu.SemaphoreType.DMA((n,)),
        ],
        compiler_params=pltpu.CompilerParams(
            collective_id=cid, has_side_effects=True, vmem_limit_bytes=40 * 1024 * 1024),
        cost_estimate=pl.CostEstimate(flops=size, transcendentals=0, bytes_accessed=3 * size * 4),
    )(x)

def ctx_sum(vals, n_z, n_core):
    n = n_z * n_core

    def kernel(v_ref, out_ref, recv, send_sem, recv_sem):
        me = lax.axis_index("z") * n_core + lax.axis_index("core")

        def peer_of(p):
            return {"z": p // n_core, "core": p % n_core}

        barrier = pltpu.get_barrier_semaphore()
        for d in range(1, n):
            pl.semaphore_signal(barrier, inc=1, device_id=peer_of(lax.rem(me + d, n)),
                                device_id_type=pl.DeviceIdType.MESH)
        pl.semaphore_wait(barrier, n - 1)
        copies = []
        for d in range(1, n):
            cp = pltpu.make_async_remote_copy(
                src_ref=v_ref, dst_ref=recv.at[me],
                send_sem=send_sem.at[d], recv_sem=recv_sem.at[me],
                device_id=peer_of(lax.rem(me + d, n)), device_id_type=pl.DeviceIdType.MESH)
            cp.start()
            copies.append(cp)
        recv[me] = v_ref[...]
        for d in range(1, n):
            src = lax.rem(me + n - d, n)
            pltpu.make_async_remote_copy(
                src_ref=v_ref, dst_ref=recv.at[src],
                send_sem=send_sem.at[d], recv_sem=recv_sem.at[src],
                device_id=peer_of(src), device_id_type=pl.DeviceIdType.MESH).wait_recv()
        total = recv[0]
        for p in range(1, n):
            total = total + recv[p]
        for cp in copies:
            cp.wait_send()
        out_ref[...] = total

    return pl.pallas_call(
        kernel,
        out_shape=jax.ShapeDtypeStruct(vals.shape, jnp.float32),
        in_specs=[pl.BlockSpec(memory_space=pltpu.VMEM)],
        out_specs=pl.BlockSpec(memory_space=pltpu.VMEM),
        scratch_shapes=[
            pltpu.VMEM((n,) + vals.shape, jnp.float32),
            pltpu.SemaphoreType.DMA((n,)),
            pltpu.SemaphoreType.DMA((n,)),
        ],
        compiler_params=pltpu.CompilerParams(collective_id=1, has_side_effects=True),
    )(vals)


def shards(hidden_acts, out_grad, old_logp, new_logp, roll_len, resp_mask, advantage):
    n_dp = lax.axis_size("dp")
    n_z = lax.axis_size("z")
    n_core = lax.axis_size("core")
    width = old_logp.shape[1]
    ctx = lax.axis_index("z") * n_core + lax.axis_index("core")
    places = ctx * width + jnp.arange(width, dtype=jnp.int32)
    masked = jnp.where(places < roll_len[0], resp_mask[0], 0).astype(jnp.float32)
    lanes = jnp.arange(128, dtype=jnp.int32)[None, :]
    local = jnp.where(lanes == 0, jnp.sum((new_logp[0] - old_logp[0]) * masked),
                      jnp.where(lanes == 1, jnp.sum(masked), 0.0))
    summed = ctx_sum(jnp.broadcast_to(local, (8, 128)).astype(jnp.float32), n_z, n_core)
    gap_sum, count = summed[0, 0], summed[0, 1]
    adv = advantage[0, 0]
    length = jnp.maximum(count, 1.0)
    seq_ratio = jnp.exp(gap_sum / length)
    active = jnp.where(adv >= 0.0, seq_ratio < 1.0 + CLIP_HIGH, seq_ratio > 1.0 - CLIP_LOW).astype(
        jnp.float32
    )
    seq_weight = -adv * seq_ratio * active / length
    token_coef = (masked * seq_weight)[:, None]
    d = out_grad.shape[1]
    col = d // (n_z * n_core)
    hid_t = hidden_acts.T
    core = lax.axis_index("core").astype(jnp.int32)

    def col_index(k, which):
        return jnp.reshape(k * n_core + which, (1,)).astype(jnp.int32)

    swap = [(0, 1), (1, 0)]

    def pre_reduced(lo, hi, z_major, per_call):
        got = []
        for k in range(0, n_z, per_call):
            theirs = block_matmul(col_index(k, 1 - core), token_coef, out_grad, hid_t, n_dp, col,
                                  lo, hi, per_call)
            got.append(lax.ppermute(theirs, "core", perm=swap))
        chip = None
        for j, k in enumerate(range(0, n_z, per_call)):
            chip = block_matmul(col_index(k, core), token_coef, out_grad, hid_t, n_dp, col, lo, hi,
                                per_call, addend=got[j], into=chip, slot=k, n_slots=n_z,
                                z_major=z_major)
        return chip

    keep = col - Z_FIRST
    dp_first = pre_reduced(0, keep, False, 2)
    rows = lax.psum_scatter(dp_first, "dp", scatter_dimension=0, tiled=True)[0]
    z_first = pre_reduced(keep, col, True, 1)
    late = z_reduce_scatter(z_first, "z", n_z, 0)
    late = z_reduce_scatter(late, "dp", n_dp, 2)
    early = z_reduce_scatter(rows, "z", n_z, 3)
    return jnp.concatenate([early, late], axis=1)


def solution(mesh):
    n_dp, n_ctx = mesh.shape["dp"], mesh.shape["ctx"]
    fine = Mesh(np.asarray(mesh.devices).reshape(n_dp, n_ctx // 2, 2), ("dp", "z", "core"))
    tok = ("dp", "z", "core")
    placed = (
        P(tok, None),
        P(tok, None),
        P("dp", ("z", "core")),
        P("dp", ("z", "core")),
        P("dp"),
        P("dp", ("z", "core")),
        P("dp", None),
    )
    return jax.shard_map(
        shards, mesh=fine, in_specs=placed, out_specs=P("dp", ("z", "core")), check_vma=False
    )
```

```python
import jax
import jax.numpy as jnp
import numpy as np
from jax import lax
from jax.experimental import pallas as pl
from jax.experimental.pallas import tpu as pltpu
from jax.sharding import Mesh
from jax.sharding import PartitionSpec as P

CLIP_LOW = 0.0003
CLIP_HIGH = 0.0004
ROW_TILE = 1536
Z_FIRST = 128


def block_matmul(col, coef, grad, hid_t, n_dp, width, lo, hi, n_blocks, addend=None, into=None,
                 slot=0, n_slots=1, z_major=False):
    hb, t = hid_t.shape
    rows = hb // n_dp
    per_tile = ROW_TILE // rows
    n_tiles = hb // ROW_TILE
    w = hi - lo

    def kernel(col_ref, coef_ref, grad_ref, hid_ref, *rest):
        rest = list(rest)
        add_ref = rest.pop(0) if addend is not None else None
        if into is not None:
            rest.pop(0)
        out_ref, scaled_ref = rest

        @pl.when(pl.program_id(1) == 0)
        def _():
            scaled_ref[...] = (coef_ref[...] * grad_ref[:, lo:hi].astype(jnp.float32)).astype(
                jnp.bfloat16)

        acc = jnp.dot(hid_ref[...], scaled_ref[...], preferred_element_type=jnp.float32)
        for k in range(per_tile):
            part = acc[k * rows:(k + 1) * rows, :]
            if add_ref is None:
                out_ref[0, k] = part
                continue
            part = part + add_ref[0, k]
            if z_major:
                out_ref[0, k] = part
            else:
                out_ref[k, 0] = part

    in_specs = [
        pl.BlockSpec((t, 1), lambda b, i, c: (0, 0)),
        pl.BlockSpec((t, width), lambda b, i, c: (0, c[0] + 2 * b)),
        pl.BlockSpec((ROW_TILE, t), lambda b, i, c: (i, 0)),
    ]
    args = [col, coef, grad, hid_t]
    if addend is not None:
        in_specs.append(pl.BlockSpec((1, per_tile, rows, w), lambda b, i, c: (b, i, 0, 0)))
        args.append(addend)
    aliases = {}
    if into is not None:
        in_specs.append(pl.BlockSpec(memory_space=pl.ANY))
        aliases = {len(args): 0}
        args.append(into)
    if addend is None:
        out_shape = jax.ShapeDtypeStruct((n_blocks, n_dp, rows, w), jnp.float32)
        out_spec = pl.BlockSpec((1, per_tile, rows, w), lambda b, i, c: (b, i, 0, 0))
    elif z_major:
        out_shape = jax.ShapeDtypeStruct((n_slots, n_dp, rows, w), jnp.float32)
        out_spec = pl.BlockSpec((1, per_tile, rows, w), lambda b, i, c: (slot + b, i, 0, 0))
    else:
        out_shape = jax.ShapeDtypeStruct((n_dp, n_slots, rows, w), jnp.float32)
        out_spec = pl.BlockSpec((per_tile, 1, rows, w), lambda b, i, c: (i, slot + b, 0, 0))
    grid_spec = pltpu.PrefetchScalarGridSpec(
        num_scalar_prefetch=1,
        grid=(n_blocks, n_tiles),
        in_specs=in_specs,
        out_specs=out_spec,
        scratch_shapes=[pltpu.VMEM((t, w), jnp.bfloat16)],
    )
    extra = hb * w * 4 * n_blocks if addend is not None else 0
    return pl.pallas_call(
        kernel,
        grid_spec=grid_spec,
        out_shape=out_shape,
        input_output_aliases=aliases,
        compiler_params=pltpu.CompilerParams(vmem_limit_bytes=48 * 1024 * 1024),
        cost_estimate=pl.CostEstimate(
            flops=2 * hb * t * w * n_blocks, transcendentals=0,
            bytes_accessed=hb * t * 2 + (t * width * 2 + hb * w * 4) * n_blocks + extra,
        ),
    )(*args)


def z_reduce_scatter(x, axis, n, cid):
    rest_shape = x.shape[1:]
    size = 1
    for s in x.shape:
        size *= s

    def kernel(x_ref, out_ref, recv, send_sem, recv_sem):
        me = lax.axis_index(axis)
        barrier = pltpu.get_barrier_semaphore()
        for d in range(1, n):
            peer = lax.rem(me + d, n)
            pl.semaphore_signal(barrier, inc=1, device_id={axis: peer},
                                device_id_type=pl.DeviceIdType.MESH)
        pl.semaphore_wait(barrier, n - 1)
        copies = []
        for d in range(1, n):
            peer = lax.rem(me + d, n)
            cp = pltpu.make_async_remote_copy(
                src_ref=x_ref.at[peer], dst_ref=recv.at[me],
                send_sem=send_sem.at[d], recv_sem=recv_sem.at[me],
                device_id={axis: peer}, device_id_type=pl.DeviceIdType.MESH)
            cp.start()
            copies.append(cp)
        total = x_ref[me]
        for d in range(1, n):
            src = lax.rem(me + n - d, n)
            incoming = pltpu.make_async_remote_copy(
                src_ref=x_ref.at[src], dst_ref=recv.at[src],
                send_sem=send_sem.at[d], recv_sem=recv_sem.at[src],
                device_id={axis: src}, device_id_type=pl.DeviceIdType.MESH)
            incoming.wait_recv()
            total = total + recv[src]
        for cp in copies:
            cp.wait_send()
        out_ref[...] = total

    return pl.pallas_call(
        kernel,
        out_shape=jax.ShapeDtypeStruct(rest_shape, jnp.float32),
        in_specs=[pl.BlockSpec(memory_space=pltpu.VMEM)],
        out_specs=pl.BlockSpec(memory_space=pltpu.VMEM),
        scratch_shapes=[
            pltpu.VMEM(x.shape, jnp.float32),
            pltpu.SemaphoreType.DMA((n,)),
            pltpu.SemaphoreType.DMA((n,)),
        ],
        compiler_params=pltpu.CompilerParams(
            collective_id=cid, has_side_effects=True, vmem_limit_bytes=40 * 1024 * 1024),
        cost_estimate=pl.CostEstimate(flops=size, transcendentals=0, bytes_accessed=3 * size * 4),
    )(x)

def ctx_sum(vals, n_z, n_core):
    n = n_z * n_core

    def kernel(v_ref, out_ref, recv, send_sem, recv_sem):
        me = lax.axis_index("z") * n_core + lax.axis_index("core")

        def peer_of(p):
            return {"z": p // n_core, "core": p % n_core}

        barrier = pltpu.get_barrier_semaphore()
        for d in range(1, n):
            pl.semaphore_signal(barrier, inc=1, device_id=peer_of(lax.rem(me + d, n)),
                                device_id_type=pl.DeviceIdType.MESH)
        pl.semaphore_wait(barrier, n - 1)
        copies = []
        for d in range(1, n):
            cp = pltpu.make_async_remote_copy(
                src_ref=v_ref, dst_ref=recv.at[me],
                send_sem=send_sem.at[d], recv_sem=recv_sem.at[me],
                device_id=peer_of(lax.rem(me + d, n)), device_id_type=pl.DeviceIdType.MESH)
            cp.start()
            copies.append(cp)
        recv[me] = v_ref[...]
        for d in range(1, n):
            src = lax.rem(me + n - d, n)
            pltpu.make_async_remote_copy(
                src_ref=v_ref, dst_ref=recv.at[src],
                send_sem=send_sem.at[d], recv_sem=recv_sem.at[src],
                device_id=peer_of(src), device_id_type=pl.DeviceIdType.MESH).wait_recv()
        total = recv[0]
        for p in range(1, n):
            total = total + recv[p]
        for cp in copies:
            cp.wait_send()
        out_ref[...] = total

    return pl.pallas_call(
        kernel,
        out_shape=jax.ShapeDtypeStruct(vals.shape, jnp.float32),
        in_specs=[pl.BlockSpec(memory_space=pltpu.VMEM)],
        out_specs=pl.BlockSpec(memory_space=pltpu.VMEM),
        scratch_shapes=[
            pltpu.VMEM((n,) + vals.shape, jnp.float32),
            pltpu.SemaphoreType.DMA((n,)),
            pltpu.SemaphoreType.DMA((n,)),
        ],
        compiler_params=pltpu.CompilerParams(collective_id=1, has_side_effects=True),
    )(vals)


def shards(hidden_acts, out_grad, old_logp, new_logp, roll_len, resp_mask, advantage):
    n_dp = lax.axis_size("dp")
    n_z = lax.axis_size("z")
    n_core = lax.axis_size("core")
    width = old_logp.shape[1]
    ctx = lax.axis_index("z") * n_core + lax.axis_index("core")
    places = ctx * width + jnp.arange(width, dtype=jnp.int32)
    masked = jnp.where(places < roll_len[0], resp_mask[0], 0).astype(jnp.float32)
    lanes = jnp.arange(128, dtype=jnp.int32)[None, :]
    local = jnp.where(lanes == 0, jnp.sum((new_logp[0] - old_logp[0]) * masked),
                      jnp.where(lanes == 1, jnp.sum(masked), 0.0))
    summed = ctx_sum(jnp.broadcast_to(local, (8, 128)).astype(jnp.float32), n_z, n_core)
    gap_sum, count = summed[0, 0], summed[0, 1]
    adv = advantage[0, 0]
    length = jnp.maximum(count, 1.0)
    seq_ratio = jnp.exp(gap_sum / length)
    active = jnp.where(adv >= 0.0, seq_ratio < 1.0 + CLIP_HIGH, seq_ratio > 1.0 - CLIP_LOW).astype(
        jnp.float32
    )
    seq_weight = -adv * seq_ratio * active / length
    token_coef = (masked * seq_weight)[:, None]
    d = out_grad.shape[1]
    col = d // (n_z * n_core)
    hid_t = hidden_acts.T
    core = lax.axis_index("core").astype(jnp.int32)

    def col_index(k, which):
        return jnp.reshape(k * n_core + which, (1,)).astype(jnp.int32)

    swap = [(0, 1), (1, 0)]

    def pre_reduced(lo, hi, z_major, per_call):
        got = []
        for k in range(0, n_z, per_call):
            theirs = block_matmul(col_index(k, 1 - core), token_coef, out_grad, hid_t, n_dp, col,
                                  lo, hi, per_call)
            got.append(lax.ppermute(theirs, "core", perm=swap))
        chip = None
        for j, k in enumerate(range(0, n_z, per_call)):
            chip = block_matmul(col_index(k, core), token_coef, out_grad, hid_t, n_dp, col, lo, hi,
                                per_call, addend=got[j], into=chip, slot=k, n_slots=n_z,
                                z_major=z_major)
        return chip

    keep = col - Z_FIRST
    dp_first = pre_reduced(0, keep, False, 2)
    rows = lax.psum_scatter(dp_first, "dp", scatter_dimension=0, tiled=True)[0]
    z_first = pre_reduced(keep, col, True, n_z)
    late = z_reduce_scatter(z_first, "z", n_z, 0)
    late = z_reduce_scatter(late, "dp", n_dp, 2)
    early = z_reduce_scatter(rows, "z", n_z, 3)
    return jnp.concatenate([early, late], axis=1)


def solution(mesh):
    n_dp, n_ctx = mesh.shape["dp"], mesh.shape["ctx"]
    fine = Mesh(np.asarray(mesh.devices).reshape(n_dp, n_ctx // 2, 2), ("dp", "z", "core"))
    tok = ("dp", "z", "core")
    placed = (
        P(tok, None),
        P(tok, None),
        P("dp", ("z", "core")),
        P("dp", ("z", "core")),
        P("dp"),
        P("dp", ("z", "core")),
        P("dp", None),
    )
    return jax.shard_map(
        shards, mesh=fine, in_specs=placed, out_specs=P("dp", ("z", "core")), check_vma=False
    )
```

```python
import jax
import jax.numpy as jnp
import numpy as np
from jax import lax
from jax.experimental import pallas as pl
from jax.experimental.pallas import tpu as pltpu
from jax.sharding import Mesh
from jax.sharding import PartitionSpec as P

CLIP_LOW = 0.0003
CLIP_HIGH = 0.0004
ROW_TILE = 1536
Z_FIRST = 128


def block_matmul(col, coef, grad, hid_t, n_dp, width, lo, hi, n_blocks, addend=None, into=None,
                 slot=0, n_slots=1, z_major=False):
    hb, t = hid_t.shape
    rows = hb // n_dp
    per_tile = ROW_TILE // rows
    n_tiles = hb // ROW_TILE
    w = hi - lo

    def kernel(col_ref, w_ref, grad_ref, hid_ref, *rest):
        rest = list(rest)
        add_ref = rest.pop(0) if addend is not None else None
        if into is not None:
            rest.pop(0)
        out_ref, scaled_ref = rest

        @pl.when(pl.program_id(1) == 0)
        def _():
            scaled_ref[...] = (w_ref[0] * grad_ref[:, lo:hi].astype(jnp.float32)).astype(
                jnp.bfloat16)

        acc = jnp.dot(hid_ref[...], scaled_ref[...], preferred_element_type=jnp.float32)
        for k in range(per_tile):
            part = acc[k * rows:(k + 1) * rows, :]
            if add_ref is None:
                out_ref[0, k] = part
                continue
            part = part + add_ref[0, k]
            if z_major:
                out_ref[0, k] = part
            else:
                out_ref[k, 0] = part

    in_specs = [
        pl.BlockSpec(memory_space=pltpu.SMEM),
        pl.BlockSpec((t, width), lambda b, i, c: (0, c[0] + 2 * b)),
        pl.BlockSpec((ROW_TILE, t), lambda b, i, c: (i, 0)),
    ]
    args = [col, coef, grad, hid_t]
    if addend is not None:
        in_specs.append(pl.BlockSpec((1, per_tile, rows, w), lambda b, i, c: (b, i, 0, 0)))
        args.append(addend)
    aliases = {}
    if into is not None:
        in_specs.append(pl.BlockSpec(memory_space=pl.ANY))
        aliases = {len(args): 0}
        args.append(into)
    if addend is None:
        out_shape = jax.ShapeDtypeStruct((n_blocks, n_dp, rows, w), jnp.float32)
        out_spec = pl.BlockSpec((1, per_tile, rows, w), lambda b, i, c: (b, i, 0, 0))
    elif z_major:
        out_shape = jax.ShapeDtypeStruct((n_slots, n_dp, rows, w), jnp.float32)
        out_spec = pl.BlockSpec((1, per_tile, rows, w), lambda b, i, c: (slot + b, i, 0, 0))
    else:
        out_shape = jax.ShapeDtypeStruct((n_dp, n_slots, rows, w), jnp.float32)
        out_spec = pl.BlockSpec((per_tile, 1, rows, w), lambda b, i, c: (i, slot + b, 0, 0))
    grid_spec = pltpu.PrefetchScalarGridSpec(
        num_scalar_prefetch=1,
        grid=(n_blocks, n_tiles),
        in_specs=in_specs,
        out_specs=out_spec,
        scratch_shapes=[pltpu.VMEM((t, w), jnp.bfloat16)],
    )
    extra = hb * w * 4 * n_blocks if addend is not None else 0
    return pl.pallas_call(
        kernel,
        grid_spec=grid_spec,
        out_shape=out_shape,
        input_output_aliases=aliases,
        compiler_params=pltpu.CompilerParams(vmem_limit_bytes=48 * 1024 * 1024),
        cost_estimate=pl.CostEstimate(
            flops=2 * hb * t * w * n_blocks, transcendentals=0,
            bytes_accessed=hb * t * 2 + (t * width * 2 + hb * w * 4) * n_blocks + extra,
        ),
    )(*args)


def z_reduce_scatter(x, axis, n, cid):
    rest_shape = x.shape[1:]
    size = 1
    for s in x.shape:
        size *= s

    def kernel(x_ref, out_ref, recv, send_sem, recv_sem):
        me = lax.axis_index(axis)
        barrier = pltpu.get_barrier_semaphore()
        for d in range(1, n):
            peer = lax.rem(me + d, n)
            pl.semaphore_signal(barrier, inc=1, device_id={axis: peer},
                                device_id_type=pl.DeviceIdType.MESH)
        pl.semaphore_wait(barrier, n - 1)
        copies = []
        for d in range(1, n):
            peer = lax.rem(me + d, n)
            cp = pltpu.make_async_remote_copy(
                src_ref=x_ref.at[peer], dst_ref=recv.at[me],
                send_sem=send_sem.at[d], recv_sem=recv_sem.at[me],
                device_id={axis: peer}, device_id_type=pl.DeviceIdType.MESH)
            cp.start()
            copies.append(cp)
        total = x_ref[me]
        for d in range(1, n):
            src = lax.rem(me + n - d, n)
            incoming = pltpu.make_async_remote_copy(
                src_ref=x_ref.at[src], dst_ref=recv.at[src],
                send_sem=send_sem.at[d], recv_sem=recv_sem.at[src],
                device_id={axis: src}, device_id_type=pl.DeviceIdType.MESH)
            incoming.wait_recv()
            total = total + recv[src]
        for cp in copies:
            cp.wait_send()
        out_ref[...] = total

    return pl.pallas_call(
        kernel,
        out_shape=jax.ShapeDtypeStruct(rest_shape, jnp.float32),
        in_specs=[pl.BlockSpec(memory_space=pltpu.VMEM)],
        out_specs=pl.BlockSpec(memory_space=pltpu.VMEM),
        scratch_shapes=[
            pltpu.VMEM(x.shape, jnp.float32),
            pltpu.SemaphoreType.DMA((n,)),
            pltpu.SemaphoreType.DMA((n,)),
        ],
        compiler_params=pltpu.CompilerParams(
            collective_id=cid, has_side_effects=True, vmem_limit_bytes=40 * 1024 * 1024),
        cost_estimate=pl.CostEstimate(flops=size, transcendentals=0, bytes_accessed=3 * size * 4),
    )(x)

def ctx_sum(vals, n_z, n_core):
    n = n_z * n_core

    def kernel(v_ref, out_ref, recv, send_sem, recv_sem):
        me = lax.axis_index("z") * n_core + lax.axis_index("core")

        def peer_of(p):
            return {"z": p // n_core, "core": p % n_core}

        barrier = pltpu.get_barrier_semaphore()
        for d in range(1, n):
            pl.semaphore_signal(barrier, inc=1, device_id=peer_of(lax.rem(me + d, n)),
                                device_id_type=pl.DeviceIdType.MESH)
        pl.semaphore_wait(barrier, n - 1)
        copies = []
        for d in range(1, n):
            cp = pltpu.make_async_remote_copy(
                src_ref=v_ref, dst_ref=recv.at[me],
                send_sem=send_sem.at[d], recv_sem=recv_sem.at[me],
                device_id=peer_of(lax.rem(me + d, n)), device_id_type=pl.DeviceIdType.MESH)
            cp.start()
            copies.append(cp)
        recv[me] = v_ref[...]
        for d in range(1, n):
            src = lax.rem(me + n - d, n)
            pltpu.make_async_remote_copy(
                src_ref=v_ref, dst_ref=recv.at[src],
                send_sem=send_sem.at[d], recv_sem=recv_sem.at[src],
                device_id=peer_of(src), device_id_type=pl.DeviceIdType.MESH).wait_recv()
        total = recv[0]
        for p in range(1, n):
            total = total + recv[p]
        for cp in copies:
            cp.wait_send()
        out_ref[...] = total

    return pl.pallas_call(
        kernel,
        out_shape=jax.ShapeDtypeStruct(vals.shape, jnp.float32),
        in_specs=[pl.BlockSpec(memory_space=pltpu.VMEM)],
        out_specs=pl.BlockSpec(memory_space=pltpu.VMEM),
        scratch_shapes=[
            pltpu.VMEM((n,) + vals.shape, jnp.float32),
            pltpu.SemaphoreType.DMA((n,)),
            pltpu.SemaphoreType.DMA((n,)),
        ],
        compiler_params=pltpu.CompilerParams(collective_id=1, has_side_effects=True),
    )(vals)


def shards(hidden_acts, out_grad, old_logp, new_logp, roll_len, resp_mask, advantage):
    n_dp = lax.axis_size("dp")
    n_z = lax.axis_size("z")
    n_core = lax.axis_size("core")
    width = old_logp.shape[1]
    ctx = lax.axis_index("z") * n_core + lax.axis_index("core")
    places = ctx * width + jnp.arange(width, dtype=jnp.int32)
    masked = jnp.where(places < roll_len[0], resp_mask[0], 0).astype(jnp.float32)
    lanes = jnp.arange(128, dtype=jnp.int32)[None, :]
    local = jnp.where(lanes == 0, jnp.sum((new_logp[0] - old_logp[0]) * masked),
                      jnp.where(lanes == 1, jnp.sum(masked), 0.0))
    summed = ctx_sum(jnp.broadcast_to(local, (8, 128)).astype(jnp.float32), n_z, n_core)
    gap_sum, count = summed[0, 0], summed[0, 1]
    adv = advantage[0, 0]
    length = jnp.maximum(count, 1.0)
    seq_ratio = jnp.exp(gap_sum / length)
    active = jnp.where(adv >= 0.0, seq_ratio < 1.0 + CLIP_HIGH, seq_ratio > 1.0 - CLIP_LOW).astype(
        jnp.float32
    )
    seq_weight = -adv * seq_ratio * active / length
    token_coef = jnp.reshape(seq_weight, (1,)).astype(jnp.float32)
    d = out_grad.shape[1]
    col = d // (n_z * n_core)
    hid_t = (hidden_acts * masked[:, None].astype(hidden_acts.dtype)).T
    core = lax.axis_index("core").astype(jnp.int32)

    def col_index(k, which):
        return jnp.reshape(k * n_core + which, (1,)).astype(jnp.int32)

    swap = [(0, 1), (1, 0)]

    def pre_reduced(lo, hi, z_major, per_call):
        got = []
        for k in range(0, n_z, per_call):
            theirs = block_matmul(col_index(k, 1 - core), token_coef, out_grad, hid_t, n_dp, col,
                                  lo, hi, per_call)
            got.append(lax.ppermute(theirs, "core", perm=swap))
        chip = None
        for j, k in enumerate(range(0, n_z, per_call)):
            chip = block_matmul(col_index(k, core), token_coef, out_grad, hid_t, n_dp, col, lo, hi,
                                per_call, addend=got[j], into=chip, slot=k, n_slots=n_z,
                                z_major=z_major)
        return chip

    keep = col - Z_FIRST
    dp_first = pre_reduced(0, keep, False, 2)
    rows = lax.psum_scatter(dp_first, "dp", scatter_dimension=0, tiled=True)[0]
    z_first = pre_reduced(keep, col, True, n_z)
    late = z_reduce_scatter(z_first, "z", n_z, 0)
    late = z_reduce_scatter(late, "dp", n_dp, 2)
    early = z_reduce_scatter(rows, "z", n_z, 3)
    return jnp.concatenate([early, late], axis=1)


def solution(mesh):
    n_dp, n_ctx = mesh.shape["dp"], mesh.shape["ctx"]
    fine = Mesh(np.asarray(mesh.devices).reshape(n_dp, n_ctx // 2, 2), ("dp", "z", "core"))
    tok = ("dp", "z", "core")
    placed = (
        P(tok, None),
        P(tok, None),
        P("dp", ("z", "core")),
        P("dp", ("z", "core")),
        P("dp"),
        P("dp", ("z", "core")),
        P("dp", None),
    )
    return jax.shard_map(
        shards, mesh=fine, in_specs=placed, out_specs=P("dp", ("z", "core")), check_vma=False
    )
```

```python
import jax
import jax.numpy as jnp
import numpy as np
from jax import lax
from jax.experimental import pallas as pl
from jax.experimental.pallas import tpu as pltpu
from jax.sharding import Mesh
from jax.sharding import PartitionSpec as P

CLIP_LOW = 0.0003
CLIP_HIGH = 0.0004
ROW_TILE = 1536
Z_FIRST = 128


def block_matmul(col, coef, grad, hid_t, n_dp, width, lo, hi, n_blocks, addend=None, into=None,
                 slot=0, n_slots=1, z_major=False):
    hb, t = hid_t.shape
    rows = hb // n_dp
    per_tile = ROW_TILE // rows
    n_tiles = hb // ROW_TILE
    w = hi - lo

    def kernel(col_ref, coef_ref, grad_ref, hid_ref, *rest):
        rest = list(rest)
        add_ref = rest.pop(0) if addend is not None else None
        if into is not None:
            rest.pop(0)
        out_ref, scaled_ref = rest

        @pl.when(pl.program_id(1) == 0)
        def _():
            scaled_ref[...] = (coef_ref[...] * grad_ref[:, lo:hi].astype(jnp.float32)).astype(
                jnp.bfloat16)

        acc = jnp.dot(hid_ref[...], scaled_ref[...], preferred_element_type=jnp.float32)
        for k in range(per_tile):
            part = acc[k * rows:(k + 1) * rows, :]
            if add_ref is None:
                out_ref[0, k] = part
                continue
            part = part + add_ref[0, k]
            if z_major:
                out_ref[0, k] = part
            else:
                out_ref[k, 0] = part

    in_specs = [
        pl.BlockSpec((t, 1), lambda b, i, c: (0, 0)),
        pl.BlockSpec((t, width), lambda b, i, c: (0, c[0] + 2 * b)),
        pl.BlockSpec((ROW_TILE, t), lambda b, i, c: (i, 0)),
    ]
    args = [col, coef, grad, hid_t]
    if addend is not None:
        in_specs.append(pl.BlockSpec((1, per_tile, rows, w), lambda b, i, c: (b, i, 0, 0)))
        args.append(addend)
    aliases = {}
    if into is not None:
        in_specs.append(pl.BlockSpec(memory_space=pl.ANY))
        aliases = {len(args): 0}
        args.append(into)
    if addend is None:
        out_shape = jax.ShapeDtypeStruct((n_blocks, n_dp, rows, w), jnp.float32)
        out_spec = pl.BlockSpec((1, per_tile, rows, w), lambda b, i, c: (b, i, 0, 0))
    elif z_major:
        out_shape = jax.ShapeDtypeStruct((n_slots, n_dp, rows, w), jnp.float32)
        out_spec = pl.BlockSpec((1, per_tile, rows, w), lambda b, i, c: (slot + b, i, 0, 0))
    else:
        out_shape = jax.ShapeDtypeStruct((n_dp, n_slots, rows, w), jnp.float32)
        out_spec = pl.BlockSpec((per_tile, 1, rows, w), lambda b, i, c: (i, slot + b, 0, 0))
    grid_spec = pltpu.PrefetchScalarGridSpec(
        num_scalar_prefetch=1,
        grid=(n_blocks, n_tiles),
        in_specs=in_specs,
        out_specs=out_spec,
        scratch_shapes=[pltpu.VMEM((t, w), jnp.bfloat16)],
    )
    extra = hb * w * 4 * n_blocks if addend is not None else 0
    return pl.pallas_call(
        kernel,
        grid_spec=grid_spec,
        out_shape=out_shape,
        input_output_aliases=aliases,
        compiler_params=pltpu.CompilerParams(vmem_limit_bytes=48 * 1024 * 1024),
        cost_estimate=pl.CostEstimate(
            flops=2 * hb * t * w * n_blocks, transcendentals=0,
            bytes_accessed=hb * t * 2 + (t * width * 2 + hb * w * 4) * n_blocks + extra,
        ),
    )(*args)


def z_reduce_scatter(x, axis, n, cid):
    rest_shape = x.shape[1:]
    size = 1
    for s in x.shape:
        size *= s

    def kernel(x_ref, out_ref, recv, send_sem, recv_sem):
        me = lax.axis_index(axis)
        barrier = pltpu.get_barrier_semaphore()
        for d in range(1, n):
            peer = lax.rem(me + d, n)
            pl.semaphore_signal(barrier, inc=1, device_id={axis: peer},
                                device_id_type=pl.DeviceIdType.MESH)
        pl.semaphore_wait(barrier, n - 1)
        copies = []
        for d in range(1, n):
            peer = lax.rem(me + d, n)
            cp = pltpu.make_async_remote_copy(
                src_ref=x_ref.at[peer], dst_ref=recv.at[me],
                send_sem=send_sem.at[d], recv_sem=recv_sem.at[me],
                device_id={axis: peer}, device_id_type=pl.DeviceIdType.MESH)
            cp.start()
            copies.append(cp)
        total = x_ref[me]
        for d in range(1, n):
            src = lax.rem(me + n - d, n)
            incoming = pltpu.make_async_remote_copy(
                src_ref=x_ref.at[src], dst_ref=recv.at[src],
                send_sem=send_sem.at[d], recv_sem=recv_sem.at[src],
                device_id={axis: src}, device_id_type=pl.DeviceIdType.MESH)
            incoming.wait_recv()
            total = total + recv[src]
        for cp in copies:
            cp.wait_send()
        out_ref[...] = total

    return pl.pallas_call(
        kernel,
        out_shape=jax.ShapeDtypeStruct(rest_shape, jnp.float32),
        in_specs=[pl.BlockSpec(memory_space=pltpu.VMEM)],
        out_specs=pl.BlockSpec(memory_space=pltpu.VMEM),
        scratch_shapes=[
            pltpu.VMEM(x.shape, jnp.float32),
            pltpu.SemaphoreType.DMA((n,)),
            pltpu.SemaphoreType.DMA((n,)),
        ],
        compiler_params=pltpu.CompilerParams(
            collective_id=cid, has_side_effects=True, vmem_limit_bytes=40 * 1024 * 1024),
        cost_estimate=pl.CostEstimate(flops=size, transcendentals=0, bytes_accessed=3 * size * 4),
    )(x)

def ctx_sum(vals, hidden, n_z, n_core):
    n = n_z * n_core

    t, hb = hidden.shape

    def kernel(v_ref, hid_ref, out_ref, ht_ref, recv, send_sem, recv_sem):
        me = lax.axis_index("z") * n_core + lax.axis_index("core")

        def peer_of(p):
            return {"z": p // n_core, "core": p % n_core}

        barrier = pltpu.get_barrier_semaphore()
        for d in range(1, n):
            pl.semaphore_signal(barrier, inc=1, device_id=peer_of(lax.rem(me + d, n)),
                                device_id_type=pl.DeviceIdType.MESH)

        @pl.loop(0, hb // 128)
        def _(j):
            cols = pl.ds(pl.multiple_of(j * 128, 128), 128)
            ht_ref[cols, :] = hid_ref[:, cols].T

        pl.semaphore_wait(barrier, n - 1)
        copies = []
        for d in range(1, n):
            cp = pltpu.make_async_remote_copy(
                src_ref=v_ref, dst_ref=recv.at[me],
                send_sem=send_sem.at[d], recv_sem=recv_sem.at[me],
                device_id=peer_of(lax.rem(me + d, n)), device_id_type=pl.DeviceIdType.MESH)
            cp.start()
            copies.append(cp)
        recv[me] = v_ref[...]
        for d in range(1, n):
            src = lax.rem(me + n - d, n)
            pltpu.make_async_remote_copy(
                src_ref=v_ref, dst_ref=recv.at[src],
                send_sem=send_sem.at[d], recv_sem=recv_sem.at[src],
                device_id=peer_of(src), device_id_type=pl.DeviceIdType.MESH).wait_recv()
        total = recv[0]
        for p in range(1, n):
            total = total + recv[p]
        for cp in copies:
            cp.wait_send()
        out_ref[...] = total

    return pl.pallas_call(
        kernel,
        out_shape=(jax.ShapeDtypeStruct(vals.shape, jnp.float32),
                   jax.ShapeDtypeStruct((hb, t), hidden.dtype)),
        in_specs=[pl.BlockSpec(memory_space=pltpu.VMEM)] * 2,
        out_specs=(pl.BlockSpec(memory_space=pltpu.VMEM),) * 2,
        scratch_shapes=[
            pltpu.VMEM((n,) + vals.shape, jnp.float32),
            pltpu.SemaphoreType.DMA((n,)),
            pltpu.SemaphoreType.DMA((n,)),
        ],
        compiler_params=pltpu.CompilerParams(
            collective_id=1, has_side_effects=True, vmem_limit_bytes=32 * 1024 * 1024),
    )(vals, hidden)


def shards(hidden_acts, out_grad, old_logp, new_logp, roll_len, resp_mask, advantage):
    n_dp = lax.axis_size("dp")
    n_z = lax.axis_size("z")
    n_core = lax.axis_size("core")
    width = old_logp.shape[1]
    ctx = lax.axis_index("z") * n_core + lax.axis_index("core")
    places = ctx * width + jnp.arange(width, dtype=jnp.int32)
    masked = jnp.where(places < roll_len[0], resp_mask[0], 0).astype(jnp.float32)
    lanes = jnp.arange(128, dtype=jnp.int32)[None, :]
    local = jnp.where(lanes == 0, jnp.sum((new_logp[0] - old_logp[0]) * masked),
                      jnp.where(lanes == 1, jnp.sum(masked), 0.0))
    summed, hid_t = ctx_sum(jnp.broadcast_to(local, (8, 128)).astype(jnp.float32), hidden_acts,
                            n_z, n_core)
    gap_sum, count = summed[0, 0], summed[0, 1]
    adv = advantage[0, 0]
    length = jnp.maximum(count, 1.0)
    seq_ratio = jnp.exp(gap_sum / length)
    active = jnp.where(adv >= 0.0, seq_ratio < 1.0 + CLIP_HIGH, seq_ratio > 1.0 - CLIP_LOW).astype(
        jnp.float32
    )
    seq_weight = -adv * seq_ratio * active / length
    token_coef = (masked * seq_weight)[:, None]
    d = out_grad.shape[1]
    col = d // (n_z * n_core)
    core = lax.axis_index("core").astype(jnp.int32)

    def col_index(k, which):
        return jnp.reshape(k * n_core + which, (1,)).astype(jnp.int32)

    swap = [(0, 1), (1, 0)]

    def pre_reduced(lo, hi, z_major, per_call):
        got = []
        for k in range(0, n_z, per_call):
            theirs = block_matmul(col_index(k, 1 - core), token_coef, out_grad, hid_t, n_dp, col,
                                  lo, hi, per_call)
            got.append(lax.ppermute(theirs, "core", perm=swap))
        chip = None
        for j, k in enumerate(range(0, n_z, per_call)):
            chip = block_matmul(col_index(k, core), token_coef, out_grad, hid_t, n_dp, col, lo, hi,
                                per_call, addend=got[j], into=chip, slot=k, n_slots=n_z,
                                z_major=z_major)
        return chip

    keep = col - Z_FIRST
    dp_first = pre_reduced(0, keep, False, 2)
    rows = lax.psum_scatter(dp_first, "dp", scatter_dimension=0, tiled=True)[0]
    z_first = pre_reduced(keep, col, True, n_z)
    late = z_reduce_scatter(z_first, "z", n_z, 0)
    late = z_reduce_scatter(late, "dp", n_dp, 2)
    early = z_reduce_scatter(rows, "z", n_z, 3)
    return jnp.concatenate([early, late], axis=1)


def solution(mesh):
    n_dp, n_ctx = mesh.shape["dp"], mesh.shape["ctx"]
    fine = Mesh(np.asarray(mesh.devices).reshape(n_dp, n_ctx // 2, 2), ("dp", "z", "core"))
    tok = ("dp", "z", "core")
    placed = (
        P(tok, None),
        P(tok, None),
        P("dp", ("z", "core")),
        P("dp", ("z", "core")),
        P("dp"),
        P("dp", ("z", "core")),
        P("dp", None),
    )
    return jax.shard_map(
        shards, mesh=fine, in_specs=placed, out_specs=P("dp", ("z", "core")), check_vma=False
    )
```

```python
import jax
import jax.numpy as jnp
import numpy as np
from jax import lax
from jax.experimental import pallas as pl
from jax.experimental.pallas import tpu as pltpu
from jax.sharding import Mesh
from jax.sharding import PartitionSpec as P

CLIP_LOW = 0.0003
CLIP_HIGH = 0.0004
ROW_TILE = 1536
Z_FIRST = 128


def block_matmul(col, coef, grad, hid_t, n_dp, width, lo, hi, n_blocks, addend=None, into=None,
                 slot=0, n_slots=1, z_major=False):
    hb, t = hid_t.shape
    rows = hb // n_dp
    per_tile = ROW_TILE // rows
    n_tiles = hb // ROW_TILE
    w = hi - lo

    def kernel(col_ref, coef_ref, grad_ref, hid_ref, *rest):
        rest = list(rest)
        add_ref = rest.pop(0) if addend is not None else None
        if into is not None:
            rest.pop(0)
        out_ref, scaled_ref = rest

        @pl.when(pl.program_id(1) == 0)
        def _():
            scaled_ref[...] = (coef_ref[...] * grad_ref[:, lo:hi].astype(jnp.float32)).astype(
                jnp.bfloat16)

        acc = jnp.dot(hid_ref[...], scaled_ref[...], preferred_element_type=jnp.float32)
        for k in range(per_tile):
            part = acc[k * rows:(k + 1) * rows, :]
            if add_ref is None:
                out_ref[0, k] = part
                continue
            part = part + add_ref[0, k]
            if z_major:
                out_ref[0, k] = part
            else:
                out_ref[k, 0] = part

    in_specs = [
        pl.BlockSpec((t, 1), lambda b, i, c: (0, 0)),
        pl.BlockSpec((t, width), lambda b, i, c: (0, c[0] + 2 * b)),
        pl.BlockSpec((ROW_TILE, t), lambda b, i, c: (i, 0)),
    ]
    args = [col, coef, grad, hid_t]
    if addend is not None:
        in_specs.append(pl.BlockSpec((1, per_tile, rows, w), lambda b, i, c: (b, i, 0, 0)))
        args.append(addend)
    aliases = {}
    if into is not None:
        in_specs.append(pl.BlockSpec(memory_space=pl.ANY))
        aliases = {len(args): 0}
        args.append(into)
    if addend is None:
        out_shape = jax.ShapeDtypeStruct((n_blocks, n_dp, rows, w), jnp.float32)
        out_spec = pl.BlockSpec((1, per_tile, rows, w), lambda b, i, c: (b, i, 0, 0))
    elif z_major:
        out_shape = jax.ShapeDtypeStruct((n_slots, n_dp, rows, w), jnp.float32)
        out_spec = pl.BlockSpec((1, per_tile, rows, w), lambda b, i, c: (slot + b, i, 0, 0))
    else:
        out_shape = jax.ShapeDtypeStruct((n_dp, n_slots, rows, w), jnp.float32)
        out_spec = pl.BlockSpec((per_tile, 1, rows, w), lambda b, i, c: (i, slot + b, 0, 0))
    grid_spec = pltpu.PrefetchScalarGridSpec(
        num_scalar_prefetch=1,
        grid=(n_blocks, n_tiles),
        in_specs=in_specs,
        out_specs=out_spec,
        scratch_shapes=[pltpu.VMEM((t, w), jnp.bfloat16)],
    )
    extra = hb * w * 4 * n_blocks if addend is not None else 0
    return pl.pallas_call(
        kernel,
        grid_spec=grid_spec,
        out_shape=out_shape,
        input_output_aliases=aliases,
        compiler_params=pltpu.CompilerParams(vmem_limit_bytes=48 * 1024 * 1024),
        cost_estimate=pl.CostEstimate(
            flops=2 * hb * t * w * n_blocks, transcendentals=0,
            bytes_accessed=hb * t * 2 + (t * width * 2 + hb * w * 4) * n_blocks + extra,
        ),
    )(*args)


def z_reduce_scatter(x, axis, n, cid):
    rest_shape = x.shape[1:]
    size = 1
    for s in x.shape:
        size *= s

    def kernel(x_ref, out_ref, recv, send_sem, recv_sem):
        me = lax.axis_index(axis)
        barrier = pltpu.get_barrier_semaphore()
        for d in range(1, n):
            peer = lax.rem(me + d, n)
            pl.semaphore_signal(barrier, inc=1, device_id={axis: peer},
                                device_id_type=pl.DeviceIdType.MESH)
        pl.semaphore_wait(barrier, n - 1)
        copies = []
        for d in range(1, n):
            peer = lax.rem(me + d, n)
            cp = pltpu.make_async_remote_copy(
                src_ref=x_ref.at[peer], dst_ref=recv.at[me],
                send_sem=send_sem.at[d], recv_sem=recv_sem.at[me],
                device_id={axis: peer}, device_id_type=pl.DeviceIdType.MESH)
            cp.start()
            copies.append(cp)
        total = x_ref[me]
        for d in range(1, n):
            src = lax.rem(me + n - d, n)
            incoming = pltpu.make_async_remote_copy(
                src_ref=x_ref.at[src], dst_ref=recv.at[src],
                send_sem=send_sem.at[d], recv_sem=recv_sem.at[src],
                device_id={axis: src}, device_id_type=pl.DeviceIdType.MESH)
            incoming.wait_recv()
            total = total + recv[src]
        for cp in copies:
            cp.wait_send()
        out_ref[...] = total

    return pl.pallas_call(
        kernel,
        out_shape=jax.ShapeDtypeStruct(rest_shape, jnp.float32),
        in_specs=[pl.BlockSpec(memory_space=pltpu.VMEM)],
        out_specs=pl.BlockSpec(memory_space=pltpu.VMEM),
        scratch_shapes=[
            pltpu.VMEM(x.shape, jnp.float32),
            pltpu.SemaphoreType.DMA((n,)),
            pltpu.SemaphoreType.DMA((n,)),
        ],
        compiler_params=pltpu.CompilerParams(
            collective_id=cid, has_side_effects=True, vmem_limit_bytes=40 * 1024 * 1024),
        cost_estimate=pl.CostEstimate(flops=size, transcendentals=0, bytes_accessed=3 * size * 4),
    )(x)

def ctx_sum(new_lp, old_lp, mask, roll_len, hidden, n_z, n_core):
    n = n_z * n_core
    t, hb = hidden.shape

    def kernel(new_ref, old_ref, mask_ref, len_ref, hid_ref, out_ref, live_ref, ht_ref,
               mine, staged, recv, copy_sem, send_sem, recv_sem):
        me = lax.axis_index("z") * n_core + lax.axis_index("core")

        def peer_of(p):
            return {"z": p // n_core, "core": p % n_core}

        barrier = pltpu.get_barrier_semaphore()
        for d in range(1, n):
            pl.semaphore_signal(barrier, inc=1, device_id=peer_of(lax.rem(me + d, n)),
                                device_id_type=pl.DeviceIdType.MESH)
        places = me * t + lax.broadcasted_iota(jnp.int32, (8, t), 1)
        live = jnp.where(places < len_ref[0], mask_ref[...], 0).astype(jnp.float32)
        gap = jnp.sum((new_ref[0:1, :] - old_ref[0:1, :]) * live[0:1, :])
        count = jnp.sum(live[0:1, :])
        lanes = lax.broadcasted_iota(jnp.int32, (8, 128), 1)
        mine[...] = jnp.where(lanes == 0, gap, jnp.where(lanes == 1, count, 0.0))
        local = pltpu.make_async_copy(mine, staged, copy_sem)
        local.start()
        live_ref[...] = live.T[:, 0:1]

        @pl.loop(0, hb // 128)
        def _(j):
            cols = pl.ds(pl.multiple_of(j * 128, 128), 128)
            ht_ref[cols, :] = hid_ref[:, cols].T

        local.wait()
        pl.semaphore_wait(barrier, n - 1)
        copies = []
        for d in range(1, n):
            cp = pltpu.make_async_remote_copy(
                src_ref=staged, dst_ref=recv.at[me],
                send_sem=send_sem.at[d], recv_sem=recv_sem.at[me],
                device_id=peer_of(lax.rem(me + d, n)), device_id_type=pl.DeviceIdType.MESH)
            cp.start()
            copies.append(cp)
        recv[me] = staged[...]
        for d in range(1, n):
            src = lax.rem(me + n - d, n)
            pltpu.make_async_remote_copy(
                src_ref=staged, dst_ref=recv.at[src],
                send_sem=send_sem.at[d], recv_sem=recv_sem.at[src],
                device_id=peer_of(src), device_id_type=pl.DeviceIdType.MESH).wait_recv()
        total = recv[0]
        for p in range(1, n):
            total = total + recv[p]
        for cp in copies:
            cp.wait_send()
        out_ref[...] = total

    vmem = pl.BlockSpec(memory_space=pltpu.VMEM)
    return pl.pallas_call(
        kernel,
        out_shape=(jax.ShapeDtypeStruct((8, 128), jnp.float32),
                   jax.ShapeDtypeStruct((t, 1), jnp.float32),
                   jax.ShapeDtypeStruct((hb, t), hidden.dtype)),
        in_specs=[vmem, vmem, vmem, pl.BlockSpec(memory_space=pltpu.SMEM), vmem],
        out_specs=(vmem, vmem, vmem),
        scratch_shapes=[
            pltpu.VMEM((8, 128), jnp.float32),
            pltpu.VMEM((8, 128), jnp.float32),
            pltpu.VMEM((n, 8, 128), jnp.float32),
            pltpu.SemaphoreType.DMA,
            pltpu.SemaphoreType.DMA((n,)),
            pltpu.SemaphoreType.DMA((n,)),
        ],
        compiler_params=pltpu.CompilerParams(
            collective_id=1, has_side_effects=True, vmem_limit_bytes=32 * 1024 * 1024),
    )(new_lp, old_lp, mask, roll_len, hidden)


def shards(hidden_acts, out_grad, old_logp, new_logp, roll_len, resp_mask, advantage):
    n_dp = lax.axis_size("dp")
    n_z = lax.axis_size("z")
    n_core = lax.axis_size("core")
    width = old_logp.shape[1]
    ctx = lax.axis_index("z") * n_core + lax.axis_index("core")
    rows8 = (8, width)
    summed, live_col, hid_t = ctx_sum(
        jnp.broadcast_to(new_logp, rows8), jnp.broadcast_to(old_logp, rows8),
        jnp.broadcast_to(resp_mask, rows8), roll_len, hidden_acts, n_z, n_core)
    gap_sum, count = summed[0, 0], summed[0, 1]
    adv = advantage[0, 0]
    length = jnp.maximum(count, 1.0)
    seq_ratio = jnp.exp(gap_sum / length)
    active = jnp.where(adv >= 0.0, seq_ratio < 1.0 + CLIP_HIGH, seq_ratio > 1.0 - CLIP_LOW).astype(
        jnp.float32
    )
    seq_weight = -adv * seq_ratio * active / length
    token_coef = live_col * seq_weight
    d = out_grad.shape[1]
    col = d // (n_z * n_core)
    core = lax.axis_index("core").astype(jnp.int32)

    def col_index(k, which):
        return jnp.reshape(k * n_core + which, (1,)).astype(jnp.int32)

    swap = [(0, 1), (1, 0)]

    def pre_reduced(lo, hi, z_major, per_call):
        got = []
        for k in range(0, n_z, per_call):
            theirs = block_matmul(col_index(k, 1 - core), token_coef, out_grad, hid_t, n_dp, col,
                                  lo, hi, per_call)
            got.append(lax.ppermute(theirs, "core", perm=swap))
        chip = None
        for j, k in enumerate(range(0, n_z, per_call)):
            chip = block_matmul(col_index(k, core), token_coef, out_grad, hid_t, n_dp, col, lo, hi,
                                per_call, addend=got[j], into=chip, slot=k, n_slots=n_z,
                                z_major=z_major)
        return chip

    keep = col - Z_FIRST
    dp_first = pre_reduced(0, keep, False, 2)
    rows = lax.psum_scatter(dp_first, "dp", scatter_dimension=0, tiled=True)[0]
    z_first = pre_reduced(keep, col, True, n_z)
    late = z_reduce_scatter(z_first, "z", n_z, 0)
    late = z_reduce_scatter(late, "dp", n_dp, 2)
    early = z_reduce_scatter(rows, "z", n_z, 3)
    return jnp.concatenate([early, late], axis=1)


def solution(mesh):
    n_dp, n_ctx = mesh.shape["dp"], mesh.shape["ctx"]
    fine = Mesh(np.asarray(mesh.devices).reshape(n_dp, n_ctx // 2, 2), ("dp", "z", "core"))
    tok = ("dp", "z", "core")
    placed = (
        P(tok, None),
        P(tok, None),
        P("dp", ("z", "core")),
        P("dp", ("z", "core")),
        P("dp"),
        P("dp", ("z", "core")),
        P("dp", None),
    )
    return jax.shard_map(
        shards, mesh=fine, in_specs=placed, out_specs=P("dp", ("z", "core")), check_vma=False
    )
```

```python
import jax
import jax.numpy as jnp
import numpy as np
from jax import lax
from jax.experimental import pallas as pl
from jax.experimental.pallas import tpu as pltpu
from jax.sharding import Mesh
from jax.sharding import PartitionSpec as P

CLIP_LOW = 0.0003
CLIP_HIGH = 0.0004
ROW_TILE = 1536
Z_FIRST = 128


def block_matmul(col, coef, grad, hid_t, n_dp, width, lo, hi, n_blocks, addend=None, into=None,
                 slot=0, n_slots=1, z_major=False):
    hb, t = hid_t.shape
    rows = hb // n_dp
    per_tile = ROW_TILE // rows
    n_tiles = hb // ROW_TILE
    w = hi - lo

    def kernel(col_ref, w_ref, grad_ref, hid_ref, *rest):
        rest = list(rest)
        add_ref = rest.pop(0) if addend is not None else None
        if into is not None:
            rest.pop(0)
        out_ref, scaled_ref = rest

        @pl.when(pl.program_id(1) == 0)
        def _():
            scaled_ref[...] = (w_ref[0] * grad_ref[:, lo:hi].astype(jnp.float32)).astype(
                jnp.bfloat16)

        acc = jnp.dot(hid_ref[...], scaled_ref[...], preferred_element_type=jnp.float32)
        for k in range(per_tile):
            part = acc[k * rows:(k + 1) * rows, :]
            if add_ref is None:
                out_ref[0, k] = part
                continue
            part = part + add_ref[0, k]
            if z_major:
                out_ref[0, k] = part
            else:
                out_ref[k, 0] = part

    in_specs = [
        pl.BlockSpec(memory_space=pltpu.SMEM),
        pl.BlockSpec((t, width), lambda b, i, c: (0, c[0] + 2 * b)),
        pl.BlockSpec((ROW_TILE, t), lambda b, i, c: (i, 0)),
    ]
    args = [col, coef, grad, hid_t]
    if addend is not None:
        in_specs.append(pl.BlockSpec((1, per_tile, rows, w), lambda b, i, c: (b, i, 0, 0)))
        args.append(addend)
    aliases = {}
    if into is not None:
        in_specs.append(pl.BlockSpec(memory_space=pl.ANY))
        aliases = {len(args): 0}
        args.append(into)
    if addend is None:
        out_shape = jax.ShapeDtypeStruct((n_blocks, n_dp, rows, w), jnp.float32)
        out_spec = pl.BlockSpec((1, per_tile, rows, w), lambda b, i, c: (b, i, 0, 0))
    elif z_major:
        out_shape = jax.ShapeDtypeStruct((n_slots, n_dp, rows, w), jnp.float32)
        out_spec = pl.BlockSpec((1, per_tile, rows, w), lambda b, i, c: (slot + b, i, 0, 0))
    else:
        out_shape = jax.ShapeDtypeStruct((n_dp, n_slots, rows, w), jnp.float32)
        out_spec = pl.BlockSpec((per_tile, 1, rows, w), lambda b, i, c: (i, slot + b, 0, 0))
    grid_spec = pltpu.PrefetchScalarGridSpec(
        num_scalar_prefetch=1,
        grid=(n_blocks, n_tiles),
        in_specs=in_specs,
        out_specs=out_spec,
        scratch_shapes=[pltpu.VMEM((t, w), jnp.bfloat16)],
    )
    extra = hb * w * 4 * n_blocks if addend is not None else 0
    return pl.pallas_call(
        kernel,
        grid_spec=grid_spec,
        out_shape=out_shape,
        input_output_aliases=aliases,
        compiler_params=pltpu.CompilerParams(vmem_limit_bytes=48 * 1024 * 1024),
        cost_estimate=pl.CostEstimate(
            flops=2 * hb * t * w * n_blocks, transcendentals=0,
            bytes_accessed=hb * t * 2 + (t * width * 2 + hb * w * 4) * n_blocks + extra,
        ),
    )(*args)


def z_reduce_scatter(x, axis, n, cid):
    rest_shape = x.shape[1:]
    size = 1
    for s in x.shape:
        size *= s

    def kernel(x_ref, out_ref, recv, send_sem, recv_sem):
        me = lax.axis_index(axis)
        barrier = pltpu.get_barrier_semaphore()
        for d in range(1, n):
            peer = lax.rem(me + d, n)
            pl.semaphore_signal(barrier, inc=1, device_id={axis: peer},
                                device_id_type=pl.DeviceIdType.MESH)
        pl.semaphore_wait(barrier, n - 1)
        copies = []
        for d in range(1, n):
            peer = lax.rem(me + d, n)
            cp = pltpu.make_async_remote_copy(
                src_ref=x_ref.at[peer], dst_ref=recv.at[me],
                send_sem=send_sem.at[d], recv_sem=recv_sem.at[me],
                device_id={axis: peer}, device_id_type=pl.DeviceIdType.MESH)
            cp.start()
            copies.append(cp)
        total = x_ref[me]
        for d in range(1, n):
            src = lax.rem(me + n - d, n)
            incoming = pltpu.make_async_remote_copy(
                src_ref=x_ref.at[src], dst_ref=recv.at[src],
                send_sem=send_sem.at[d], recv_sem=recv_sem.at[src],
                device_id={axis: src}, device_id_type=pl.DeviceIdType.MESH)
            incoming.wait_recv()
            total = total + recv[src]
        for cp in copies:
            cp.wait_send()
        out_ref[...] = total

    return pl.pallas_call(
        kernel,
        out_shape=jax.ShapeDtypeStruct(rest_shape, jnp.float32),
        in_specs=[pl.BlockSpec(memory_space=pltpu.VMEM)],
        out_specs=pl.BlockSpec(memory_space=pltpu.VMEM),
        scratch_shapes=[
            pltpu.VMEM(x.shape, jnp.float32),
            pltpu.SemaphoreType.DMA((n,)),
            pltpu.SemaphoreType.DMA((n,)),
        ],
        compiler_params=pltpu.CompilerParams(
            collective_id=cid, has_side_effects=True, vmem_limit_bytes=40 * 1024 * 1024),
        cost_estimate=pl.CostEstimate(flops=size, transcendentals=0, bytes_accessed=3 * size * 4),
    )(x)

def ctx_sum(new_lp, old_lp, mask, roll_len, hidden, n_z, n_core):
    n = n_z * n_core
    t, hb = hidden.shape

    def kernel(new_ref, old_ref, mask_ref, len_ref, hid_ref, out_ref, live_ref, ht_ref,
               mine, staged, recv, copy_sem, send_sem, recv_sem):
        me = lax.axis_index("z") * n_core + lax.axis_index("core")

        def peer_of(p):
            return {"z": p // n_core, "core": p % n_core}

        barrier = pltpu.get_barrier_semaphore()
        for d in range(1, n):
            pl.semaphore_signal(barrier, inc=1, device_id=peer_of(lax.rem(me + d, n)),
                                device_id_type=pl.DeviceIdType.MESH)
        places = me * t + lax.broadcasted_iota(jnp.int32, (8, t), 1)
        live = jnp.where(places < len_ref[0], mask_ref[...], 0).astype(jnp.float32)
        gap = jnp.sum((new_ref[0:1, :] - old_ref[0:1, :]) * live[0:1, :])
        count = jnp.sum(live[0:1, :])
        lanes = lax.broadcasted_iota(jnp.int32, (8, 128), 1)
        mine[...] = jnp.where(lanes == 0, gap, jnp.where(lanes == 1, count, 0.0))
        local = pltpu.make_async_copy(mine, staged, copy_sem)
        local.start()
        live_col = live.T[:, 0:1]
        live_ref[...] = live_col
        live_hid = live_col.astype(hid_ref.dtype)

        @pl.loop(0, hb // 128)
        def _(j):
            cols = pl.ds(pl.multiple_of(j * 128, 128), 128)
            ht_ref[cols, :] = (hid_ref[:, cols] * live_hid).T

        local.wait()
        pl.semaphore_wait(barrier, n - 1)
        copies = []
        for d in range(1, n):
            cp = pltpu.make_async_remote_copy(
                src_ref=staged, dst_ref=recv.at[me],
                send_sem=send_sem.at[d], recv_sem=recv_sem.at[me],
                device_id=peer_of(lax.rem(me + d, n)), device_id_type=pl.DeviceIdType.MESH)
            cp.start()
            copies.append(cp)
        recv[me] = staged[...]
        for d in range(1, n):
            src = lax.rem(me + n - d, n)
            pltpu.make_async_remote_copy(
                src_ref=staged, dst_ref=recv.at[src],
                send_sem=send_sem.at[d], recv_sem=recv_sem.at[src],
                device_id=peer_of(src), device_id_type=pl.DeviceIdType.MESH).wait_recv()
        total = recv[0]
        for p in range(1, n):
            total = total + recv[p]
        for cp in copies:
            cp.wait_send()
        out_ref[...] = total

    vmem = pl.BlockSpec(memory_space=pltpu.VMEM)
    return pl.pallas_call(
        kernel,
        out_shape=(jax.ShapeDtypeStruct((8, 128), jnp.float32),
                   jax.ShapeDtypeStruct((t, 1), jnp.float32),
                   jax.ShapeDtypeStruct((hb, t), hidden.dtype)),
        in_specs=[vmem, vmem, vmem, pl.BlockSpec(memory_space=pltpu.SMEM), vmem],
        out_specs=(vmem, vmem, vmem),
        scratch_shapes=[
            pltpu.VMEM((8, 128), jnp.float32),
            pltpu.VMEM((8, 128), jnp.float32),
            pltpu.VMEM((n, 8, 128), jnp.float32),
            pltpu.SemaphoreType.DMA,
            pltpu.SemaphoreType.DMA((n,)),
            pltpu.SemaphoreType.DMA((n,)),
        ],
        compiler_params=pltpu.CompilerParams(
            collective_id=1, has_side_effects=True, vmem_limit_bytes=32 * 1024 * 1024),
    )(new_lp, old_lp, mask, roll_len, hidden)


def shards(hidden_acts, out_grad, old_logp, new_logp, roll_len, resp_mask, advantage):
    n_dp = lax.axis_size("dp")
    n_z = lax.axis_size("z")
    n_core = lax.axis_size("core")
    width = old_logp.shape[1]
    ctx = lax.axis_index("z") * n_core + lax.axis_index("core")
    rows8 = (8, width)
    summed, live_col, hid_t = ctx_sum(
        jnp.broadcast_to(new_logp, rows8), jnp.broadcast_to(old_logp, rows8),
        jnp.broadcast_to(resp_mask, rows8), roll_len, hidden_acts, n_z, n_core)
    gap_sum, count = summed[0, 0], summed[0, 1]
    adv = advantage[0, 0]
    length = jnp.maximum(count, 1.0)
    seq_ratio = jnp.exp(gap_sum / length)
    active = jnp.where(adv >= 0.0, seq_ratio < 1.0 + CLIP_HIGH, seq_ratio > 1.0 - CLIP_LOW).astype(
        jnp.float32
    )
    seq_weight = -adv * seq_ratio * active / length
    token_coef = jnp.reshape(seq_weight, (1,)).astype(jnp.float32)
    d = out_grad.shape[1]
    col = d // (n_z * n_core)
    core = lax.axis_index("core").astype(jnp.int32)

    def col_index(k, which):
        return jnp.reshape(k * n_core + which, (1,)).astype(jnp.int32)

    swap = [(0, 1), (1, 0)]

    def pre_reduced(lo, hi, z_major, per_call):
        got = []
        for k in range(0, n_z, per_call):
            theirs = block_matmul(col_index(k, 1 - core), token_coef, out_grad, hid_t, n_dp, col,
                                  lo, hi, per_call)
            got.append(lax.ppermute(theirs, "core", perm=swap))
        chip = None
        for j, k in enumerate(range(0, n_z, per_call)):
            chip = block_matmul(col_index(k, core), token_coef, out_grad, hid_t, n_dp, col, lo, hi,
                                per_call, addend=got[j], into=chip, slot=k, n_slots=n_z,
                                z_major=z_major)
        return chip

    keep = col - Z_FIRST
    dp_first = pre_reduced(0, keep, False, 2)
    rows = lax.psum_scatter(dp_first, "dp", scatter_dimension=0, tiled=True)[0]
    z_first = pre_reduced(keep, col, True, n_z)
    late = z_reduce_scatter(z_first, "z", n_z, 0)
    late = z_reduce_scatter(late, "dp", n_dp, 2)
    early = z_reduce_scatter(rows, "z", n_z, 3)
    return jnp.concatenate([early, late], axis=1)


def solution(mesh):
    n_dp, n_ctx = mesh.shape["dp"], mesh.shape["ctx"]
    fine = Mesh(np.asarray(mesh.devices).reshape(n_dp, n_ctx // 2, 2), ("dp", "z", "core"))
    tok = ("dp", "z", "core")
    placed = (
        P(tok, None),
        P(tok, None),
        P("dp", ("z", "core")),
        P("dp", ("z", "core")),
        P("dp"),
        P("dp", ("z", "core")),
        P("dp", None),
    )
    return jax.shard_map(
        shards, mesh=fine, in_specs=placed, out_specs=P("dp", ("z", "core")), check_vma=False
    )
```

```python
import jax
import jax.numpy as jnp
import numpy as np
from jax import lax
from jax.experimental import pallas as pl
from jax.experimental.pallas import tpu as pltpu
from jax.sharding import Mesh
from jax.sharding import PartitionSpec as P

CLIP_LOW = 0.0003
CLIP_HIGH = 0.0004
ROW_TILE = 1536
Z_FIRST = 128


def block_matmul(col, coef, grad, hid_t, n_dp, width, lo, hi, n_blocks, addend=None, into=None,
                 slot=0, n_slots=1, z_major=False):
    hb, t = hid_t.shape
    rows = hb // n_dp
    per_tile = ROW_TILE // rows
    n_tiles = hb // ROW_TILE
    w = hi - lo

    def kernel(col_ref, w_ref, grad_ref, hid_ref, *rest):
        rest = list(rest)
        add_ref = rest.pop(0) if addend is not None else None
        if into is not None:
            rest.pop(0)
        out_ref, scaled_ref = rest

        @pl.when(pl.program_id(1) == 0)
        def _():
            scaled_ref[...] = (w_ref[0] * grad_ref[:, lo:hi].astype(jnp.float32)).astype(
                jnp.bfloat16)

        acc = jnp.dot(hid_ref[...], scaled_ref[...], preferred_element_type=jnp.float32)
        for k in range(per_tile):
            part = acc[k * rows:(k + 1) * rows, :]
            if add_ref is None:
                out_ref[0, k] = part
                continue
            part = part + add_ref[0, k]
            if z_major:
                out_ref[0, k] = part
            else:
                out_ref[k, 0] = part

    in_specs = [
        pl.BlockSpec(memory_space=pltpu.SMEM),
        pl.BlockSpec((t, width), lambda b, i, c: (0, c[0] + 2 * b)),
        pl.BlockSpec((ROW_TILE, t), lambda b, i, c: (i, 0)),
    ]
    args = [col, coef, grad, hid_t]
    if addend is not None:
        in_specs.append(pl.BlockSpec((1, per_tile, rows, w), lambda b, i, c: (b, i, 0, 0)))
        args.append(addend)
    aliases = {}
    if into is not None:
        in_specs.append(pl.BlockSpec(memory_space=pl.ANY))
        aliases = {len(args): 0}
        args.append(into)
    if addend is None:
        out_shape = jax.ShapeDtypeStruct((n_blocks, n_dp, rows, w), jnp.float32)
        out_spec = pl.BlockSpec((1, per_tile, rows, w), lambda b, i, c: (b, i, 0, 0))
    elif z_major:
        out_shape = jax.ShapeDtypeStruct((n_slots, n_dp, rows, w), jnp.float32)
        out_spec = pl.BlockSpec((1, per_tile, rows, w), lambda b, i, c: (slot + b, i, 0, 0))
    else:
        out_shape = jax.ShapeDtypeStruct((n_dp, n_slots, rows, w), jnp.float32)
        out_spec = pl.BlockSpec((per_tile, 1, rows, w), lambda b, i, c: (i, slot + b, 0, 0))
    grid_spec = pltpu.PrefetchScalarGridSpec(
        num_scalar_prefetch=1,
        grid=(n_blocks, n_tiles),
        in_specs=in_specs,
        out_specs=out_spec,
        scratch_shapes=[pltpu.VMEM((t, w), jnp.bfloat16)],
    )
    extra = hb * w * 4 * n_blocks if addend is not None else 0
    return pl.pallas_call(
        kernel,
        grid_spec=grid_spec,
        out_shape=out_shape,
        input_output_aliases=aliases,
        compiler_params=pltpu.CompilerParams(vmem_limit_bytes=48 * 1024 * 1024),
        cost_estimate=pl.CostEstimate(
            flops=2 * hb * t * w * n_blocks, transcendentals=0,
            bytes_accessed=hb * t * 2 + (t * width * 2 + hb * w * 4) * n_blocks + extra,
        ),
    )(*args)


def z_reduce_scatter(x, axis, n, cid):
    rest_shape = x.shape[1:]
    size = 1
    for s in x.shape:
        size *= s

    def kernel(x_ref, out_ref, recv, send_sem, recv_sem):
        me = lax.axis_index(axis)
        barrier = pltpu.get_barrier_semaphore()
        for d in range(1, n):
            peer = lax.rem(me + d, n)
            pl.semaphore_signal(barrier, inc=1, device_id={axis: peer},
                                device_id_type=pl.DeviceIdType.MESH)
        pl.semaphore_wait(barrier, n - 1)
        copies = []
        for d in range(1, n):
            peer = lax.rem(me + d, n)
            cp = pltpu.make_async_remote_copy(
                src_ref=x_ref.at[peer], dst_ref=recv.at[me],
                send_sem=send_sem.at[d], recv_sem=recv_sem.at[me],
                device_id={axis: peer}, device_id_type=pl.DeviceIdType.MESH)
            cp.start()
            copies.append(cp)
        total = x_ref[me]
        for d in range(1, n):
            src = lax.rem(me + n - d, n)
            incoming = pltpu.make_async_remote_copy(
                src_ref=x_ref.at[src], dst_ref=recv.at[src],
                send_sem=send_sem.at[d], recv_sem=recv_sem.at[src],
                device_id={axis: src}, device_id_type=pl.DeviceIdType.MESH)
            incoming.wait_recv()
            total = total + recv[src]
        for cp in copies:
            cp.wait_send()
        out_ref[...] = total

    return pl.pallas_call(
        kernel,
        out_shape=jax.ShapeDtypeStruct(rest_shape, jnp.float32),
        in_specs=[pl.BlockSpec(memory_space=pltpu.VMEM)],
        out_specs=pl.BlockSpec(memory_space=pltpu.VMEM),
        scratch_shapes=[
            pltpu.VMEM(x.shape, jnp.float32),
            pltpu.SemaphoreType.DMA((n,)),
            pltpu.SemaphoreType.DMA((n,)),
        ],
        compiler_params=pltpu.CompilerParams(
            collective_id=cid, has_side_effects=True, vmem_limit_bytes=40 * 1024 * 1024),
        cost_estimate=pl.CostEstimate(flops=size, transcendentals=0, bytes_accessed=3 * size * 4),
    )(x)

def ctx_sum(new_lp, old_lp, mask, roll_len, hidden, n_z, n_core):
    n = n_z * n_core
    t, hb = hidden.shape

    def kernel(new_ref, old_ref, mask_ref, len_ref, hid_hbm, out_ref, live_ref, ht_ref,
               hid_ref, mine, staged, recv, hid_sem, copy_sem, send_sem, recv_sem):
        me = lax.axis_index("z") * n_core + lax.axis_index("core")
        fetch = pltpu.make_async_copy(hid_hbm, hid_ref, hid_sem)
        fetch.start()

        def peer_of(p):
            return {"z": p // n_core, "core": p % n_core}

        barrier = pltpu.get_barrier_semaphore()
        for d in range(1, n):
            pl.semaphore_signal(barrier, inc=1, device_id=peer_of(lax.rem(me + d, n)),
                                device_id_type=pl.DeviceIdType.MESH)
        places = me * t + lax.broadcasted_iota(jnp.int32, (8, t), 1)
        mask8 = jnp.broadcast_to(mask_ref[...], (8, t))
        live = jnp.where(places < len_ref[0], mask8, 0).astype(jnp.float32)
        gap = jnp.sum((new_ref[...] - old_ref[...]) * live[0:1, :])
        count = jnp.sum(live[0:1, :])
        lanes = lax.broadcasted_iota(jnp.int32, (8, 128), 1)
        mine[...] = jnp.where(lanes == 0, gap, jnp.where(lanes == 1, count, 0.0))
        local = pltpu.make_async_copy(mine, staged, copy_sem)
        local.start()
        live_col = live.T[:, 0:1]
        live_ref[...] = live_col
        live_hid = live_col.astype(hid_ref.dtype)

        fetch.wait()

        @pl.loop(0, hb // 128)
        def _(j):
            cols = pl.ds(pl.multiple_of(j * 128, 128), 128)
            ht_ref[cols, :] = (hid_ref[:, cols] * live_hid).T

        local.wait()
        pl.semaphore_wait(barrier, n - 1)
        copies = []
        for d in range(1, n):
            cp = pltpu.make_async_remote_copy(
                src_ref=staged, dst_ref=recv.at[me],
                send_sem=send_sem.at[d], recv_sem=recv_sem.at[me],
                device_id=peer_of(lax.rem(me + d, n)), device_id_type=pl.DeviceIdType.MESH)
            cp.start()
            copies.append(cp)
        recv[me] = staged[...]
        for d in range(1, n):
            src = lax.rem(me + n - d, n)
            pltpu.make_async_remote_copy(
                src_ref=staged, dst_ref=recv.at[src],
                send_sem=send_sem.at[d], recv_sem=recv_sem.at[src],
                device_id=peer_of(src), device_id_type=pl.DeviceIdType.MESH).wait_recv()
        total = recv[0]
        for p in range(1, n):
            total = total + recv[p]
        for cp in copies:
            cp.wait_send()
        out_ref[...] = total

    vmem = pl.BlockSpec(memory_space=pltpu.VMEM)
    return pl.pallas_call(
        kernel,
        out_shape=(jax.ShapeDtypeStruct((8, 128), jnp.float32),
                   jax.ShapeDtypeStruct((t, 1), jnp.float32),
                   jax.ShapeDtypeStruct((hb, t), hidden.dtype)),
        in_specs=[vmem, vmem, vmem, pl.BlockSpec(memory_space=pltpu.SMEM),
                  pl.BlockSpec(memory_space=pl.ANY)],
        out_specs=(vmem, vmem, vmem),
        scratch_shapes=[
            pltpu.VMEM((t, hb), hidden.dtype),
            pltpu.VMEM((8, 128), jnp.float32),
            pltpu.VMEM((8, 128), jnp.float32),
            pltpu.VMEM((n, 8, 128), jnp.float32),
            pltpu.SemaphoreType.DMA,
            pltpu.SemaphoreType.DMA,
            pltpu.SemaphoreType.DMA((n,)),
            pltpu.SemaphoreType.DMA((n,)),
        ],
        compiler_params=pltpu.CompilerParams(
            collective_id=1, has_side_effects=True, vmem_limit_bytes=32 * 1024 * 1024),
    )(new_lp, old_lp, mask, roll_len, hidden)


def shards(hidden_acts, out_grad, old_logp, new_logp, roll_len, resp_mask, advantage):
    n_dp = lax.axis_size("dp")
    n_z = lax.axis_size("z")
    n_core = lax.axis_size("core")
    width = old_logp.shape[1]
    ctx = lax.axis_index("z") * n_core + lax.axis_index("core")
    summed, live_col, hid_t = ctx_sum(new_logp, old_logp, resp_mask, roll_len, hidden_acts,
                                      n_z, n_core)
    gap_sum, count = summed[0, 0], summed[0, 1]
    adv = advantage[0, 0]
    length = jnp.maximum(count, 1.0)
    seq_ratio = jnp.exp(gap_sum / length)
    active = jnp.where(adv >= 0.0, seq_ratio < 1.0 + CLIP_HIGH, seq_ratio > 1.0 - CLIP_LOW).astype(
        jnp.float32
    )
    seq_weight = -adv * seq_ratio * active / length
    token_coef = jnp.reshape(seq_weight, (1,)).astype(jnp.float32)
    d = out_grad.shape[1]
    col = d // (n_z * n_core)
    core = lax.axis_index("core").astype(jnp.int32)

    def col_index(k, which):
        return jnp.reshape(k * n_core + which, (1,)).astype(jnp.int32)

    swap = [(0, 1), (1, 0)]

    def pre_reduced(lo, hi, z_major, per_call):
        got = []
        for k in range(0, n_z, per_call):
            theirs = block_matmul(col_index(k, 1 - core), token_coef, out_grad, hid_t, n_dp, col,
                                  lo, hi, per_call)
            got.append(lax.ppermute(theirs, "core", perm=swap))
        chip = None
        for j, k in enumerate(range(0, n_z, per_call)):
            chip = block_matmul(col_index(k, core), token_coef, out_grad, hid_t, n_dp, col, lo, hi,
                                per_call, addend=got[j], into=chip, slot=k, n_slots=n_z,
                                z_major=z_major)
        return chip

    keep = col - Z_FIRST
    dp_first = pre_reduced(0, keep, False, 2)
    rows = lax.psum_scatter(dp_first, "dp", scatter_dimension=0, tiled=True)[0]
    z_first = pre_reduced(keep, col, True, n_z)
    late = z_reduce_scatter(z_first, "z", n_z, 0)
    late = z_reduce_scatter(late, "dp", n_dp, 2)
    early = z_reduce_scatter(rows, "z", n_z, 3)
    return jnp.concatenate([early, late], axis=1)


def solution(mesh):
    n_dp, n_ctx = mesh.shape["dp"], mesh.shape["ctx"]
    fine = Mesh(np.asarray(mesh.devices).reshape(n_dp, n_ctx // 2, 2), ("dp", "z", "core"))
    tok = ("dp", "z", "core")
    placed = (
        P(tok, None),
        P(tok, None),
        P("dp", ("z", "core")),
        P("dp", ("z", "core")),
        P("dp"),
        P("dp", ("z", "core")),
        P("dp", None),
    )
    return jax.shard_map(
        shards, mesh=fine, in_specs=placed, out_specs=P("dp", ("z", "core")), check_vma=False
    )
```

```python
import jax
import jax.numpy as jnp
import numpy as np
from jax import lax
from jax.experimental import pallas as pl
from jax.experimental.pallas import tpu as pltpu
from jax.sharding import Mesh
from jax.sharding import PartitionSpec as P

CLIP_LOW = 0.0003
CLIP_HIGH = 0.0004
ROW_TILE = 1536
Z_FIRST = 128


def block_matmul(col, coef, grad, hid_t, n_dp, width, lo, hi, n_blocks, addend=None, into=None,
                 slot=0, n_slots=1, z_major=False):
    hb, t = hid_t.shape
    rows = hb // n_dp
    per_tile = ROW_TILE // rows
    n_tiles = hb // ROW_TILE
    w = hi - lo

    def kernel(col_ref, w_ref, grad_ref, hid_ref, *rest):
        rest = list(rest)
        add_ref = rest.pop(0) if addend is not None else None
        if into is not None:
            rest.pop(0)
        out_ref, scaled_ref = rest

        @pl.when(pl.program_id(1) == 0)
        def _():
            scaled_ref[...] = (w_ref[0] * grad_ref[:, lo:hi].astype(jnp.float32)).astype(
                jnp.bfloat16)

        acc = jnp.dot(hid_ref[...], scaled_ref[...], preferred_element_type=jnp.float32)
        for k in range(per_tile):
            part = acc[k * rows:(k + 1) * rows, :]
            if add_ref is None:
                out_ref[0, k] = part
                continue
            part = part + add_ref[0, k]
            if z_major:
                out_ref[0, k] = part
            else:
                out_ref[k, 0] = part

    in_specs = [
        pl.BlockSpec(memory_space=pltpu.SMEM),
        pl.BlockSpec((t, width), lambda b, i, c: (0, c[0] + 2 * b)),
        pl.BlockSpec((ROW_TILE, t), lambda b, i, c: (i, 0)),
    ]
    args = [col, coef, grad, hid_t]
    if addend is not None:
        in_specs.append(pl.BlockSpec((1, per_tile, rows, w), lambda b, i, c: (b, i, 0, 0)))
        args.append(addend)
    aliases = {}
    if into is not None:
        in_specs.append(pl.BlockSpec(memory_space=pl.ANY))
        aliases = {len(args): 0}
        args.append(into)
    if addend is None:
        out_shape = jax.ShapeDtypeStruct((n_blocks, n_dp, rows, w), jnp.float32)
        out_spec = pl.BlockSpec((1, per_tile, rows, w), lambda b, i, c: (b, i, 0, 0))
    elif z_major:
        out_shape = jax.ShapeDtypeStruct((n_slots, n_dp, rows, w), jnp.float32)
        out_spec = pl.BlockSpec((1, per_tile, rows, w), lambda b, i, c: (slot + b, i, 0, 0))
    else:
        out_shape = jax.ShapeDtypeStruct((n_dp, n_slots, rows, w), jnp.float32)
        out_spec = pl.BlockSpec((per_tile, 1, rows, w), lambda b, i, c: (i, slot + b, 0, 0))
    grid_spec = pltpu.PrefetchScalarGridSpec(
        num_scalar_prefetch=1,
        grid=(n_blocks, n_tiles),
        in_specs=in_specs,
        out_specs=out_spec,
        scratch_shapes=[pltpu.VMEM((t, w), jnp.bfloat16)],
    )
    extra = hb * w * 4 * n_blocks if addend is not None else 0
    return pl.pallas_call(
        kernel,
        grid_spec=grid_spec,
        out_shape=out_shape,
        input_output_aliases=aliases,
        compiler_params=pltpu.CompilerParams(vmem_limit_bytes=48 * 1024 * 1024),
        cost_estimate=pl.CostEstimate(
            flops=2 * hb * t * w * n_blocks, transcendentals=0,
            bytes_accessed=hb * t * 2 + (t * width * 2 + hb * w * 4) * n_blocks + extra,
        ),
    )(*args)


def z_reduce_scatter(x, axis, n, cid):
    rest_shape = x.shape[1:]
    size = 1
    for s in x.shape:
        size *= s

    def kernel(x_ref, out_ref, recv, send_sem, recv_sem):
        me = lax.axis_index(axis)
        barrier = pltpu.get_barrier_semaphore()
        for d in range(1, n):
            peer = lax.rem(me + d, n)
            pl.semaphore_signal(barrier, inc=1, device_id={axis: peer},
                                device_id_type=pl.DeviceIdType.MESH)
        pl.semaphore_wait(barrier, n - 1)
        copies = []
        for d in range(1, n):
            peer = lax.rem(me + d, n)
            cp = pltpu.make_async_remote_copy(
                src_ref=x_ref.at[peer], dst_ref=recv.at[me],
                send_sem=send_sem.at[d], recv_sem=recv_sem.at[me],
                device_id={axis: peer}, device_id_type=pl.DeviceIdType.MESH)
            cp.start()
            copies.append(cp)
        total = x_ref[me]
        for d in range(1, n):
            src = lax.rem(me + n - d, n)
            incoming = pltpu.make_async_remote_copy(
                src_ref=x_ref.at[src], dst_ref=recv.at[src],
                send_sem=send_sem.at[d], recv_sem=recv_sem.at[src],
                device_id={axis: src}, device_id_type=pl.DeviceIdType.MESH)
            incoming.wait_recv()
            total = total + recv[src]
        for cp in copies:
            cp.wait_send()
        out_ref[...] = total

    return pl.pallas_call(
        kernel,
        out_shape=jax.ShapeDtypeStruct(rest_shape, jnp.float32),
        in_specs=[pl.BlockSpec(memory_space=pltpu.VMEM)],
        out_specs=pl.BlockSpec(memory_space=pltpu.VMEM),
        scratch_shapes=[
            pltpu.VMEM(x.shape, jnp.float32),
            pltpu.SemaphoreType.DMA((n,)),
            pltpu.SemaphoreType.DMA((n,)),
        ],
        compiler_params=pltpu.CompilerParams(
            collective_id=cid, has_side_effects=True, vmem_limit_bytes=40 * 1024 * 1024),
        cost_estimate=pl.CostEstimate(flops=size, transcendentals=0, bytes_accessed=3 * size * 4),
    )(x)

def ctx_sum(new_lp, old_lp, mask, roll_len, hidden, n_z, n_core):
    n = n_z * n_core
    t, hb = hidden.shape

    def kernel(new_ref, old_ref, mask_ref, len_ref, hid_hbm, out_ref, live_ref, ht_ref,
               hid_ref, mine, staged, recv, hid_sem, copy_sem, send_sem, recv_sem):
        me = lax.axis_index("z") * n_core + lax.axis_index("core")
        fetch = pltpu.make_async_copy(hid_hbm, hid_ref, hid_sem)
        fetch.start()

        def peer_of(p):
            return {"z": p // n_core, "core": p % n_core}

        barrier = pltpu.get_barrier_semaphore()
        for d in range(1, n):
            pl.semaphore_signal(barrier, inc=1, device_id=peer_of(lax.rem(me + d, n)),
                                device_id_type=pl.DeviceIdType.MESH)
        places = me * t + lax.broadcasted_iota(jnp.int32, (8, t), 1)
        mask8 = jnp.broadcast_to(mask_ref[...], (8, t))
        live = jnp.where(places < len_ref[0], mask8, 0).astype(jnp.float32)
        gap = jnp.sum((new_ref[...] - old_ref[...]) * live[0:1, :])
        count = jnp.sum(live[0:1, :])
        lanes = lax.broadcasted_iota(jnp.int32, (8, 128), 1)
        mine[...] = jnp.where(lanes == 0, gap, jnp.where(lanes == 1, count, 0.0))
        local = pltpu.make_async_copy(mine, staged, copy_sem)
        local.start()
        live_col = live.T[:, 0:1]
        live_ref[...] = live_col
        live_hid = live_col.astype(hid_ref.dtype)

        fetch.wait()
        chunks = hb // 128

        def transpose(first, last):
            @pl.loop(first, last)
            def _(j):
                cols = pl.ds(pl.multiple_of(j * 128, 128), 128)
                ht_ref[cols, :] = (hid_ref[:, cols] * live_hid).T

        transpose(0, chunks // 2)
        local.wait()
        pl.semaphore_wait(barrier, n - 1)
        copies = []
        for d in range(1, n):
            cp = pltpu.make_async_remote_copy(
                src_ref=staged, dst_ref=recv.at[me],
                send_sem=send_sem.at[d], recv_sem=recv_sem.at[me],
                device_id=peer_of(lax.rem(me + d, n)), device_id_type=pl.DeviceIdType.MESH)
            cp.start()
            copies.append(cp)
        recv[me] = staged[...]
        transpose(chunks // 2, chunks)
        for d in range(1, n):
            src = lax.rem(me + n - d, n)
            pltpu.make_async_remote_copy(
                src_ref=staged, dst_ref=recv.at[src],
                send_sem=send_sem.at[d], recv_sem=recv_sem.at[src],
                device_id=peer_of(src), device_id_type=pl.DeviceIdType.MESH).wait_recv()
        total = recv[0]
        for p in range(1, n):
            total = total + recv[p]
        for cp in copies:
            cp.wait_send()
        out_ref[...] = total

    vmem = pl.BlockSpec(memory_space=pltpu.VMEM)
    return pl.pallas_call(
        kernel,
        out_shape=(jax.ShapeDtypeStruct((8, 128), jnp.float32),
                   jax.ShapeDtypeStruct((t, 1), jnp.float32),
                   jax.ShapeDtypeStruct((hb, t), hidden.dtype)),
        in_specs=[vmem, vmem, vmem, pl.BlockSpec(memory_space=pltpu.SMEM),
                  pl.BlockSpec(memory_space=pl.ANY)],
        out_specs=(vmem, vmem, vmem),
        scratch_shapes=[
            pltpu.VMEM((t, hb), hidden.dtype),
            pltpu.VMEM((8, 128), jnp.float32),
            pltpu.VMEM((8, 128), jnp.float32),
            pltpu.VMEM((n, 8, 128), jnp.float32),
            pltpu.SemaphoreType.DMA,
            pltpu.SemaphoreType.DMA,
            pltpu.SemaphoreType.DMA((n,)),
            pltpu.SemaphoreType.DMA((n,)),
        ],
        compiler_params=pltpu.CompilerParams(
            collective_id=1, has_side_effects=True, vmem_limit_bytes=32 * 1024 * 1024),
    )(new_lp, old_lp, mask, roll_len, hidden)


def shards(hidden_acts, out_grad, old_logp, new_logp, roll_len, resp_mask, advantage):
    n_dp = lax.axis_size("dp")
    n_z = lax.axis_size("z")
    n_core = lax.axis_size("core")
    width = old_logp.shape[1]
    ctx = lax.axis_index("z") * n_core + lax.axis_index("core")
    summed, live_col, hid_t = ctx_sum(new_logp, old_logp, resp_mask, roll_len, hidden_acts,
                                      n_z, n_core)
    gap_sum, count = summed[0, 0], summed[0, 1]
    adv = advantage[0, 0]
    length = jnp.maximum(count, 1.0)
    seq_ratio = jnp.exp(gap_sum / length)
    active = jnp.where(adv >= 0.0, seq_ratio < 1.0 + CLIP_HIGH, seq_ratio > 1.0 - CLIP_LOW).astype(
        jnp.float32
    )
    seq_weight = -adv * seq_ratio * active / length
    token_coef = jnp.reshape(seq_weight, (1,)).astype(jnp.float32)
    d = out_grad.shape[1]
    col = d // (n_z * n_core)
    core = lax.axis_index("core").astype(jnp.int32)

    def col_index(k, which):
        return jnp.reshape(k * n_core + which, (1,)).astype(jnp.int32)

    swap = [(0, 1), (1, 0)]

    def pre_reduced(lo, hi, z_major, per_call):
        got = []
        for k in range(0, n_z, per_call):
            theirs = block_matmul(col_index(k, 1 - core), token_coef, out_grad, hid_t, n_dp, col,
                                  lo, hi, per_call)
            got.append(lax.ppermute(theirs, "core", perm=swap))
        chip = None
        for j, k in enumerate(range(0, n_z, per_call)):
            chip = block_matmul(col_index(k, core), token_coef, out_grad, hid_t, n_dp, col, lo, hi,
                                per_call, addend=got[j], into=chip, slot=k, n_slots=n_z,
                                z_major=z_major)
        return chip

    keep = col - Z_FIRST
    dp_first = pre_reduced(0, keep, False, 2)
    rows = lax.psum_scatter(dp_first, "dp", scatter_dimension=0, tiled=True)[0]
    z_first = pre_reduced(keep, col, True, n_z)
    late = z_reduce_scatter(z_first, "z", n_z, 0)
    late = z_reduce_scatter(late, "dp", n_dp, 2)
    early = z_reduce_scatter(rows, "z", n_z, 3)
    return jnp.concatenate([early, late], axis=1)


def solution(mesh):
    n_dp, n_ctx = mesh.shape["dp"], mesh.shape["ctx"]
    fine = Mesh(np.asarray(mesh.devices).reshape(n_dp, n_ctx // 2, 2), ("dp", "z", "core"))
    tok = ("dp", "z", "core")
    placed = (
        P(tok, None),
        P(tok, None),
        P("dp", ("z", "core")),
        P("dp", ("z", "core")),
        P("dp"),
        P("dp", ("z", "core")),
        P("dp", None),
    )
    return jax.shard_map(
        shards, mesh=fine, in_specs=placed, out_specs=P("dp", ("z", "core")), check_vma=False
    )
```

```python
import jax
import jax.numpy as jnp
import numpy as np
from jax import lax
from jax.experimental import pallas as pl
from jax.experimental.pallas import tpu as pltpu
from jax.sharding import Mesh
from jax.sharding import PartitionSpec as P

CLIP_LOW = 0.0003
CLIP_HIGH = 0.0004
ROW_TILE = 1536
Z_FIRST = 128


def block_matmul(col, coef, grad, hid_t, n_dp, width, lo, hi, n_blocks, addend=None, into=None,
                 slot=0, n_slots=1, z_major=False):
    hb, t = hid_t.shape
    rows = hb // n_dp
    per_tile = ROW_TILE // rows
    n_tiles = hb // ROW_TILE
    w = hi - lo

    def kernel(col_ref, w_ref, grad_ref, hid_ref, *rest):
        rest = list(rest)
        add_ref = rest.pop(0) if addend is not None else None
        if into is not None:
            rest.pop(0)
        out_ref, scaled_ref = rest

        @pl.when(pl.program_id(1) == 0)
        def _():
            scaled_ref[...] = (w_ref[0] * grad_ref[:, lo:hi].astype(jnp.float32)).astype(
                jnp.bfloat16)

        acc = jnp.dot(hid_ref[...], scaled_ref[...], preferred_element_type=jnp.float32)
        for k in range(per_tile):
            part = acc[k * rows:(k + 1) * rows, :]
            if add_ref is None:
                out_ref[0, k] = part
                continue
            part = part + add_ref[0, k]
            if z_major:
                out_ref[0, k] = part
            else:
                out_ref[k, 0] = part

    in_specs = [
        pl.BlockSpec(memory_space=pltpu.SMEM),
        pl.BlockSpec((t, width), lambda b, i, c: (0, c[0] + 2 * b)),
        pl.BlockSpec((ROW_TILE, t), lambda b, i, c: (i, 0)),
    ]
    args = [col, coef, grad, hid_t]
    if addend is not None:
        in_specs.append(pl.BlockSpec((1, per_tile, rows, w), lambda b, i, c: (b, i, 0, 0)))
        args.append(addend)
    aliases = {}
    if into is not None:
        in_specs.append(pl.BlockSpec(memory_space=pl.ANY))
        aliases = {len(args): 0}
        args.append(into)
    if addend is None:
        out_shape = jax.ShapeDtypeStruct((n_blocks, n_dp, rows, w), jnp.float32)
        out_spec = pl.BlockSpec((1, per_tile, rows, w), lambda b, i, c: (b, i, 0, 0))
    elif z_major:
        out_shape = jax.ShapeDtypeStruct((n_slots, n_dp, rows, w), jnp.float32)
        out_spec = pl.BlockSpec((1, per_tile, rows, w), lambda b, i, c: (slot + b, i, 0, 0))
    else:
        out_shape = jax.ShapeDtypeStruct((n_dp, n_slots, rows, w), jnp.float32)
        out_spec = pl.BlockSpec((per_tile, 1, rows, w), lambda b, i, c: (i, slot + b, 0, 0))
    grid_spec = pltpu.PrefetchScalarGridSpec(
        num_scalar_prefetch=1,
        grid=(n_blocks, n_tiles),
        in_specs=in_specs,
        out_specs=out_spec,
        scratch_shapes=[pltpu.VMEM((t, w), jnp.bfloat16)],
    )
    extra = hb * w * 4 * n_blocks if addend is not None else 0
    return pl.pallas_call(
        kernel,
        grid_spec=grid_spec,
        out_shape=out_shape,
        input_output_aliases=aliases,
        compiler_params=pltpu.CompilerParams(vmem_limit_bytes=48 * 1024 * 1024),
        cost_estimate=pl.CostEstimate(
            flops=2 * hb * t * w * n_blocks, transcendentals=0,
            bytes_accessed=hb * t * 2 + (t * width * 2 + hb * w * 4) * n_blocks + extra,
        ),
    )(*args)


def z_reduce_scatter(x, axis, n, cid):
    rest_shape = x.shape[1:]
    size = 1
    for s in x.shape:
        size *= s

    def kernel(x_ref, out_ref, recv, send_sem, recv_sem):
        me = lax.axis_index(axis)
        barrier = pltpu.get_barrier_semaphore()
        for d in range(1, n):
            peer = lax.rem(me + d, n)
            pl.semaphore_signal(barrier, inc=1, device_id={axis: peer},
                                device_id_type=pl.DeviceIdType.MESH)
        pl.semaphore_wait(barrier, n - 1)
        copies = []
        for d in range(1, n):
            peer = lax.rem(me + d, n)
            cp = pltpu.make_async_remote_copy(
                src_ref=x_ref.at[peer], dst_ref=recv.at[me],
                send_sem=send_sem.at[d], recv_sem=recv_sem.at[me],
                device_id={axis: peer}, device_id_type=pl.DeviceIdType.MESH)
            cp.start()
            copies.append(cp)
        total = x_ref[me]
        for d in range(1, n):
            src = lax.rem(me + n - d, n)
            incoming = pltpu.make_async_remote_copy(
                src_ref=x_ref.at[src], dst_ref=recv.at[src],
                send_sem=send_sem.at[d], recv_sem=recv_sem.at[src],
                device_id={axis: src}, device_id_type=pl.DeviceIdType.MESH)
            incoming.wait_recv()
            total = total + recv[src]
        for cp in copies:
            cp.wait_send()
        out_ref[...] = total

    return pl.pallas_call(
        kernel,
        out_shape=jax.ShapeDtypeStruct(rest_shape, jnp.float32),
        in_specs=[pl.BlockSpec(memory_space=pltpu.VMEM)],
        out_specs=pl.BlockSpec(memory_space=pltpu.VMEM),
        scratch_shapes=[
            pltpu.VMEM(x.shape, jnp.float32),
            pltpu.SemaphoreType.DMA((n,)),
            pltpu.SemaphoreType.DMA((n,)),
        ],
        compiler_params=pltpu.CompilerParams(
            collective_id=cid, has_side_effects=True, vmem_limit_bytes=40 * 1024 * 1024),
        cost_estimate=pl.CostEstimate(flops=size, transcendentals=0, bytes_accessed=3 * size * 4),
    )(x)

def ctx_sum(new_lp, old_lp, mask, roll_len, hidden, n_z, n_core):
    n = n_z * n_core
    t, hb = hidden.shape

    def kernel(new_hbm, old_hbm, mask_hbm, len_ref, hid_hbm, out_ref, live_ref, ht_ref,
               hid_ref, new_ref, old_ref, mask_ref, mine, staged, recv, hid_sem, row_sem,
               copy_sem, send_sem, recv_sem):
        me = lax.axis_index("z") * n_core + lax.axis_index("core")
        rows = [pltpu.make_async_copy(a, b, row_sem.at[i]) for i, (a, b) in enumerate(
            ((new_hbm, new_ref), (old_hbm, old_ref), (mask_hbm, mask_ref)))]
        for cp in rows:
            cp.start()
        fetch = pltpu.make_async_copy(hid_hbm, hid_ref, hid_sem)
        fetch.start()

        def peer_of(p):
            return {"z": p // n_core, "core": p % n_core}

        barrier = pltpu.get_barrier_semaphore()
        for d in range(1, n):
            pl.semaphore_signal(barrier, inc=1, device_id=peer_of(lax.rem(me + d, n)),
                                device_id_type=pl.DeviceIdType.MESH)
        for cp in rows:
            cp.wait()
        places = me * t + lax.broadcasted_iota(jnp.int32, (8, t), 1)
        mask8 = jnp.broadcast_to(mask_ref[...], (8, t))
        live = jnp.where(places < len_ref[0], mask8, 0).astype(jnp.float32)
        gap = jnp.sum((new_ref[...] - old_ref[...]) * live[0:1, :])
        count = jnp.sum(live[0:1, :])
        lanes = lax.broadcasted_iota(jnp.int32, (8, 128), 1)
        mine[...] = jnp.where(lanes == 0, gap, jnp.where(lanes == 1, count, 0.0))
        local = pltpu.make_async_copy(mine, staged, copy_sem)
        local.start()
        live_col = live.T[:, 0:1]
        live_ref[...] = live_col
        live_hid = live_col.astype(hid_ref.dtype)

        fetch.wait()
        chunks = hb // 128

        def transpose(first, last):
            @pl.loop(first, last)
            def _(j):
                cols = pl.ds(pl.multiple_of(j * 128, 128), 128)
                ht_ref[cols, :] = (hid_ref[:, cols] * live_hid).T

        transpose(0, chunks // 2)
        local.wait()
        pl.semaphore_wait(barrier, n - 1)
        copies = []
        for d in range(1, n):
            cp = pltpu.make_async_remote_copy(
                src_ref=staged, dst_ref=recv.at[me],
                send_sem=send_sem.at[d], recv_sem=recv_sem.at[me],
                device_id=peer_of(lax.rem(me + d, n)), device_id_type=pl.DeviceIdType.MESH)
            cp.start()
            copies.append(cp)
        recv[me] = staged[...]
        transpose(chunks // 2, chunks)
        for d in range(1, n):
            src = lax.rem(me + n - d, n)
            pltpu.make_async_remote_copy(
                src_ref=staged, dst_ref=recv.at[src],
                send_sem=send_sem.at[d], recv_sem=recv_sem.at[src],
                device_id=peer_of(src), device_id_type=pl.DeviceIdType.MESH).wait_recv()
        total = recv[0]
        for p in range(1, n):
            total = total + recv[p]
        for cp in copies:
            cp.wait_send()
        out_ref[...] = total

    vmem = pl.BlockSpec(memory_space=pltpu.VMEM)
    return pl.pallas_call(
        kernel,
        out_shape=(jax.ShapeDtypeStruct((8, 128), jnp.float32),
                   jax.ShapeDtypeStruct((t, 1), jnp.float32),
                   jax.ShapeDtypeStruct((hb, t), hidden.dtype)),
        in_specs=[pl.BlockSpec(memory_space=pl.ANY)] * 3 + [
            pl.BlockSpec(memory_space=pltpu.SMEM), pl.BlockSpec(memory_space=pl.ANY)],
        out_specs=(vmem, vmem, vmem),
        scratch_shapes=[
            pltpu.VMEM((t, hb), hidden.dtype),
            pltpu.VMEM(new_lp.shape, new_lp.dtype),
            pltpu.VMEM(old_lp.shape, old_lp.dtype),
            pltpu.VMEM(mask.shape, mask.dtype),
            pltpu.VMEM((8, 128), jnp.float32),
            pltpu.VMEM((8, 128), jnp.float32),
            pltpu.VMEM((n, 8, 128), jnp.float32),
            pltpu.SemaphoreType.DMA,
            pltpu.SemaphoreType.DMA((3,)),
            pltpu.SemaphoreType.DMA,
            pltpu.SemaphoreType.DMA((n,)),
            pltpu.SemaphoreType.DMA((n,)),
        ],
        compiler_params=pltpu.CompilerParams(
            collective_id=1, has_side_effects=True, vmem_limit_bytes=64 * 1024 * 1024),
    )(new_lp, old_lp, mask, roll_len, hidden)


def shards(hidden_acts, out_grad, old_logp, new_logp, roll_len, resp_mask, advantage):
    n_dp = lax.axis_size("dp")
    n_z = lax.axis_size("z")
    n_core = lax.axis_size("core")
    width = old_logp.shape[1]
    ctx = lax.axis_index("z") * n_core + lax.axis_index("core")
    summed, live_col, hid_t = ctx_sum(new_logp, old_logp, resp_mask, roll_len, hidden_acts,
                                      n_z, n_core)
    gap_sum, count = summed[0, 0], summed[0, 1]
    adv = advantage[0, 0]
    length = jnp.maximum(count, 1.0)
    seq_ratio = jnp.exp(gap_sum / length)
    active = jnp.where(adv >= 0.0, seq_ratio < 1.0 + CLIP_HIGH, seq_ratio > 1.0 - CLIP_LOW).astype(
        jnp.float32
    )
    seq_weight = -adv * seq_ratio * active / length
    token_coef = jnp.reshape(seq_weight, (1,)).astype(jnp.float32)
    d = out_grad.shape[1]
    col = d // (n_z * n_core)
    core = lax.axis_index("core").astype(jnp.int32)

    def col_index(k, which):
        return jnp.reshape(k * n_core + which, (1,)).astype(jnp.int32)

    swap = [(0, 1), (1, 0)]

    def pre_reduced(lo, hi, z_major, per_call):
        got = []
        for k in range(0, n_z, per_call):
            theirs = block_matmul(col_index(k, 1 - core), token_coef, out_grad, hid_t, n_dp, col,
                                  lo, hi, per_call)
            got.append(lax.ppermute(theirs, "core", perm=swap))
        chip = None
        for j, k in enumerate(range(0, n_z, per_call)):
            chip = block_matmul(col_index(k, core), token_coef, out_grad, hid_t, n_dp, col, lo, hi,
                                per_call, addend=got[j], into=chip, slot=k, n_slots=n_z,
                                z_major=z_major)
        return chip

    keep = col - Z_FIRST
    dp_first = pre_reduced(0, keep, False, 2)
    rows = lax.psum_scatter(dp_first, "dp", scatter_dimension=0, tiled=True)[0]
    z_first = pre_reduced(keep, col, True, n_z)
    late = z_reduce_scatter(z_first, "z", n_z, 0)
    late = z_reduce_scatter(late, "dp", n_dp, 2)
    early = z_reduce_scatter(rows, "z", n_z, 3)
    return jnp.concatenate([early, late], axis=1)


def solution(mesh):
    n_dp, n_ctx = mesh.shape["dp"], mesh.shape["ctx"]
    fine = Mesh(np.asarray(mesh.devices).reshape(n_dp, n_ctx // 2, 2), ("dp", "z", "core"))
    tok = ("dp", "z", "core")
    placed = (
        P(tok, None),
        P(tok, None),
        P("dp", ("z", "core")),
        P("dp", ("z", "core")),
        P("dp"),
        P("dp", ("z", "core")),
        P("dp", None),
    )
    return jax.shard_map(
        shards, mesh=fine, in_specs=placed, out_specs=P("dp", ("z", "core")), check_vma=False
    )
```

```python
import jax
import jax.numpy as jnp
import numpy as np
from jax import lax
from jax.experimental import pallas as pl
from jax.experimental.pallas import tpu as pltpu
from jax.sharding import Mesh
from jax.sharding import PartitionSpec as P

CLIP_LOW = 0.0003
CLIP_HIGH = 0.0004
ROW_TILE = 1536
Z_FIRST = 128


def block_matmul(col, coef, grad, hid_t, n_dp, width, lo, hi, n_blocks, addend=None, into=None,
                 slot=0, n_slots=1, z_major=False):
    hb, t = hid_t.shape
    rows = hb // n_dp
    per_tile = ROW_TILE // rows
    n_tiles = hb // ROW_TILE
    w = hi - lo

    def kernel(col_ref, w_ref, grad_ref, hid_ref, *rest):
        rest = list(rest)
        add_ref = rest.pop(0) if addend is not None else None
        if into is not None:
            rest.pop(0)
        out_ref, scaled_ref = rest

        @pl.when(pl.program_id(1) == 0)
        def _():
            scaled_ref[...] = (w_ref[0] * grad_ref[:, lo:hi].astype(jnp.float32)).astype(
                jnp.bfloat16)

        acc = jnp.dot(hid_ref[...], scaled_ref[...], preferred_element_type=jnp.float32)
        for k in range(per_tile):
            part = acc[k * rows:(k + 1) * rows, :]
            if add_ref is None:
                out_ref[0, k] = part
                continue
            part = part + add_ref[0, k]
            if z_major:
                out_ref[0, k] = part
            else:
                out_ref[k, 0] = part

    in_specs = [
        pl.BlockSpec(memory_space=pltpu.SMEM),
        pl.BlockSpec((t, width), lambda b, i, c: (0, c[0] + 2 * b)),
        pl.BlockSpec((ROW_TILE, t), lambda b, i, c: (i, 0)),
    ]
    args = [col, coef, grad, hid_t]
    if addend is not None:
        in_specs.append(pl.BlockSpec((1, per_tile, rows, w), lambda b, i, c: (b, i, 0, 0)))
        args.append(addend)
    aliases = {}
    if into is not None:
        in_specs.append(pl.BlockSpec(memory_space=pl.ANY))
        aliases = {len(args): 0}
        args.append(into)
    if addend is None:
        out_shape = jax.ShapeDtypeStruct((n_blocks, n_dp, rows, w), jnp.float32)
        out_spec = pl.BlockSpec((1, per_tile, rows, w), lambda b, i, c: (b, i, 0, 0))
    elif z_major:
        out_shape = jax.ShapeDtypeStruct((n_slots, n_dp, rows, w), jnp.float32)
        out_spec = pl.BlockSpec((1, per_tile, rows, w), lambda b, i, c: (slot + b, i, 0, 0))
    else:
        out_shape = jax.ShapeDtypeStruct((n_dp, n_slots, rows, w), jnp.float32)
        out_spec = pl.BlockSpec((per_tile, 1, rows, w), lambda b, i, c: (i, slot + b, 0, 0))
    grid_spec = pltpu.PrefetchScalarGridSpec(
        num_scalar_prefetch=1,
        grid=(n_blocks, n_tiles),
        in_specs=in_specs,
        out_specs=out_spec,
        scratch_shapes=[pltpu.VMEM((t, w), jnp.bfloat16)],
    )
    extra = hb * w * 4 * n_blocks if addend is not None else 0
    return pl.pallas_call(
        kernel,
        grid_spec=grid_spec,
        out_shape=out_shape,
        input_output_aliases=aliases,
        compiler_params=pltpu.CompilerParams(vmem_limit_bytes=48 * 1024 * 1024),
        cost_estimate=pl.CostEstimate(
            flops=2 * hb * t * w * n_blocks, transcendentals=0,
            bytes_accessed=hb * t * 2 + (t * width * 2 + hb * w * 4) * n_blocks + extra,
        ),
    )(*args)


def z_reduce_scatter(x, axis, n, cid, in_place=False):
    rest_shape = x.shape[1:]
    size = 1
    for s in x.shape:
        size *= s

    def kernel(x_ref, out_ref, recv, own, own_sem, send_sem, recv_sem):
        me = lax.axis_index(axis)
        if in_place:
            fetch = pltpu.make_async_copy(x_ref.at[me], own, own_sem)
            fetch.start()
        barrier = pltpu.get_barrier_semaphore()
        for d in range(1, n):
            peer = lax.rem(me + d, n)
            pl.semaphore_signal(barrier, inc=1, device_id={axis: peer},
                                device_id_type=pl.DeviceIdType.MESH)
        pl.semaphore_wait(barrier, n - 1)
        copies = []
        for d in range(1, n):
            peer = lax.rem(me + d, n)
            cp = pltpu.make_async_remote_copy(
                src_ref=x_ref.at[peer], dst_ref=recv.at[me],
                send_sem=send_sem.at[d], recv_sem=recv_sem.at[me],
                device_id={axis: peer}, device_id_type=pl.DeviceIdType.MESH)
            cp.start()
            copies.append(cp)
        if in_place:
            fetch.wait()
            total = own[...]
        else:
            total = x_ref[me]
        for d in range(1, n):
            src = lax.rem(me + n - d, n)
            incoming = pltpu.make_async_remote_copy(
                src_ref=x_ref.at[src], dst_ref=recv.at[src],
                send_sem=send_sem.at[d], recv_sem=recv_sem.at[src],
                device_id={axis: src}, device_id_type=pl.DeviceIdType.MESH)
            incoming.wait_recv()
            total = total + recv[src]
        for cp in copies:
            cp.wait_send()
        out_ref[...] = total

    return pl.pallas_call(
        kernel,
        out_shape=jax.ShapeDtypeStruct(rest_shape, jnp.float32),
        in_specs=[pl.BlockSpec(memory_space=pl.ANY if in_place else pltpu.VMEM)],
        out_specs=pl.BlockSpec(memory_space=pltpu.VMEM),
        scratch_shapes=[
            pltpu.VMEM(x.shape, jnp.float32),
            pltpu.VMEM(rest_shape, jnp.float32),
            pltpu.SemaphoreType.DMA,
            pltpu.SemaphoreType.DMA((n,)),
            pltpu.SemaphoreType.DMA((n,)),
        ],
        compiler_params=pltpu.CompilerParams(
            collective_id=cid, has_side_effects=True,
            vmem_limit_bytes=(64 if in_place else 40) * 1024 * 1024),
        cost_estimate=pl.CostEstimate(flops=size, transcendentals=0, bytes_accessed=3 * size * 4),
    )(x)

def ctx_sum(new_lp, old_lp, mask, roll_len, hidden, n_z, n_core):
    n = n_z * n_core
    t, hb = hidden.shape

    def kernel(new_ref, old_ref, mask_ref, len_ref, hid_hbm, out_ref, live_ref, ht_ref,
               hid_ref, mine, staged, recv, hid_sem, copy_sem, send_sem, recv_sem):
        me = lax.axis_index("z") * n_core + lax.axis_index("core")
        fetch = pltpu.make_async_copy(hid_hbm, hid_ref, hid_sem)
        fetch.start()

        def peer_of(p):
            return {"z": p // n_core, "core": p % n_core}

        barrier = pltpu.get_barrier_semaphore()
        for d in range(1, n):
            pl.semaphore_signal(barrier, inc=1, device_id=peer_of(lax.rem(me + d, n)),
                                device_id_type=pl.DeviceIdType.MESH)
        places = me * t + lax.broadcasted_iota(jnp.int32, (8, t), 1)
        mask8 = jnp.broadcast_to(mask_ref[...], (8, t))
        live = jnp.where(places < len_ref[0], mask8, 0).astype(jnp.float32)
        gap = jnp.sum((new_ref[...] - old_ref[...]) * live[0:1, :])
        count = jnp.sum(live[0:1, :])
        lanes = lax.broadcasted_iota(jnp.int32, (8, 128), 1)
        mine[...] = jnp.where(lanes == 0, gap, jnp.where(lanes == 1, count, 0.0))
        local = pltpu.make_async_copy(mine, staged, copy_sem)
        local.start()
        live_col = live.T[:, 0:1]
        live_ref[...] = live_col
        live_hid = live_col.astype(hid_ref.dtype)

        fetch.wait()
        chunks = hb // 128

        def transpose(first, last):
            @pl.loop(first, last)
            def _(j):
                cols = pl.ds(pl.multiple_of(j * 128, 128), 128)
                ht_ref[cols, :] = (hid_ref[:, cols] * live_hid).T

        transpose(0, chunks // 2)
        local.wait()
        pl.semaphore_wait(barrier, n - 1)
        copies = []
        for d in range(1, n):
            cp = pltpu.make_async_remote_copy(
                src_ref=staged, dst_ref=recv.at[me],
                send_sem=send_sem.at[d], recv_sem=recv_sem.at[me],
                device_id=peer_of(lax.rem(me + d, n)), device_id_type=pl.DeviceIdType.MESH)
            cp.start()
            copies.append(cp)
        recv[me] = staged[...]
        transpose(chunks // 2, chunks)
        for d in range(1, n):
            src = lax.rem(me + n - d, n)
            pltpu.make_async_remote_copy(
                src_ref=staged, dst_ref=recv.at[src],
                send_sem=send_sem.at[d], recv_sem=recv_sem.at[src],
                device_id=peer_of(src), device_id_type=pl.DeviceIdType.MESH).wait_recv()
        total = recv[0]
        for p in range(1, n):
            total = total + recv[p]
        for cp in copies:
            cp.wait_send()
        out_ref[...] = total

    vmem = pl.BlockSpec(memory_space=pltpu.VMEM)
    return pl.pallas_call(
        kernel,
        out_shape=(jax.ShapeDtypeStruct((8, 128), jnp.float32),
                   jax.ShapeDtypeStruct((t, 1), jnp.float32),
                   jax.ShapeDtypeStruct((hb, t), hidden.dtype)),
        in_specs=[vmem, vmem, vmem, pl.BlockSpec(memory_space=pltpu.SMEM),
                  pl.BlockSpec(memory_space=pl.ANY)],
        out_specs=(vmem, vmem, vmem),
        scratch_shapes=[
            pltpu.VMEM((t, hb), hidden.dtype),
            pltpu.VMEM((8, 128), jnp.float32),
            pltpu.VMEM((8, 128), jnp.float32),
            pltpu.VMEM((n, 8, 128), jnp.float32),
            pltpu.SemaphoreType.DMA,
            pltpu.SemaphoreType.DMA,
            pltpu.SemaphoreType.DMA((n,)),
            pltpu.SemaphoreType.DMA((n,)),
        ],
        compiler_params=pltpu.CompilerParams(
            collective_id=1, has_side_effects=True, vmem_limit_bytes=32 * 1024 * 1024),
    )(new_lp, old_lp, mask, roll_len, hidden)


def shards(hidden_acts, out_grad, old_logp, new_logp, roll_len, resp_mask, advantage):
    n_dp = lax.axis_size("dp")
    n_z = lax.axis_size("z")
    n_core = lax.axis_size("core")
    width = old_logp.shape[1]
    ctx = lax.axis_index("z") * n_core + lax.axis_index("core")
    summed, live_col, hid_t = ctx_sum(new_logp, old_logp, resp_mask, roll_len, hidden_acts,
                                      n_z, n_core)
    gap_sum, count = summed[0, 0], summed[0, 1]
    adv = advantage[0, 0]
    length = jnp.maximum(count, 1.0)
    seq_ratio = jnp.exp(gap_sum / length)
    active = jnp.where(adv >= 0.0, seq_ratio < 1.0 + CLIP_HIGH, seq_ratio > 1.0 - CLIP_LOW).astype(
        jnp.float32
    )
    seq_weight = -adv * seq_ratio * active / length
    token_coef = jnp.reshape(seq_weight, (1,)).astype(jnp.float32)
    d = out_grad.shape[1]
    col = d // (n_z * n_core)
    core = lax.axis_index("core").astype(jnp.int32)

    def col_index(k, which):
        return jnp.reshape(k * n_core + which, (1,)).astype(jnp.int32)

    swap = [(0, 1), (1, 0)]

    def pre_reduced(lo, hi, z_major, per_call):
        got = []
        for k in range(0, n_z, per_call):
            theirs = block_matmul(col_index(k, 1 - core), token_coef, out_grad, hid_t, n_dp, col,
                                  lo, hi, per_call)
            got.append(lax.ppermute(theirs, "core", perm=swap))
        chip = None
        for j, k in enumerate(range(0, n_z, per_call)):
            chip = block_matmul(col_index(k, core), token_coef, out_grad, hid_t, n_dp, col, lo, hi,
                                per_call, addend=got[j], into=chip, slot=k, n_slots=n_z,
                                z_major=z_major)
        return chip

    keep = col - Z_FIRST
    dp_first = pre_reduced(0, keep, False, 2)
    rows = lax.psum_scatter(dp_first, "dp", scatter_dimension=0, tiled=True)[0]
    z_first = pre_reduced(keep, col, True, n_z)
    late = z_reduce_scatter(z_first, "z", n_z, 0)
    late = z_reduce_scatter(late, "dp", n_dp, 2)
    early = z_reduce_scatter(rows, "z", n_z, 3, in_place=True)
    return jnp.concatenate([early, late], axis=1)


def solution(mesh):
    n_dp, n_ctx = mesh.shape["dp"], mesh.shape["ctx"]
    fine = Mesh(np.asarray(mesh.devices).reshape(n_dp, n_ctx // 2, 2), ("dp", "z", "core"))
    tok = ("dp", "z", "core")
    placed = (
        P(tok, None),
        P(tok, None),
        P("dp", ("z", "core")),
        P("dp", ("z", "core")),
        P("dp"),
        P("dp", ("z", "core")),
        P("dp", None),
    )
    return jax.shard_map(
        shards, mesh=fine, in_specs=placed, out_specs=P("dp", ("z", "core")), check_vma=False
    )
```

```python
import jax
import jax.numpy as jnp
import numpy as np
from jax import lax
from jax.experimental import pallas as pl
from jax.experimental.pallas import tpu as pltpu
from jax.sharding import Mesh
from jax.sharding import PartitionSpec as P

CLIP_LOW = 0.0003
CLIP_HIGH = 0.0004
ROW_TILE = 1536
Z_FIRST = 128


def block_matmul(col, coef, grad, hid_t, n_dp, width, lo, hi, n_blocks, addend=None, into=None,
                 slot=0, n_slots=1, z_major=False):
    hb, t = hid_t.shape
    rows = hb // n_dp
    per_tile = ROW_TILE // rows
    n_tiles = hb // ROW_TILE
    w = hi - lo

    def kernel(col_ref, w_ref, grad_ref, hid_ref, *rest):
        rest = list(rest)
        add_ref = rest.pop(0) if addend is not None else None
        if into is not None:
            rest.pop(0)
        out_ref, scaled_ref = rest

        @pl.when(pl.program_id(1) == 0)
        def _():
            scaled_ref[...] = (w_ref[0] * grad_ref[:, lo:hi].astype(jnp.float32)).astype(
                jnp.bfloat16)

        acc = jnp.dot(hid_ref[...], scaled_ref[...], preferred_element_type=jnp.float32)
        for k in range(per_tile):
            part = acc[k * rows:(k + 1) * rows, :]
            if add_ref is None:
                out_ref[0, k] = part
                continue
            part = part + add_ref[0, k]
            if z_major:
                out_ref[0, k] = part
            else:
                out_ref[k, 0] = part

    in_specs = [
        pl.BlockSpec(memory_space=pltpu.SMEM),
        pl.BlockSpec((t, width), lambda b, i, c: (0, c[0] + 2 * b)),
        pl.BlockSpec((ROW_TILE, t), lambda b, i, c: (i, 0)),
    ]
    args = [col, coef, grad, hid_t]
    if addend is not None:
        in_specs.append(pl.BlockSpec((1, per_tile, rows, w), lambda b, i, c: (b, i, 0, 0)))
        args.append(addend)
    aliases = {}
    if into is not None:
        in_specs.append(pl.BlockSpec(memory_space=pl.ANY))
        aliases = {len(args): 0}
        args.append(into)
    if addend is None:
        out_shape = jax.ShapeDtypeStruct((n_blocks, n_dp, rows, w), jnp.float32)
        out_spec = pl.BlockSpec((1, per_tile, rows, w), lambda b, i, c: (b, i, 0, 0))
    elif z_major:
        out_shape = jax.ShapeDtypeStruct((n_slots, n_dp, rows, w), jnp.float32)
        out_spec = pl.BlockSpec((1, per_tile, rows, w), lambda b, i, c: (slot + b, i, 0, 0))
    else:
        out_shape = jax.ShapeDtypeStruct((n_dp, n_slots, rows, w), jnp.float32)
        out_spec = pl.BlockSpec((per_tile, 1, rows, w), lambda b, i, c: (i, slot + b, 0, 0))
    grid_spec = pltpu.PrefetchScalarGridSpec(
        num_scalar_prefetch=1,
        grid=(n_blocks, n_tiles),
        in_specs=in_specs,
        out_specs=out_spec,
        scratch_shapes=[pltpu.VMEM((t, w), jnp.bfloat16)],
    )
    extra = hb * w * 4 * n_blocks if addend is not None else 0
    return pl.pallas_call(
        kernel,
        grid_spec=grid_spec,
        out_shape=out_shape,
        input_output_aliases=aliases,
        compiler_params=pltpu.CompilerParams(vmem_limit_bytes=48 * 1024 * 1024),
        cost_estimate=pl.CostEstimate(
            flops=2 * hb * t * w * n_blocks, transcendentals=0,
            bytes_accessed=hb * t * 2 + (t * width * 2 + hb * w * 4) * n_blocks + extra,
        ),
    )(*args)


def z_reduce_scatter(x, axis, n, cid, in_place=False):
    rest_shape = x.shape[1:]
    size = 1
    for s in x.shape:
        size *= s

    def kernel(x_ref, out_ref, recv, own, own_sem, send_sem, recv_sem):
        me = lax.axis_index(axis)
        if in_place:
            fetch = pltpu.make_async_copy(x_ref.at[me], own, own_sem)
            fetch.start()
        barrier = pltpu.get_barrier_semaphore()
        for d in range(1, n):
            peer = lax.rem(me + d, n)
            pl.semaphore_signal(barrier, inc=1, device_id={axis: peer},
                                device_id_type=pl.DeviceIdType.MESH)
        pl.semaphore_wait(barrier, n - 1)
        copies = []
        for d in range(1, n):
            peer = lax.rem(me + d, n)
            cp = pltpu.make_async_remote_copy(
                src_ref=x_ref.at[peer], dst_ref=recv.at[me],
                send_sem=send_sem.at[d], recv_sem=recv_sem.at[me],
                device_id={axis: peer}, device_id_type=pl.DeviceIdType.MESH)
            cp.start()
            copies.append(cp)
        if in_place:
            fetch.wait()
            total = own[...]
        else:
            total = x_ref[me]
        for d in range(1, n):
            src = lax.rem(me + n - d, n)
            incoming = pltpu.make_async_remote_copy(
                src_ref=x_ref.at[src], dst_ref=recv.at[src],
                send_sem=send_sem.at[d], recv_sem=recv_sem.at[src],
                device_id={axis: src}, device_id_type=pl.DeviceIdType.MESH)
            incoming.wait_recv()
            total = total + recv[src]
        for cp in copies:
            cp.wait_send()
        out_ref[...] = total

    return pl.pallas_call(
        kernel,
        out_shape=jax.ShapeDtypeStruct(rest_shape, jnp.float32),
        in_specs=[pl.BlockSpec(memory_space=pl.ANY if in_place else pltpu.VMEM)],
        out_specs=pl.BlockSpec(memory_space=pltpu.VMEM),
        scratch_shapes=[
            pltpu.VMEM(x.shape, jnp.float32),
            pltpu.VMEM(rest_shape, jnp.float32),
            pltpu.SemaphoreType.DMA,
            pltpu.SemaphoreType.DMA((n,)),
            pltpu.SemaphoreType.DMA((n,)),
        ],
        compiler_params=pltpu.CompilerParams(
            collective_id=cid, has_side_effects=True,
            vmem_limit_bytes=(64 if in_place else 40) * 1024 * 1024),
        cost_estimate=pl.CostEstimate(flops=size, transcendentals=0, bytes_accessed=3 * size * 4),
    )(x)

def ctx_sum(new_lp, old_lp, mask, roll_len, hidden, n_z, n_core):
    n = n_z * n_core
    t, hb = hidden.shape

    def kernel(new_hbm, old_hbm, mask_hbm, len_ref, hid_hbm, out_ref, live_ref, ht_ref,
               hid_ref, new_ref, old_ref, mask_ref, mine, staged, recv, hid_sem, row_sem,
               copy_sem, send_sem, recv_sem):
        me = lax.axis_index("z") * n_core + lax.axis_index("core")
        rows = [pltpu.make_async_copy(a, b, row_sem.at[i]) for i, (a, b) in enumerate(
            ((new_hbm, new_ref), (old_hbm, old_ref), (mask_hbm, mask_ref)))]
        for cp in rows:
            cp.start()
        fetch = pltpu.make_async_copy(hid_hbm, hid_ref, hid_sem)
        fetch.start()

        def peer_of(p):
            return {"z": p // n_core, "core": p % n_core}

        barrier = pltpu.get_barrier_semaphore()
        for d in range(1, n):
            pl.semaphore_signal(barrier, inc=1, device_id=peer_of(lax.rem(me + d, n)),
                                device_id_type=pl.DeviceIdType.MESH)
        for cp in rows:
            cp.wait()
        places = me * t + lax.broadcasted_iota(jnp.int32, (8, t), 1)
        mask8 = jnp.broadcast_to(mask_ref[...], (8, t))
        live = jnp.where(places < len_ref[0], mask8, 0).astype(jnp.float32)
        gap = jnp.sum((new_ref[...] - old_ref[...]) * live[0:1, :])
        count = jnp.sum(live[0:1, :])
        lanes = lax.broadcasted_iota(jnp.int32, (8, 128), 1)
        mine[...] = jnp.where(lanes == 0, gap, jnp.where(lanes == 1, count, 0.0))
        local = pltpu.make_async_copy(mine, staged, copy_sem)
        local.start()
        live_col = live.T[:, 0:1]
        live_ref[...] = live_col
        live_hid = live_col.astype(hid_ref.dtype)

        fetch.wait()
        chunks = hb // 128

        def transpose(first, last):
            @pl.loop(first, last)
            def _(j):
                cols = pl.ds(pl.multiple_of(j * 128, 128), 128)
                ht_ref[cols, :] = (hid_ref[:, cols] * live_hid).T

        transpose(0, chunks // 2)
        local.wait()
        pl.semaphore_wait(barrier, n - 1)
        copies = []
        for d in range(1, n):
            cp = pltpu.make_async_remote_copy(
                src_ref=staged, dst_ref=recv.at[me],
                send_sem=send_sem.at[d], recv_sem=recv_sem.at[me],
                device_id=peer_of(lax.rem(me + d, n)), device_id_type=pl.DeviceIdType.MESH)
            cp.start()
            copies.append(cp)
        recv[me] = staged[...]
        transpose(chunks // 2, chunks)
        for d in range(1, n):
            src = lax.rem(me + n - d, n)
            pltpu.make_async_remote_copy(
                src_ref=staged, dst_ref=recv.at[src],
                send_sem=send_sem.at[d], recv_sem=recv_sem.at[src],
                device_id=peer_of(src), device_id_type=pl.DeviceIdType.MESH).wait_recv()
        total = recv[0]
        for p in range(1, n):
            total = total + recv[p]
        for cp in copies:
            cp.wait_send()
        out_ref[...] = total

    vmem = pl.BlockSpec(memory_space=pltpu.VMEM)
    return pl.pallas_call(
        kernel,
        out_shape=(jax.ShapeDtypeStruct((8, 128), jnp.float32),
                   jax.ShapeDtypeStruct((t, 1), jnp.float32),
                   jax.ShapeDtypeStruct((hb, t), hidden.dtype)),
        in_specs=[pl.BlockSpec(memory_space=pl.ANY)] * 3 + [
            pl.BlockSpec(memory_space=pltpu.SMEM), pl.BlockSpec(memory_space=pl.ANY)],
        out_specs=(vmem, vmem, vmem),
        scratch_shapes=[
            pltpu.VMEM((t, hb), hidden.dtype),
            pltpu.VMEM(new_lp.shape, new_lp.dtype),
            pltpu.VMEM(old_lp.shape, old_lp.dtype),
            pltpu.VMEM(mask.shape, mask.dtype),
            pltpu.VMEM((8, 128), jnp.float32),
            pltpu.VMEM((8, 128), jnp.float32),
            pltpu.VMEM((n, 8, 128), jnp.float32),
            pltpu.SemaphoreType.DMA,
            pltpu.SemaphoreType.DMA((3,)),
            pltpu.SemaphoreType.DMA,
            pltpu.SemaphoreType.DMA((n,)),
            pltpu.SemaphoreType.DMA((n,)),
        ],
        compiler_params=pltpu.CompilerParams(
            collective_id=1, has_side_effects=True, vmem_limit_bytes=64 * 1024 * 1024),
    )(new_lp, old_lp, mask, roll_len, hidden)


def shards(hidden_acts, out_grad, old_logp, new_logp, roll_len, resp_mask, advantage):
    n_dp = lax.axis_size("dp")
    n_z = lax.axis_size("z")
    n_core = lax.axis_size("core")
    width = old_logp.shape[1]
    ctx = lax.axis_index("z") * n_core + lax.axis_index("core")
    summed, live_col, hid_t = ctx_sum(new_logp, old_logp, resp_mask, roll_len, hidden_acts,
                                      n_z, n_core)
    gap_sum, count = summed[0, 0], summed[0, 1]
    adv = advantage[0, 0]
    length = jnp.maximum(count, 1.0)
    seq_ratio = jnp.exp(gap_sum / length)
    active = jnp.where(adv >= 0.0, seq_ratio < 1.0 + CLIP_HIGH, seq_ratio > 1.0 - CLIP_LOW).astype(
        jnp.float32
    )
    seq_weight = -adv * seq_ratio * active / length
    token_coef = jnp.reshape(seq_weight, (1,)).astype(jnp.float32)
    d = out_grad.shape[1]
    col = d // (n_z * n_core)
    core = lax.axis_index("core").astype(jnp.int32)

    def col_index(k, which):
        return jnp.reshape(k * n_core + which, (1,)).astype(jnp.int32)

    swap = [(0, 1), (1, 0)]

    def pre_reduced(lo, hi, z_major, per_call):
        got = []
        for k in range(0, n_z, per_call):
            theirs = block_matmul(col_index(k, 1 - core), token_coef, out_grad, hid_t, n_dp, col,
                                  lo, hi, per_call)
            got.append(lax.ppermute(theirs, "core", perm=swap))
        chip = None
        for j, k in enumerate(range(0, n_z, per_call)):
            chip = block_matmul(col_index(k, core), token_coef, out_grad, hid_t, n_dp, col, lo, hi,
                                per_call, addend=got[j], into=chip, slot=k, n_slots=n_z,
                                z_major=z_major)
        return chip

    keep = col - Z_FIRST
    dp_first = pre_reduced(0, keep, False, 2)
    rows = lax.psum_scatter(dp_first, "dp", scatter_dimension=0, tiled=True)[0]
    z_first = pre_reduced(keep, col, True, n_z)
    late = z_reduce_scatter(z_first, "z", n_z, 0)
    late = z_reduce_scatter(late, "dp", n_dp, 2)
    early = z_reduce_scatter(rows, "z", n_z, 3, in_place=True)
    return jnp.concatenate([early, late], axis=1)


def solution(mesh):
    n_dp, n_ctx = mesh.shape["dp"], mesh.shape["ctx"]
    fine = Mesh(np.asarray(mesh.devices).reshape(n_dp, n_ctx // 2, 2), ("dp", "z", "core"))
    tok = ("dp", "z", "core")
    placed = (
        P(tok, None),
        P(tok, None),
        P("dp", ("z", "core")),
        P("dp", ("z", "core")),
        P("dp"),
        P("dp", ("z", "core")),
        P("dp", None),
    )
    return jax.shard_map(
        shards, mesh=fine, in_specs=placed, out_specs=P("dp", ("z", "core")), check_vma=False
    )
```
